32 devices in a mesh: blk: 4 (over z), sub: 8 (over y, x, core).
Axes of the slice: x: 2, y: 2, z: 4, core: 2. Of those that a mesh axis runs over, the one named last changes fastest.
Arguments:
- rhs: float32 [256, 16, 256], P(('blk', 'sub')), may hold values from -6 to 6
- leaf_neighbors: int32 [256, 6], P(('blk', 'sub')), may hold values from -1 to 255, as said below
- parent_neighbors: int32 [32, 6], replicated, may hold values from -1 to 31, as said below
- children: int32 [32, 8], replicated, may hold values from 0 to 255, as said below
- owners: int32 [32], replicated, may hold values from 0 to 7, as said below
- parent_places: int32 [32], replicated, may hold values from 0 to 31, as said below
Outputs:
- leaf_solution: float32 [256, 16, 256], P(('blk', 'sub'))
- parent_solution: float32 [96, 16, 256], P(('blk', 'sub'))
The draws below stay inside these ranges and needn't reach their ends.
Inputs may be any that keep to these rules, and one draw needn't show every extreme that they name: `leaf_neighbors`: entry f of block b is the leaf block across face f of b, or -1 on the domain's boundary; the relation is mutual. Leaves d * 8 onward are the blocks of device d in order of blk then sub; a range is the 64 leaves of one index of blk. The -x and +x neighbours of a leaf belong to the devices one index lower and one index higher along sub with the same blk index; its -y and +y neighbours belong to its own device; its -z and +z neighbours belong to its own device or to the device one index lower or higher along blk with the same sub index. `parent_neighbors`: entry f of parent p is the parent block across face f of p, or -1; mutual. Range r holds the parents r * 8 onward; x and y neighbours lie in the same range, -z and +z neighbours in the range just below or above. Entry o = 4 oz + 2 oy + ox names the child in octant (oz, oy, ox); every leaf is the child of one parent, and a parent's children lie in the leaf range with the same index as the parent's range; its four children with ox = 0 belong to one device of even index 2k along sub and its four with ox = 1 to the device 2k + 1 with the same blk index. `owners`: within each range no index owns more than 3 parents, and some index owns exactly 3. `parent_places`: A permutation; parents of range r have places r * 8 onward.
All inputs are finite; a program needn't handle non-finite values.
Results may differ from the reference program's by a relative error of at most 0.0003.
Values sent between devices are 32-bit elements; how exact they have to be, the bound alone decides.
No kernel may reach another device: no remote copies, remote signals or barrier semaphores. Data moves between devices by JAX's collectives and lax.ppermute only.
A program may use at most 64 MiB of HBM per device.

```python
import jax
import jax.numpy as jnp

BLK_DEV = 8
ROOT_SWEEPS = 8
LEAVES = 256
PARENTS = 32
PMOST = 3
PSLOTS = 96
N_BLK = 4
N_SUB = 8


def neighbours(grid):
    padded = jnp.pad(grid, 1, constant_values=-1)
    lists = jnp.stack([padded[1:-1, 1:-1, :-2], padded[1:-1, 1:-1, 2:], padded[1:-1, :-2, 1:-1], padded[1:-1, 2:, 1:-1], padded[:-2, 1:-1, 1:-1], padded[2:, 1:-1, 1:-1]], axis=-1).reshape(-1, 6)
    return jnp.zeros((grid.size, 6), jnp.int32).at[grid.reshape(-1)].set(lists.astype(jnp.int32))


def one_range(range_key):
    parent_len = BLK_DEV * N_SUB // 8
    first_key, second_key = jax.random.split(range_key)
    shuffled = jax.random.permutation(first_key, parent_len)
    heavy = jax.random.randint(second_key, (), 0, N_SUB)
    slot_number = jnp.arange(parent_len, dtype=jnp.int32)
    assigned = jnp.where(slot_number < PMOST, heavy, (heavy + 1 + (slot_number - PMOST) % (N_SUB - 1)) % N_SUB)
    return jnp.zeros((parent_len,), jnp.int32).at[shuffled].set(assigned.astype(jnp.int32))


def layout(key):
    width_x = N_SUB
    width_y = BLK_DEV // 2
    depth_z = 2 * N_BLK
    range_len = BLK_DEV * N_SUB
    parent_len = range_len // 8
    device_keys = jax.random.split(jax.random.fold_in(key, 11), N_BLK * N_SUB)
    device_order = jax.vmap(lambda device_key: jax.random.permutation(device_key, BLK_DEV))(device_keys).astype(jnp.int32)
    level_z = jnp.arange(depth_z, dtype=jnp.int32)[:, None, None]
    level_y = jnp.arange(width_y, dtype=jnp.int32)[None, :, None]
    level_x = jnp.arange(width_x, dtype=jnp.int32)[None, None, :]
    device_id = level_z // 2 * N_SUB + level_x + 0 * level_y
    slot_id = level_z % 2 * width_y + level_y + 0 * level_x
    leaf_ids = (device_id * BLK_DEV + device_order[device_id, slot_id]).astype(jnp.int32)
    parent_keys = jax.random.split(jax.random.fold_in(key, 12), N_BLK)
    parent_order = jax.vmap(lambda range_key: jax.random.permutation(range_key, parent_len))(parent_keys).astype(jnp.int32)
    parent_ids = (jnp.arange(N_BLK, dtype=jnp.int32)[:, None] * parent_len + parent_order).reshape(N_BLK, width_y // 2, width_x // 2)
    leaf_lists = neighbours(leaf_ids)
    parent_lists = neighbours(parent_ids)
    kids = leaf_ids.reshape(N_BLK, 2, width_y // 2, 2, width_x // 2, 2).transpose(0, 2, 4, 1, 3, 5).reshape(-1, 8)
    child_lists = jnp.zeros((PARENTS, 8), jnp.int32).at[parent_ids.reshape(-1)].set(kids)
    place_list = jnp.zeros((PARENTS,), jnp.int32).at[parent_ids.reshape(-1)].set(jnp.arange(PARENTS, dtype=jnp.int32))
    owner_keys = jax.random.split(jax.random.fold_in(key, 13), N_BLK)
    owner_list = jax.vmap(one_range)(owner_keys).reshape(-1)
    return (leaf_lists, parent_lists, child_lists, owner_list, place_list)


def draw_leaf_neighbors(key, part):
    return layout(key)[0]


def draw_parent_neighbors(key, part):
    return layout(key)[1]


def draw_children(key, part):
    return layout(key)[2]


def draw_owners(key, part):
    return layout(key)[3]


def draw_parent_places(key, part):
    return layout(key)[4]


def draw_rhs(key, part):
    shape = (LEAVES, 16, 256)
    return jnp.clip(jax.random.normal(key, shape, jnp.float32), -6.0, 6.0)


def setup_inputs(seed: int = 0) -> dict:
    splits = jax.random.split(jax.random.key(seed), 7)
    rhs = draw_rhs(jax.random.fold_in(splits[6], 71), 0)
    leaf_neighbors = draw_leaf_neighbors(jax.random.fold_in(splits[6], 71), 0)
    parent_neighbors = draw_parent_neighbors(jax.random.fold_in(splits[6], 71), 0)
    children = draw_children(jax.random.fold_in(splits[6], 71), 0)
    owners = draw_owners(jax.random.fold_in(splits[6], 71), 0)
    parent_places = draw_parent_places(jax.random.fold_in(splits[6], 71), 0)
    return dict(rhs=rhs, leaf_neighbors=leaf_neighbors, parent_neighbors=parent_neighbors, children=children, owners=owners, parent_places=parent_places)


relax_weight = 0.8


def block_faces(values):
    blocks = values.shape[0]
    cube_cells = values.reshape(blocks, 16, 16, 16)
    stacked = jnp.stack([cube_cells[:, :, :, 0], cube_cells[:, :, :, 15], cube_cells[:, :, 0, :], cube_cells[:, :, 15, :], cube_cells[:, 0], cube_cells[:, 15]], axis=1)
    return stacked.reshape(blocks, 6, 256)


def apply_operator(values, ghosts):
    blocks = values.shape[0]
    cube_cells = values.reshape(blocks, 16, 16, 16)
    shell_faces = ghosts.reshape(blocks, 6, 16, 16)
    beside_all = jnp.concatenate([shell_faces[:, 0][:, :, :, None], cube_cells[:, :, :, :-1]], axis=3)
    beside_all = beside_all + jnp.concatenate([cube_cells[:, :, :, 1:], shell_faces[:, 1][:, :, :, None]], axis=3)
    beside_all = beside_all + jnp.concatenate([shell_faces[:, 2][:, :, None, :], cube_cells[:, :, :-1, :]], axis=2)
    beside_all = beside_all + jnp.concatenate([cube_cells[:, :, 1:, :], shell_faces[:, 3][:, :, None, :]], axis=2)
    beside_all = beside_all + jnp.concatenate([shell_faces[:, 4][:, None], cube_cells[:, :-1]], axis=1)
    beside_all = beside_all + jnp.concatenate([cube_cells[:, 1:], shell_faces[:, 5][:, None]], axis=1)
    return (6.0 * cube_cells - beside_all).reshape(blocks, 16, 256)


def jacobi_sweep(values, forcing, ghosts):
    return values + (relax_weight / 6.0) * (forcing - apply_operator(values, ghosts))


def global_ghosts(values, neighbours):
    face_rows = block_faces(values)
    opposite = jnp.array([1, 0, 3, 2, 5, 4], dtype=jnp.int32)
    picked = face_rows[jnp.maximum(neighbours, 0), opposite[None, :]]
    return jnp.where((neighbours >= 0)[:, :, None], picked, 0.0)


def restrict_octants(values):
    blocks = values.shape[0]
    return (values.reshape(blocks, 8, 2, 8, 2, 8, 2).mean(axis=(2, 4, 6)) * 4.0).reshape(blocks, 512)


def assemble(octant_rows):
    blocks = octant_rows.shape[0]
    return octant_rows.reshape(blocks, 2, 2, 2, 8, 8, 8).transpose(0, 1, 4, 2, 5, 3, 6).reshape(blocks, 16, 256)


def coarsen(values):
    blocks = values.shape[0]
    return (values.reshape(blocks, 4, 4, 4, 4, 4, 4).mean(axis=(2, 4, 6)) * 16.0).reshape(blocks, 64)


def widen_root(coarse):
    blocks = coarse.shape[0]
    return jnp.broadcast_to(coarse.reshape(blocks, 4, 1, 4, 1, 4, 1), (blocks, 4, 4, 4, 4, 4, 4)).reshape(blocks, 16, 256)


def octant_split(values):
    blocks = values.shape[0]
    return values.reshape(blocks, 2, 8, 2, 8, 2, 8).transpose(0, 1, 3, 5, 2, 4, 6).reshape(blocks, 8, 512)


def widen_leaf(octant):
    blocks = octant.shape[0]
    return jnp.broadcast_to(octant.reshape(blocks, 8, 1, 8, 1, 8, 1), (blocks, 8, 2, 8, 2, 8, 2)).reshape(blocks, 16, 256)


def slot_ranks(range_owners):
    width = range_owners.shape[1]
    same_owner = range_owners[:, :, None] == range_owners[:, None, :]
    earlier = jnp.arange(width, dtype=jnp.int32)[:, None] > jnp.arange(width, dtype=jnp.int32)[None, :]
    return jnp.sum(same_owner & earlier[None], axis=2).astype(jnp.int32)


def root_relax(root_values, root_source):
    padded = jnp.pad(root_values, 1)
    beside_all = padded[2:, 1:-1, 1:-1] + padded[:-2, 1:-1, 1:-1]
    beside_all = beside_all + padded[1:-1, 2:, 1:-1] + padded[1:-1, :-2, 1:-1]
    beside_all = beside_all + padded[1:-1, 1:-1, 2:] + padded[1:-1, 1:-1, :-2]
    return root_values + (relax_weight / 6.0) * (root_source - (6.0 * root_values - beside_all))


def reference(rhs, leaf_neighbors, parent_neighbors, children, owners, parent_places):
    factor = relax_weight / 6.0
    sweep_one = factor * rhs
    second = jacobi_sweep(sweep_one, rhs, global_ghosts(sweep_one, leaf_neighbors))
    residual = rhs - apply_operator(second, global_ghosts(second, leaf_neighbors))
    source = assemble(restrict_octants(residual)[children])
    parent_one = factor * source
    parent_two = jacobi_sweep(parent_one, source, global_ghosts(parent_one, parent_neighbors))
    parent_rest = source - apply_operator(parent_two, global_ghosts(parent_two, parent_neighbors))
    ordered = jnp.zeros((PARENTS, 64), jnp.float32).at[parent_places].set(coarsen(parent_rest))
    side_y = BLK_DEV // 4
    side_x = N_SUB // 2
    root_source = ordered.reshape(N_BLK, side_y, side_x, 4, 4, 4).transpose(0, 3, 1, 4, 2, 5).reshape(4 * N_BLK, 4 * side_y, 4 * side_x)
    root_source = root_source - jnp.mean(root_source)
    root_values = jnp.zeros_like(root_source)
    for repeat in range(ROOT_SWEEPS):
        root_values = root_relax(root_values, root_source)
    root_back = root_values.reshape(N_BLK, 4, side_y, 4, side_x, 4).transpose(0, 2, 4, 1, 3, 5).reshape(PARENTS, 64)[parent_places]
    parent_three = parent_two + widen_root(root_back)
    parent_four = jacobi_sweep(parent_three, source, global_ghosts(parent_three, parent_neighbors))
    lifted = jnp.zeros((LEAVES, 512), jnp.float32).at[children.reshape(-1)].set(octant_split(parent_four).reshape(PARENTS * 8, 512))
    leaf_three = second + widen_leaf(lifted)
    leaf_solution = jacobi_sweep(leaf_three, rhs, global_ghosts(leaf_three, leaf_neighbors))
    parent_len = PARENTS // N_BLK
    range_owners = owners.reshape(N_BLK, parent_len)
    slot_row = ((jnp.arange(N_BLK, dtype=jnp.int32)[:, None] * N_SUB + range_owners) * PMOST + slot_ranks(range_owners)).reshape(-1)
    parent_solution = jnp.zeros((PSLOTS, 16, 256), jnp.float32).at[slot_row].set(parent_four)
    return leaf_solution, parent_solution
```

```python
import functools

import jax
import jax.numpy as jnp
from jax import lax
from jax.experimental import pallas as pl
from jax.experimental.pallas import tpu as pltpu
from jax.sharding import PartitionSpec as P

ROOT_SWEEPS = 8
PMOST = 3


relax_weight = 0.8


def extended(block, sides, width):
    for axis, dim in sides:
        count = lax.axis_size(axis)
        forward = [(i, i + 1) for i in range(count - 1)]
        backward = [(target, source) for source, target in forward]
        low = lax.ppermute(
            lax.slice_in_dim(block, block.shape[dim] - width, None, axis=dim), axis, forward
        )
        high = lax.ppermute(lax.slice_in_dim(block, 0, width, axis=dim), axis, backward)
        block = jnp.concatenate([low, block, high], axis=dim)
    return block


def lane_parts():
    lanes = jnp.arange(256, dtype=jnp.int32)
    return (lanes // 16, lanes % 16)


def exact_dot(left, table):
    return jnp.einsum("...k,kl->...l", left, table, precision=lax.Precision.HIGHEST)


def spread_table(column):
    lane_y, lane_x = lane_parts()
    picked = (jnp.arange(16, dtype=jnp.int32)[:, None] == lane_y[None, :]) & (
        lane_x[None, :] == column
    )
    return picked.astype(jnp.float32)


def block_faces(values):
    blocks = values.shape[0]
    stacked = jnp.stack(
        [
            values[:, :, 0::16].reshape(blocks, 256),
            values[:, :, 15::16].reshape(blocks, 256),
            values[:, :, 0:16].reshape(blocks, 256),
            values[:, :, 240:256].reshape(blocks, 256),
            values[:, 0],
            values[:, 15],
        ],
        axis=1,
    )
    return stacked


def apply_operator(values, ghosts):
    blocks = values.shape[0]
    lane_y, lane_x = lane_parts()
    ghost_x_low = ghosts[:, 0].reshape(blocks, 16, 16)
    ghost_x_high = ghosts[:, 1].reshape(blocks, 16, 16)
    ghost_y_low = ghosts[:, 2].reshape(blocks, 16, 16)
    ghost_y_high = ghosts[:, 3].reshape(blocks, 16, 16)
    from_left = jnp.where(
        lane_x[None, None, :] > 0, jnp.pad(values, ((0, 0), (0, 0), (1, 0)))[:, :, :256], 0.0
    )
    from_right = jnp.where(
        lane_x[None, None, :] < 15, jnp.pad(values, ((0, 0), (0, 0), (0, 1)))[:, :, 1:], 0.0
    )
    beside_all = from_left + exact_dot(ghost_x_low, spread_table(0))
    beside_all = beside_all + from_right + exact_dot(ghost_x_high, spread_table(15))
    beside_all = (
        beside_all
        + jnp.pad(values, ((0, 0), (0, 0), (16, 0)))[:, :, :256]
        + jnp.pad(ghost_y_low, ((0, 0), (0, 0), (0, 240)))
    )
    beside_all = (
        beside_all
        + jnp.pad(values, ((0, 0), (0, 0), (0, 16)))[:, :, 16:]
        + jnp.pad(ghost_y_high, ((0, 0), (0, 0), (240, 0)))
    )
    beside_all = beside_all + jnp.concatenate([ghosts[:, 4][:, None], values[:, :-1]], axis=1)
    beside_all = beside_all + jnp.concatenate([values[:, 1:], ghosts[:, 5][:, None]], axis=1)
    return 6.0 * values - beside_all


def jacobi_sweep(values, forcing, ghosts):
    return values + relax_weight / 6.0 * (forcing - apply_operator(values, ghosts))


def restrict_table():
    lane_y, lane_x = lane_parts()
    target = lane_y // 2 * 8 + lane_x // 2
    return (target[:, None] == jnp.arange(64, dtype=jnp.int32)[None, :]).astype(jnp.float32)


def coarse_table():
    lane_y, lane_x = lane_parts()
    target = lane_y // 4 * 4 + lane_x // 4
    return (target[:, None] == jnp.arange(16, dtype=jnp.int32)[None, :]).astype(jnp.float32)


def place_table():
    source_id = jnp.arange(256, dtype=jnp.int32)
    octant_y = source_id // 128
    octant_x = source_id // 64 % 2
    inner_y = source_id // 8 % 8
    inner_x = source_id % 8
    target = (8 * octant_y + inner_y) * 16 + 8 * octant_x + inner_x
    return (target[:, None] == jnp.arange(256, dtype=jnp.int32)[None, :]).astype(jnp.float32)


def restrict_octants(values):
    blocks = values.shape[0]
    paired = values.reshape(blocks, 8, 2, 256).sum(axis=2)
    return (exact_dot(paired, restrict_table()) * 0.5).reshape(blocks, 512)


def assemble(octant_rows):
    blocks = octant_rows.shape[0]
    arranged = (
        octant_rows.reshape(blocks, 2, 2, 2, 8, 64)
        .transpose(0, 1, 4, 2, 3, 5)
        .reshape(blocks, 16, 256)
    )
    return exact_dot(arranged, place_table())


def coarsen(values):
    blocks = values.shape[0]
    layered = values.reshape(blocks, 4, 4, 256).sum(axis=2)
    return (exact_dot(layered, coarse_table()) * 0.25).reshape(blocks, 64)


def widen_root(coarse):
    blocks = coarse.shape[0]
    flat = exact_dot(coarse.reshape(blocks, 4, 16), coarse_table().T)
    return jnp.repeat(flat, 4, axis=1)


def octant_split(values):
    blocks = values.shape[0]
    moved = exact_dot(values, place_table().T)
    return moved.reshape(blocks, 2, 8, 2, 2, 64).transpose(0, 1, 3, 4, 2, 5).reshape(blocks, 8, 512)


def widen_leaf(octant):
    blocks = octant.shape[0]
    flat = exact_dot(octant.reshape(blocks, 8, 64), restrict_table().T)
    return jnp.repeat(flat, 2, axis=1)


def slot_ranks(range_owners):
    width = range_owners.shape[1]
    same_owner = range_owners[:, :, None] == range_owners[:, None, :]
    earlier = (
        jnp.arange(width, dtype=jnp.int32)[:, None] > jnp.arange(width, dtype=jnp.int32)[None, :]
    )
    return jnp.sum(same_owner & earlier[None], axis=2)


def root_relax(root_values, root_source, row_len):
    plane_len = root_values.shape[1]
    padded_z = jnp.pad(root_values, ((1, 1), (0, 0)))
    padded_row = jnp.pad(root_values, ((0, 0), (row_len, row_len)))
    column_x = jnp.arange(plane_len, dtype=jnp.int32)[None, :] % row_len
    beside_all = padded_z[:-2] + padded_z[2:]
    beside_all = (
        beside_all
        + padded_row[:, :plane_len]
        + padded_row[:, 2 * row_len : 2 * row_len + plane_len]
    )
    beside_all = beside_all + jnp.where(
        column_x > 0, padded_row[:, row_len - 1 : row_len - 1 + plane_len], 0.0
    )
    beside_all = beside_all + jnp.where(
        column_x < row_len - 1, padded_row[:, row_len + 1 : row_len + 1 + plane_len], 0.0
    )
    return root_values + relax_weight / 6.0 * (root_source - (6.0 * root_values - beside_all))


def stack_table(range_faces, outer_faces):
    row_count = range_faces.shape[0]
    return jnp.concatenate(
        [
            range_faces.reshape(row_count * 6, 256),
            outer_faces[0],
            outer_faces[1],
            jnp.zeros((1, 256), jnp.float32),
        ],
        axis=0,
    )


def lookup(face_table, rows_index):
    blocks = rows_index.shape[0]
    return jnp.take(face_table, rows_index.reshape(-1), axis=0).reshape(blocks, 6, 256)


def table_index(neighbours, range_start, range_len):
    opposite = jnp.array([1, 0, 3, 2, 5, 4], dtype=jnp.int32)
    local_id = neighbours - range_start
    inside = (local_id >= 0) & (local_id < range_len)
    from_below = (neighbours >= 0) & (local_id < 0)
    from_above = local_id >= range_len
    rows_index = jnp.where(inside, local_id * 6 + opposite[None, :], range_len * 8)
    rows_index = jnp.where(from_below, range_len * 6 + local_id + range_len, rows_index)
    return jnp.where(from_above, range_len * 7 + local_id - range_len, rows_index)


def leaf_index(neighbours, blk_here, sub_here, sub_count):
    blocks = neighbours.shape[0]
    opposite = jnp.array([1, 0, 3, 2, 5, 4], dtype=jnp.int32)
    clamped = jnp.maximum(neighbours, 0)
    device_id = clamped // blocks
    local_id = clamped % blocks
    other_blk = device_id // sub_count
    other_sub = device_id % sub_count
    present = neighbours >= 0
    same_blk = present & (other_blk == blk_here)
    same_sub = present & (other_sub == sub_here)
    rows_index = jnp.where(same_blk & same_sub, local_id * 6 + opposite[None, :], blocks * 10)
    rows_index = jnp.where(
        same_blk & (other_sub == sub_here - 1), blocks * 6 + local_id, rows_index
    )
    rows_index = jnp.where(
        same_blk & (other_sub == sub_here + 1), blocks * 7 + local_id, rows_index
    )
    rows_index = jnp.where(
        same_sub & (other_blk == blk_here - 1), blocks * 8 + local_id, rows_index
    )
    rows_index = jnp.where(
        same_sub & (other_blk == blk_here + 1), blocks * 9 + local_id, rows_index
    )
    return rows_index


def leaf_table(values):
    face_rows = block_faces(values)
    blocks = face_rows.shape[0]
    side_rows = jnp.stack([face_rows[:, 0], face_rows[:, 1]], axis=0)
    side_wide = extended(side_rows, (("sub", 0),), 1)
    edge_rows = jnp.stack([face_rows[:, 4], face_rows[:, 5]], axis=0)
    edge_wide = extended(edge_rows, (("blk", 0),), 1)
    return jnp.concatenate(
        [
            face_rows.reshape(blocks * 6, 256),
            side_wide[0],
            side_wide[3],
            edge_wide[0],
            edge_wide[3],
            jnp.zeros((1, 256), jnp.float32),
        ],
        axis=0,
    )


def range_table(values):
    face_rows = block_faces(values)
    edge_rows = jnp.stack([face_rows[:, 4], face_rows[:, 5]], axis=0)
    widened = extended(edge_rows, (("blk", 0),), 1)
    return stack_table(face_rows, jnp.stack([widened[0], widened[3]], axis=0))


def general_local(rhs, leaf_neighbors, parent_neighbors, children, owners, parent_places):
    factor = relax_weight / 6.0
    blk_count = lax.axis_size("blk")
    sub_count = lax.axis_size("sub")
    blk_here = lax.axis_index("blk")
    sub_here = lax.axis_index("sub")
    blocks = rhs.shape[0]
    range_len = blocks * sub_count
    parent_len = range_len // 8
    range_start = blk_here * range_len
    parent_start = blk_here * parent_len
    leaf_rows = leaf_index(leaf_neighbors, blk_here, sub_here, sub_count)
    sweep_one = factor * rhs
    second = jacobi_sweep(sweep_one, rhs, lookup(leaf_table(sweep_one), leaf_rows))
    residual = rhs - apply_operator(second, lookup(leaf_table(second), leaf_rows))
    octant_rows = lax.all_gather(restrict_octants(residual), "sub", axis=0, tiled=True)
    range_children = lax.dynamic_slice_in_dim(children, parent_start, parent_len, 0) - range_start
    ranks_all = slot_ranks(owners.reshape(blk_count, parent_len)).reshape(-1)
    range_owners = lax.dynamic_slice_in_dim(owners, parent_start, parent_len, 0)
    range_ranks = lax.dynamic_slice_in_dim(ranks_all, parent_start, parent_len, 0)
    slot_match = (range_owners[None, :] == sub_here) & (
        range_ranks[None, :] == jnp.arange(PMOST, dtype=jnp.int32)[:, None]
    )
    filled = jnp.any(slot_match, axis=1)
    slot_local = jnp.sum(
        jnp.where(slot_match, jnp.arange(parent_len, dtype=jnp.int32)[None, :], 0), axis=1
    )
    filled_gain = filled.astype(jnp.float32)[:, None, None]
    own_local = sub_here * blocks + jnp.arange(blocks, dtype=jnp.int32)
    matches = range_children.reshape(-1)[None, :] == own_local[:, None]
    flat_place = jnp.sum(
        jnp.where(matches, jnp.arange(parent_len * 8, dtype=jnp.int32)[None, :], 0), axis=1
    )
    leaf_parent = flat_place // 8
    leaf_octant = flat_place % 8
    source = assemble(octant_rows[range_children])
    parent_rows = table_index(
        lax.dynamic_slice_in_dim(parent_neighbors, parent_start, parent_len, 0),
        parent_start,
        parent_len,
    )
    global_places = lax.dynamic_slice_in_dim(parent_places, parent_start, parent_len, 0)
    keep_gain = jnp.ones((parent_len, 1, 1), jnp.float32)
    parent_one = factor * source
    parent_two = jacobi_sweep(parent_one, source, lookup(range_table(parent_one), parent_rows))
    parent_rest = source - apply_operator(parent_two, lookup(range_table(parent_two), parent_rows))
    coarse = coarsen(parent_rest)
    root_slab = (
        jnp.zeros((parent_len, 64), jnp.float32).at[global_places - parent_start].set(coarse)
    )
    ordered = lax.all_gather(root_slab, "blk", axis=0, tiled=True)
    side_y = blocks // 4
    side_x = sub_count // 2
    root_source = (
        ordered.reshape(blk_count, side_y, side_x, 4, 4, 4)
        .transpose(0, 3, 1, 4, 2, 5)
        .reshape(4 * blk_count, 16 * side_y * side_x)
    )
    root_source = root_source - jnp.mean(root_source)
    root_values = jnp.zeros_like(root_source)
    for repeat in range(ROOT_SWEEPS):
        root_values = root_relax(root_values, root_source, 4 * side_x)
    root_back = (
        root_values.reshape(blk_count, 4, side_y, 4, side_x, 4)
        .transpose(0, 2, 4, 1, 3, 5)
        .reshape(blk_count * parent_len, 64)[global_places]
    )
    parent_three = parent_two + widen_root(root_back) * keep_gain
    parent_four = jacobi_sweep(parent_three, source, lookup(range_table(parent_three), parent_rows))
    parent_solution = parent_four[slot_local] * filled_gain
    own_parents = parent_four[leaf_parent]
    pieces = octant_split(own_parents)
    chosen = jnp.take_along_axis(pieces, leaf_octant[:, None, None], axis=1)[:, 0]
    leaf_three = second + widen_leaf(chosen)
    leaf_solution = jacobi_sweep(leaf_three, rhs, lookup(leaf_table(leaf_three), leaf_rows))
    return (leaf_solution, parent_solution)


FACTOR = relax_weight / 6.0
SELF = 1.0 - 6.0 * FACTOR
LANES = 128
OWN_ROWS = 64
MSG_ROWS = 32


def lane_iota(shape):
    return lax.broadcasted_iota(jnp.int32, shape, len(shape) - 1)


def row_iota(shape):
    return lax.broadcasted_iota(jnp.int32, shape, len(shape) - 2)


def turn(values, shift, axis):
    size = values.shape[axis]
    shift = shift % size
    if shift == 0:
        return values
    return pltpu.roll(values, shift, axis)


def split_dot(left, table):
    high = left.astype(jnp.bfloat16)
    low = (left - high.astype(jnp.float32)).astype(jnp.bfloat16)
    return jnp.dot(high, table, preferred_element_type=jnp.float32) + jnp.dot(
        low, table, preferred_element_type=jnp.float32
    )


def zero_one(condition, scale=1.0):
    return jnp.where(condition, scale, 0.0).astype(jnp.bfloat16)


def beside_x(chunk, width):
    cell = lane_iota(chunk.shape) % width
    low = jnp.where(cell > 0, turn(chunk, 1, 1), 0.0)
    high = jnp.where(cell < width - 1, turn(chunk, -1, 1), 0.0)
    return low + high


def y_pair(chunks, width):
    lane = lane_iota(chunks[0].shape)
    up = [turn(chunk, width, 1) for chunk in chunks]
    down = [turn(chunk, -width, 1) for chunk in chunks]
    zero = jnp.zeros_like(chunks[0])
    lower = []
    upper = []
    for k in range(len(chunks)):
        before = up[k - 1] if k > 0 else zero
        after = down[k + 1] if k + 1 < len(chunks) else zero
        lower.append(jnp.where(lane < width, before, up[k]))
        upper.append(jnp.where(lane >= LANES - width, after, down[k]))
    return lower, upper


def z_pair(chunk):
    rows = chunk.shape[0]
    row = row_iota(chunk.shape)
    lower = jnp.where(row > 0, turn(chunk, 1, 0), 0.0)
    upper = jnp.where(row < rows - 1, turn(chunk, -1, 0), 0.0)
    return lower, upper


def fine_beside(chunks):
    lower, upper = y_pair(chunks, 16)
    in_x = [beside_x(chunk, 16) for chunk in chunks]
    in_y = [a + b for a, b in zip(lower, upper)]
    in_z = []
    for chunk in chunks:
        below, above = z_pair(chunk)
        in_z.append(below + above)
    return in_x, in_y, in_z


def coarse_x_pair(columns, index, half):
    chunk = columns[index][half]
    cell = lane_iota(chunk.shape) % 8
    low = turn(chunk, 1, 1)
    high = turn(chunk, -1, 1)
    if index > 0:
        low = jnp.where(cell == 0, turn(columns[index - 1][half], -7, 1), low)
    else:
        low = jnp.where(cell == 0, 0.0, low)
    if index + 1 < len(columns):
        high = jnp.where(cell == 7, turn(columns[index + 1][half], 7, 1), high)
    else:
        high = jnp.where(cell == 7, 0.0, high)
    return low, high


def coarse_beside(columns):
    result = []
    for index in range(len(columns)):
        lower, upper = y_pair(columns[index], 8)
        halves = []
        for half in range(len(columns[index])):
            chunk = columns[index][half]
            low, high = coarse_x_pair(columns, index, half)
            total = low + high + lower[half] + upper[half]
            total = total + turn(chunk, 1, 0) + turn(chunk, -1, 0)
            halves.append(total)
        result.append(halves)
    return result


def count_true(condition):
    return jnp.sum(jnp.where(condition, 1.0, 0.0))


def list_check(sub_count, blk_count, blocks, leaf_ref, parent_ref, cell_ref, sub_here, blk_here):
    wide_y = blocks // 2
    side_y = wide_y // 2
    side_x = sub_count // 2
    parents = cell_ref.shape[0]
    side_yx = side_y * side_x
    layer = wide_y * sub_count
    children = cell_ref[:, 0:8]
    octant = lane_iota((parents, 8))
    place = jnp.broadcast_to(cell_ref[:, 8:9], (parents, 8))
    cell_z = 2 * lax.div(place, side_yx) + lax.div(octant, 4)
    cell_y = 2 * lax.rem(lax.div(place, side_x), side_y) + lax.rem(lax.div(octant, 2), 2)
    cell_x = 2 * lax.rem(place, side_x) + lax.rem(octant, 2)
    code = (cell_z * wide_y + cell_y) * sub_count + cell_x
    wrong = count_true(lax.div(children, blocks) != lax.div(cell_z, 2) * sub_count + cell_x)
    width = 6 * blocks
    listed = leaf_ref[...]
    lane = lane_iota((1, width))
    own = (blk_here * sub_count + sub_here) * blocks + lax.rem(lane, blocks)
    found = jnp.zeros((parents, width), jnp.int32)
    found_own = jnp.zeros((parents, width), jnp.int32)
    for o in range(8):
        child = children[:, o : o + 1]
        value = code[:, o : o + 1]
        found = jnp.where(child == listed, value, found)
        found_own = jnp.where(child == own, value, found_own)
    found = jnp.sum(found.astype(jnp.float32), axis=0, keepdims=True).astype(jnp.int32)
    found_own = jnp.sum(found_own.astype(jnp.float32), axis=0, keepdims=True).astype(jnp.int32)
    own_z = lax.div(found_own, layer)
    own_y = lax.rem(lax.div(found_own, sub_count), wide_y)
    own_x = lax.rem(found_own, sub_count)
    face = lax.div(lane, blocks)

    def by_axis(first, second, third):
        return jnp.where(face < 2, first, jnp.where(face < 4, second, third))

    sign = 2 * lax.rem(face, 2) - 1
    goal = by_axis(own_x, own_y, own_z) + sign
    exists = (goal >= 0) & (goal < by_axis(sub_count, wide_y, 2 * blk_count))
    wanted = found_own + sign * by_axis(1, sub_count, layer)
    wrong = wrong + jnp.sum(
        jnp.where(
            exists,
            jnp.where((listed >= 0) & (found == wanted), 0.0, 1.0),
            jnp.where(listed < 0, 0.0, 1.0),
        )
    )
    position = lax.rem(own_z, 2) * wide_y + own_y
    listed = parent_ref[0:1, :]
    place = parent_ref[1:2, :]
    shape = (parents, 6 * parents)
    hit = row_iota(shape) == listed
    found = jnp.sum(
        jnp.where(hit, cell_ref[:, 8:9].astype(jnp.float32), 0.0), axis=0, keepdims=True
    ).astype(jnp.int32)
    face = lax.div(lane_iota((1, 6 * parents)), parents)
    sign = 2 * lax.rem(face, 2) - 1
    goal = sign + by_axis(
        lax.rem(place, side_x), lax.rem(lax.div(place, side_x), side_y), lax.div(place, side_yx)
    )
    exists = (goal >= 0) & (goal < by_axis(side_x, side_y, blk_count))
    wanted = place + sign * by_axis(1, side_x, side_yx)
    wrong = wrong + jnp.sum(
        jnp.where(
            exists,
            jnp.where((listed >= 0) & (found == wanted), 0.0, 1.0),
            jnp.where(listed < 0, 0.0, 1.0),
        )
    )
    return position, jnp.where(wrong == 0.0, 1.0, 0.0)


def limits(sub_count, blk_count):
    sub_here = lax.axis_index("sub")
    blk_here = lax.axis_index("blk")

    def gain(condition):
        return jnp.where(condition, 1.0, 0.0).astype(jnp.float32)

    return (
        sub_here,
        blk_here,
        gain(sub_here > 0),
        gain(sub_here < sub_count - 1),
        gain(blk_here > 0),
        gain(blk_here < blk_count - 1),
    )


def push_kernel(
    sub_count, blk_count, blk_bits, leaf_ref, parent_ref, cell_ref, rhs_ref,
    position_ref, own_ref, own_part_ref, faces_ref, *rest
):
    msg_refs = rest[:blk_bits]
    placed, rows_s, rows_g, left_a, left_c, coarse_s = rest[blk_bits:]
    blocks = rhs_ref.shape[0]
    wide_y = blocks // 2
    chunk_count = 2 * wide_y
    f = FACTOR
    f2 = f * f
    sub_here, blk_here, x_low, x_high, z_low, z_high = limits(sub_count, blk_count)
    position, good = list_check(
        sub_count, blk_count, blocks, leaf_ref, parent_ref, cell_ref, sub_here, blk_here
    )
    for slot in range(blocks):
        at = jnp.clip(position[0, slot], 0, blocks - 1)
        position_ref[slot] = at
        placed[at] = rhs_ref[slot]
    s = []
    for k in range(chunk_count):
        lanes = slice(LANES * (k % 2), LANES * (k % 2) + LANES)
        s.append(
            jnp.concatenate([placed[k // 2, :, lanes], placed[wide_y + k // 2, :, lanes]], axis=0)
        )
    shape = s[0].shape
    cell = lane_iota(shape) % 16
    row = row_iota(shape)
    top = shape[0] - 1
    back = (
        jnp.where(cell == 0, x_low, 0.0)
        + jnp.where(cell == 15, x_high, 0.0)
        + jnp.where(row == 0, z_low, 0.0)
        + jnp.where(row == top, z_high, 0.0)
    ) * f2
    sx, sy, sz = fine_beside(s)
    w = [SELF * a + f * (x + y + z) for a, x, y, z in zip(s, sx, sy, sz)]
    wx, wy, wz = fine_beside(w)
    for k in range(chunk_count):
        half = slice(LANES * (k % 2), LANES * (k % 2) + LANES)
        r = SELF * w[k] + f * (wx[k] + wy[k] + wz[k]) + back * s[k]
        part = f * (s[k] + w[k] + r)
        own_part_ref[k // 2, :, half] = part[:16]
        own_part_ref[wide_y + k // 2, :, half] = part[16:]
        rows_s[k] = r
        base = (SELF * f + f2) * s[k] + f * w[k]
        gx = base + f2 * (sy[k] + sz[k])
        rows_g[k] = gx
        gz = base + f2 * (sx[k] + sy[k])
        line = 48 * (k // 2)
        left_a[line + 16 : line + 17, half] = gz[0:1]
        left_a[line + 17 : line + 18, half] = gz[top : top + 1]
        left_a[line + 40 : line + 41, half] = (2.0 * f2) * s[k][0:1]
        left_a[line + 41 : line + 42, half] = (2.0 * f2) * s[k][top : top + 1]
        line_c = 64 * (k // 2)
        left_c[line_c : line_c + 32, half] = gx + (f - f2) * s[k]
        left_c[line_c + 32 : line_c + 64, half] = s[k]
        edge = gz + (f - f2) * s[k]
        for bit in range(blk_bits):
            upward = (blk_here // (1 << bit)) % 2 == 0
            msg_refs[bit][16 + k // 2 : 17 + k // 2, half] = jnp.where(
                upward, edge[top : top + 1], edge[0:1]
            )
            msg_refs[bit][16 + wide_y + k // 2 : 17 + wide_y + k // 2, half] = jnp.where(
                upward, s[k][top : top + 1], s[k][0:1]
            )
    for k in range(chunk_count):
        half = slice(LANES * (k % 2), LANES * (k % 2) + LANES)
        line = 48 * (k // 2)
        left_a[line : line + 16, half] = (
            rows_s[k, pl.ds(0, 16, stride=2), :] + rows_s[k, pl.ds(1, 16, stride=2), :]
        )
        left_a[line + 24 : line + 40, half] = (
            rows_g[k, pl.ds(0, 16, stride=2), :] + rows_g[k, pl.ds(1, 16, stride=2), :]
        )
    key = row_iota((256, LANES))
    col = lane_iota((256, LANES))
    key_y = key // 16
    key_x = key % 16
    col_y = (col % 64) // 8
    col_x = col % 8
    same_y = key_y // 2 == col_y
    table_a = zero_one(
        same_y
        & (
            ((col < 64) & (key_x // 2 == col_x))
            | ((col >= 64) & (col_x == 7) & (key_x == 0))
            | ((col >= 64) & (col_x == 0) & (key_x == 15))
        ),
        0.5,
    )
    out_a = split_dot(left_a[...], table_a)
    table_c = zero_one(
        (key_y == col % 64) & (((col < 64) & (key_x == 0)) | ((col >= 64) & (key_x == 15)))
    )
    out_c = split_dot(left_c[...], table_c)
    faces = out_c[0:64]
    for yy in range(1, wide_y):
        faces = faces + turn(out_c[64 * yy : 64 * yy + 64], 16 * yy, 1)
    faces_ref[...] = faces
    lane24 = lane_iota((24, LANES))
    main = []
    side = []
    for half in range(2):
        first = out_a[96 * half : 96 * half + 24]
        second = out_a[96 * half + 48 : 96 * half + 72]
        main.append(jnp.where(lane24 < 64, first, turn(second, 64, 1)))
        first = out_a[96 * half + 24 : 96 * half + 48]
        second = out_a[96 * half + 72 : 96 * half + 96]
        side.append(jnp.where(lane24 < 64, turn(first, 64, 1), second))
    own_ref[...] = jnp.zeros(own_ref.shape, jnp.float32)
    for half in range(2):
        lanes = slice(LANES * half, LANES * half + LANES)
        for base_row, piece in ((0, main[half]), (24, side[half])):
            own_ref[base_row + 4 : base_row + 20, lanes] = piece[0:16]
            own_ref[base_row + 3 : base_row + 4, lanes] = piece[16:17] * z_low
            own_ref[base_row + 20 : base_row + 21, lanes] = piece[17:18] * z_high
    own_ref[56:64, :] = jnp.zeros((8, 256), jnp.float32) + good
    cell8 = lane24 % 8
    row24 = row_iota((24, LANES))
    inside_z = jnp.where(row24 < 4, z_low, jnp.where(row24 >= 20, z_high, 1.0))
    gain = [inside_z * x_low, inside_z, inside_z * x_high]
    main24 = [own_ref[0:24, 0:LANES], own_ref[0:24, LANES:256]]
    side24 = [own_ref[24:48, 0:LANES], own_ref[24:48, LANES:256]]
    columns = [
        [jnp.where(cell8 == 7, piece, 0.0) * x_low for piece in side24],
        main24,
        [jnp.where(cell8 == 0, piece, 0.0) * x_high for piece in side24],
    ]
    near = coarse_beside(columns)
    wp = [
        [gain[b] * (SELF * columns[b][h] + f * near[b][h]) for h in range(2)] for b in range(3)
    ]
    near = coarse_beside(wp)
    for b in range(3):
        for h in range(2):
            coarse_s[2 * b + h, 0:24] = gain[b] * (SELF * wp[b][h] + f * near[b][h])
            coarse_s[2 * b + h, 24:32] = jnp.zeros((8, LANES), jnp.float32)
    pieces = []
    for k in range(6):
        pieces.append(
            coarse_s[k, pl.ds(0, 8, stride=4), :]
            + coarse_s[k, pl.ds(1, 8, stride=4), :]
            + coarse_s[k, pl.ds(2, 8, stride=4), :]
            + coarse_s[k, pl.ds(3, 8, stride=4), :]
        )
    root_left = jnp.concatenate(pieces, axis=1)
    root_lanes = 16 * sub_count
    key = row_iota((6 * LANES, root_lanes))
    col = lane_iota((6 * LANES, root_lanes))
    target = (
        ((key // LANES) % 2 * 4 + key % LANES // 32) * (2 * sub_count)
        + 2 * (sub_here + key // 256 - 1)
        + key % 8 // 4
    )
    root_part = split_dot(root_left, zero_one(col == target, 0.25))
    own_ref[48:56, 0:root_lanes] = root_part
    for bit in range(blk_bits):
        upward = (blk_here // (1 << bit)) % 2 == 0
        ref = msg_refs[bit]
        ref[8:16, :] = own_ref[48:56, :]
        ref[24:32, :] = jnp.zeros((8, 256), jnp.float32) + good
        ref[24:25, 0:LANES] = jnp.where(upward, faces[63:64], faces[32:33])
        for base_row, source in ((0, 0), (4, 24)):
            ref[base_row : base_row + 4, :] = jnp.where(
                upward, own_ref[source + 17 : source + 21, :], own_ref[source + 3 : source + 7, :]
            )


def neighbour_pick(blk_here, blk_count, msg_refs):
    spans = []
    step = 1
    while step < blk_count:
        spans.append(step)
        step = 2 * step + 1

    def picker(other):
        choices = [(blk_here ^ other) == d for d in spans]

        def read(rows, lanes):
            value = msg_refs[spans[-1] - 1][rows, lanes]
            for choice, d in zip(choices[:-1], spans[:-1]):
                value = jnp.where(choice, msg_refs[d - 1][rows, lanes], value)
            return value

        return read

    return picker(blk_here - 1), picker(blk_here + 1)


def root_tiles(sub_count, blk_count):
    return (sub_count * blk_count // 16 + 1) // 2


def join_kernel(sub_count, blk_count, own_ref, faces_ref, *rest):
    msg_refs = rest[: blk_count - 1]
    out_ref, root_s = rest[blk_count - 1 :]
    _, blk_here, _, _, z_low, z_high = limits(sub_count, blk_count)
    below, above = neighbour_pick(blk_here, blk_count, msg_refs)
    row8 = row_iota((8, LANES))
    low_rows = (row8 >= 1) & (row8 < 5)
    high_rows = (row8 >= 3) & (row8 < 7)
    for half in range(2):
        lanes = slice(LANES * half, LANES * half + LANES)
        low = below(slice(0, 8), lanes) * z_low
        high = above(slice(0, 8), lanes) * z_high
        for base, low_turn, high_turn in ((0, 1, 3), (24, 5, 7)):
            out_ref[base : base + 8, lanes] = own_ref[base : base + 8, lanes] + jnp.where(
                low_rows, turn(low, low_turn, 0), 0.0
            )
            out_ref[base + 8 : base + 16, lanes] = own_ref[base + 8 : base + 16, lanes]
            out_ref[base + 16 : base + 24, lanes] = own_ref[
                base + 16 : base + 24, lanes
            ] + jnp.where(high_rows, turn(high, high_turn, 0), 0.0)
    root_s[...] = jnp.zeros(root_s.shape, jnp.float32)
    good = own_ref[56:64, 0:LANES]
    for d in range(blk_count):
        start = 4 * (blk_here ^ d) + 3
        for part in range(root_s.shape[0]):
            lanes = slice(LANES * part, LANES * part + LANES)
            value = own_ref[48:56, lanes] if d == 0 else msg_refs[d - 1][8:16, lanes]
            root_s[part, pl.ds(start, 8), :] = root_s[part, pl.ds(start, 8), :] + value
        if d > 0:
            good = jnp.minimum(good, msg_refs[d - 1][24:32, LANES:256])
    tile = 0
    for start in range(0, 4 * blk_count, 8):
        for part in range(root_s.shape[0]):
            row = 48 + 8 * (tile // 2)
            lanes = slice(LANES * (tile % 2), LANES * (tile % 2) + LANES)
            out_ref[row : row + 8, lanes] = root_s[part, 4 + start : 12 + start]
            tile += 1
    row = 48 + 8 * root_tiles(sub_count, blk_count)
    low = below(slice(24, 32), slice(0, LANES)) * z_low
    high = above(slice(24, 32), slice(0, LANES)) * z_high
    out_ref[row : row + 8, 0:LANES] = jnp.where(row8 == 0, low, turn(high, 1, 0))
    out_ref[row : row + 8, LANES:256] = good
    out_ref[row + 8 : row + 40, 0:LANES] = faces_ref[0:32]
    out_ref[row + 8 : row + 40, LANES:256] = faces_ref[32:64]


def owned_slots(sub_count, blk_count, slots, sub_here, blk_here, owner_ref, cell_ref):
    parents = owner_ref.shape[1]
    parent_len = parents // blk_count
    side_y = parent_len // (sub_count // 2)
    side_x = sub_count // 2
    owners = owner_ref[0:1, :]
    places = owner_ref[1:2, :]
    number = lane_iota((1, parents))
    shape = (parents, parents)
    in_range = lax.div(number, parent_len) == blk_here
    mine = in_range & (owners == sub_here)
    column = cell_ref[:, 9:10]
    row = row_iota((parents, 1))
    column_mine = (column == sub_here) & (lax.div(row, parent_len) == blk_here)
    rank = jnp.sum(
        jnp.where(column_mine & (row_iota(shape) < lane_iota(shape)), 1.0, 0.0),
        axis=0,
        keepdims=True,
    )
    found = []
    for k in range(slots):
        chosen = jnp.where(mine & (rank == float(k)), 1.0, 0.0)
        place = jnp.sum(chosen * places.astype(jnp.float32)).astype(jnp.int32)
        found.append(
            (lax.rem(lax.div(place, side_x), side_y), lax.rem(place, side_x), jnp.sum(chosen))
        )
    return found


def solve_kernel(
    sub_count, blk_count, slots, positions, owner_ref, cell_ref, all_ref, part_ref, *rest
):
    msg_refs = rest[: blk_count - 1]
    leaf_ref, parent_ref = rest[blk_count - 1 : blk_count + 1]
    placed, par_s, root_s, fine_s, push_s = rest[blk_count + 1 :]
    blocks = part_ref.shape[0]
    wide_y = blocks // 2
    f = FACTOR
    f2 = f * f
    sub_here, blk_here, x_low, x_high, z_low, z_high = limits(sub_count, blk_count)
    below, above = neighbour_pick(blk_here, blk_count, msg_refs)
    owned = owned_slots(sub_count, blk_count, slots, sub_here, blk_here, owner_ref, cell_ref)
    row8 = row_iota((8, LANES))
    cell24 = lax.rem(lane_iota((24, LANES)), 8)
    row24 = row_iota((24, LANES))
    source = []
    for c in range(sub_count):
        halves = []
        for half in range(2):
            lanes = slice(LANES * half, LANES * half + LANES)
            value = all_ref[c, 0:24, lanes]
            if c + 1 < sub_count:
                value = value + jnp.where(cell24 == 7, all_ref[c + 1, 24:48, lanes], 0.0)
            if c > 0:
                value = value + jnp.where(cell24 == 0, all_ref[c - 1, 24:48, lanes], 0.0)
            halves.append(value)
        source.append(halves)

    root_lanes = 16 * sub_count
    row_len = 2 * sub_count
    root_rows = 4 * blk_count
    parts = root_lanes // LANES
    tile_rows = []
    tile = 0
    for _ in range(0, root_rows, 8):
        pieces = []
        for part in range(parts):
            row = 48 + 8 * (tile // 2)
            lanes = slice(LANES * (tile % 2), LANES * (tile % 2) + LANES)
            total = all_ref[0, row : row + 8, lanes]
            for c in range(1, sub_count):
                total = total + all_ref[c, row : row + 8, lanes]
            pieces.append(total)
            tile += 1
        tile_rows.append(jnp.concatenate(pieces, axis=1))
    root_source = jnp.concatenate(tile_rows, axis=0)
    root_source = root_source - jnp.sum(root_source) / (root_rows * root_lanes)
    shape = root_source.shape
    lane = lane_iota(shape)
    row = row_iota(shape)
    values = f * root_source
    for _ in range(ROOT_SWEEPS - 1):
        total = jnp.where(lane % row_len > 0, turn(values, 1, 1), 0.0)
        total = total + jnp.where(lane % row_len < row_len - 1, turn(values, -1, 1), 0.0)
        total = total + jnp.where(lane >= row_len, turn(values, row_len, 1), 0.0)
        total = total + jnp.where(lane < root_lanes - row_len, turn(values, -row_len, 1), 0.0)
        total = total + jnp.where(row > 0, turn(values, 1, 0), 0.0)
        total = total + jnp.where(row < root_rows - 1, turn(values, -1, 0), 0.0)
        values = SELF * values + f * (root_source + total)
    root_s[...] = jnp.zeros(root_s.shape, jnp.float32)
    for part in range(parts):
        root_s[part, 4 : 4 + root_rows] = values[:, LANES * part : LANES * part + LANES]
    mine = jnp.concatenate(
        [root_s[part, pl.ds(4 * blk_here + 3, 8), :] for part in range(parts)], axis=1
    )
    left = jnp.concatenate([turn(mine, -2 * c, 1) for c in range(sub_count)], axis=0)
    key = row_iota((root_lanes, 256))
    col = lane_iota((root_lanes, 256))
    wide = split_dot(left, zero_one(key == (col // 32) * row_len + col % 8 // 4))

    valid = (
        (row24 >= 2)
        & (row24 < 22)
        & ((row24 >= 4) | (z_low > 0.0))
        & ((row24 < 20) | (z_high > 0.0))
    )
    near = coarse_beside(source)
    three = []
    for c in range(sub_count):
        halves = []
        for half in range(2):
            lanes = slice(LANES * half, LANES * half + LANES)
            wp = SELF * source[c][half] + f * near[c][half]
            tiles = []
            for t in range(3):
                first = wide[8 * c + 2 * t : 8 * c + 2 * t + 1, lanes]
                second = wide[8 * c + 2 * t + 1 : 8 * c + 2 * t + 2, lanes]
                tiles.append(
                    jnp.where(
                        row8 < 4,
                        jnp.broadcast_to(first, (8, LANES)),
                        jnp.broadcast_to(second, (8, LANES)),
                    )
                )
            value = f * (source[c][half] + wp) + jnp.concatenate(tiles, axis=0)
            halves.append(jnp.where(valid, value, 0.0))
        three.append(halves)
    near = coarse_beside(three)
    for c in range(sub_count):
        for half in range(2):
            value = SELF * three[c][half] + f * (near[c][half] + source[c][half])
            par_s[c, half] = jnp.where(valid, value, 0.0)

    pieces = []
    for k in range(slots):
        half, place_x, filled = owned[k]
        pieces.append(
            jnp.concatenate(
                [par_s[2 * place_x, half, 4:20], par_s[2 * place_x + 1, half, 4:20]], axis=1
            )
            * filled
        )
    left = jnp.concatenate(pieces, axis=0)
    key = row_iota((256, 256))
    col = lane_iota((256, 256))
    table = zero_one(key == (col % 16 // 8) * 128 + (col // 16) * 8 + col % 8)
    moved = split_dot(left, table)
    for k in range(slots):
        parent_ref[k] = moved[16 * k : 16 * k + 16]

    before = jnp.maximum(sub_here - 1, 0)
    after = jnp.minimum(sub_here + 1, sub_count - 1)
    columns = [
        [par_s[before, half] * x_low for half in range(2)],
        [par_s[sub_here, half] for half in range(2)],
        [par_s[after, half] * x_high for half in range(2)],
    ]
    centre = columns[1]
    in_y = y_pair(centre, 8)
    lane16 = lane_iota((16, LANES))
    left_rows = []
    in_x = [coarse_x_pair(columns, 1, half) for half in range(2)]
    blend = {}
    for half in range(2):
        for zp in range(2):
            base = (SELF + 3.0 * f) * centre[half] + f * turn(centre[half], 1 - 2 * zp, 0)
            for yp in range(2):
                for xp in range(2):
                    value = base + f * (in_y[yp][half] + in_x[half][xp])
                    blend[half, zp, 2 * yp + xp] = value[4:20]
    for yy in range(wide_y):
        half = yy // 2
        for zp in range(2):
            pair = []
            for v in (0, 2):
                first = blend[half, zp, v]
                second = blend[half, zp, v + 1]
                if yy % 2 == 0:
                    second = turn(second, 64, 1)
                else:
                    first = turn(first, 64, 1)
                pair.append(jnp.where(lane16 < 64, first, second))
            left_rows.append(jnp.concatenate(pair, axis=1))
    left = jnp.concatenate(left_rows, axis=0)
    key = row_iota((256, 256))
    col = lane_iota((256, 256))
    col_y = col // 16
    col_x = col % 16
    target = (col_y % 2 * 2 + col_x % 2) * 64 + col_y // 2 * 8 + col_x // 2
    spread = split_dot(left, zero_one(key == target))
    for yy in range(wide_y):
        for zp in range(2):
            line = 16 * (2 * yy + zp)
            fine_s[2 * yy, pl.ds(zp, 16, stride=2), :] = spread[line : line + 16, 0:128]
            fine_s[2 * yy + 1, pl.ds(zp, 16, stride=2), :] = spread[line : line + 16, 128:256]

    line = 48 + 8 * root_tiles(sub_count, blk_count)
    lane64 = lane_iota((32, LANES))
    row32 = row_iota((32, LANES))
    from_low = all_ref[before, line + 8 : line + 40, 0:LANES] * x_low
    low_values = all_ref[before, line + 8 : line + 40, LANES:256] * x_low
    from_high = all_ref[after, line + 8 : line + 40, 0:LANES] * x_high
    high_values = all_ref[after, line + 8 : line + 40, LANES:256] * x_high
    low_line = all_ref[before, line : line + 8, 0:LANES] * (2.0 * f2 * x_low)
    high_line = all_ref[after, line : line + 8, 0:LANES] * (2.0 * f2 * x_high)
    low_line = [jnp.broadcast_to(low_line[k : k + 1], (32, LANES)) for k in range(2)]
    high_line = [jnp.broadcast_to(high_line[k : k + 1], (32, LANES)) for k in range(2)]
    edge_low = (
        from_low
        + jnp.where(row32 == 0, low_line[0], 0.0)
        + jnp.where(row32 == 31, low_line[1], 0.0)
    )
    edge_high = (
        from_high
        + jnp.where(row32 == 0, high_line[0], 0.0)
        + jnp.where(row32 == 31, high_line[1], 0.0)
    )
    left = jnp.concatenate(
        [
            jnp.where(lane64 < 64, turn(edge_low, 64, 1), f2 * low_values),
            jnp.where(lane64 < 64, edge_high, f2 * turn(high_values, 64, 1)),
        ],
        axis=1,
    )
    fine_lanes = 256 * wide_y
    key = row_iota((256, fine_lanes))
    col = lane_iota((256, fine_lanes))
    kind = key // 64
    kind_x = jnp.where(kind == 0, 0, jnp.where(kind == 1, 1, jnp.where(kind == 2, 15, 14)))
    push = split_dot(left, zero_one((key % 64 == col // 16) & (col % 16 == kind_x)))
    push_s[...] = push
    own_low = below(slice(16, 24), slice(0, 256)) * z_low
    own_high = above(slice(16, 24), slice(0, 256)) * z_high
    for yy in range(wide_y):
        lanes = slice(256 * yy, 256 * yy + 256)
        push_s[0:1, lanes] = push_s[0:1, lanes] + own_low[yy : yy + 1]
        push_s[1:2, lanes] = push_s[1:2, lanes] + f2 * own_low[wide_y + yy : wide_y + yy + 1]
        push_s[31:32, lanes] = push_s[31:32, lanes] + own_high[yy : yy + 1]
        push_s[30:31, lanes] = push_s[30:31, lanes] + f2 * own_high[wide_y + yy : wide_y + yy + 1]
    for zz in range(2):
        for yy in range(wide_y):
            rows = slice(16 * zz, 16 * zz + 16)
            lanes = slice(256 * yy, 256 * yy + 256)
            index = zz * wide_y + yy
            fine = jnp.concatenate([fine_s[2 * yy, rows], fine_s[2 * yy + 1, rows]], axis=1)
            placed[index] = part_ref[index] + fine + f * push_s[rows, lanes]
    for slot in range(blocks):
        leaf_ref[slot] = placed[positions[slot]]


def paired(count, step):
    return [(i, i ^ step) for i in range(count)]


def local(rhs, leaf_neighbors, parent_neighbors, children, owners, parent_places):
    blk_count = lax.axis_size("blk")
    sub_count = lax.axis_size("sub")
    blocks = rhs.shape[0]
    wide_y = blocks // 2
    blk_bits = blk_count.bit_length() - 1
    f32 = jnp.float32
    vmem = pl.BlockSpec(memory_space=pltpu.VMEM)
    smem = pl.BlockSpec(memory_space=pltpu.SMEM)
    leaf_row = leaf_neighbors.T.reshape(1, -1)
    parent_rows = jnp.stack([parent_neighbors.T.reshape(-1), jnp.tile(parent_places, 6)])
    owner_rows = jnp.stack([owners, parent_places])
    cells = jnp.concatenate([children, parent_places[:, None], owners[:, None]], axis=1)
    outs = pl.pallas_call(
        functools.partial(push_kernel, sub_count, blk_count, blk_bits),
        name="push",
        out_shape=[
            jax.ShapeDtypeStruct((blocks,), jnp.int32),
            jax.ShapeDtypeStruct((OWN_ROWS, 256), f32),
            jax.ShapeDtypeStruct((blocks, 16, 256), f32),
            jax.ShapeDtypeStruct((64, LANES), f32),
        ]
        + [jax.ShapeDtypeStruct((MSG_ROWS, 256), f32)] * blk_bits,
        in_specs=[vmem] * 4,
        out_specs=[smem] + [vmem] * (3 + blk_bits),
        scratch_shapes=[
            pltpu.VMEM((blocks, 16, 256), f32),
            pltpu.VMEM((2 * wide_y, 32, LANES), f32),
            pltpu.VMEM((2 * wide_y, 32, LANES), f32),
            pltpu.VMEM((48 * wide_y, 256), f32),
            pltpu.VMEM((64 * wide_y, 256), f32),
            pltpu.VMEM((6, 32, LANES), f32),
        ],
    )(leaf_row, parent_rows, cells, rhs)
    positions, own, own_part, faces = outs[:4]
    messages = outs[4:]
    received = [
        lax.ppermute(messages[d.bit_length() - 1], "blk", paired(blk_count, d))
        for d in range(1, blk_count)
    ]
    root_parts = 16 * sub_count // LANES
    joined_rows = 48 + 8 * root_tiles(sub_count, blk_count) + 8 + 32
    joined = pl.pallas_call(
        functools.partial(join_kernel, sub_count, blk_count),
        name="join",
        out_shape=jax.ShapeDtypeStruct((joined_rows, 256), f32),
        in_specs=[vmem] * (1 + blk_count),
        out_specs=vmem,
        scratch_shapes=[pltpu.VMEM((root_parts, 4 * blk_count + 8, LANES), f32)],
    )(own, faces, *received)
    gathered = lax.all_gather(joined, "sub", axis=0, tiled=False)
    good = jnp.min(gathered[:, joined_rows - 40, LANES])

    def fast():
        return tuple(
            pl.pallas_call(
                functools.partial(solve_kernel, sub_count, blk_count, PMOST),
                name="solve",
                out_shape=[
                    jax.ShapeDtypeStruct((blocks, 16, 256), f32),
                    jax.ShapeDtypeStruct((PMOST, 16, 256), f32),
                ],
                in_specs=[smem] + [vmem] * (4 + blk_count - 1),
                out_specs=[vmem] * 2,
                scratch_shapes=[
                    pltpu.VMEM((blocks, 16, 256), f32),
                    pltpu.VMEM((sub_count, 2, 24, LANES), f32),
                    pltpu.VMEM((root_parts, 4 * blk_count + 8, LANES), f32),
                    pltpu.VMEM((2 * wide_y, 32, LANES), f32),
                    pltpu.VMEM((32, 256 * wide_y), f32),
                ],
            )(positions, owner_rows, cells, gathered, own_part, *received)
        )

    def general():
        return general_local(
            rhs, leaf_neighbors, parent_neighbors, children, owners, parent_places
        )

    return lax.cond(good > 0.5, fast, general)


def solution(mesh):
    in_specs = (P(("blk", "sub"), None, None), P(("blk", "sub"), None), P(), P(), P(), P())
    out_specs = (P(("blk", "sub"), None, None), P(("blk", "sub"), None, None))
    return jax.shard_map(local, mesh=mesh, in_specs=in_specs, out_specs=out_specs, check_vma=False)
```

```python
import functools

import jax
import jax.numpy as jnp
from jax import lax
import numpy as np
from jax.experimental import pallas as pl
from jax.experimental.pallas import tpu as pltpu
from jax.sharding import PartitionSpec as P

ROOT_SWEEPS = 8
PMOST = 3


relax_weight = 0.8


def extended(block, sides, width):
    for axis, dim in sides:
        count = lax.axis_size(axis)
        forward = [(i, i + 1) for i in range(count - 1)]
        backward = [(target, source) for source, target in forward]
        low = lax.ppermute(
            lax.slice_in_dim(block, block.shape[dim] - width, None, axis=dim), axis, forward
        )
        high = lax.ppermute(lax.slice_in_dim(block, 0, width, axis=dim), axis, backward)
        block = jnp.concatenate([low, block, high], axis=dim)
    return block


def lane_parts():
    lanes = jnp.arange(256, dtype=jnp.int32)
    return (lanes // 16, lanes % 16)


def exact_dot(left, table):
    return jnp.einsum("...k,kl->...l", left, table, precision=lax.Precision.HIGHEST)


def spread_table(column):
    lane_y, lane_x = lane_parts()
    picked = (jnp.arange(16, dtype=jnp.int32)[:, None] == lane_y[None, :]) & (
        lane_x[None, :] == column
    )
    return picked.astype(jnp.float32)


def block_faces(values):
    blocks = values.shape[0]
    stacked = jnp.stack(
        [
            values[:, :, 0::16].reshape(blocks, 256),
            values[:, :, 15::16].reshape(blocks, 256),
            values[:, :, 0:16].reshape(blocks, 256),
            values[:, :, 240:256].reshape(blocks, 256),
            values[:, 0],
            values[:, 15],
        ],
        axis=1,
    )
    return stacked


def apply_operator(values, ghosts):
    blocks = values.shape[0]
    lane_y, lane_x = lane_parts()
    ghost_x_low = ghosts[:, 0].reshape(blocks, 16, 16)
    ghost_x_high = ghosts[:, 1].reshape(blocks, 16, 16)
    ghost_y_low = ghosts[:, 2].reshape(blocks, 16, 16)
    ghost_y_high = ghosts[:, 3].reshape(blocks, 16, 16)
    from_left = jnp.where(
        lane_x[None, None, :] > 0, jnp.pad(values, ((0, 0), (0, 0), (1, 0)))[:, :, :256], 0.0
    )
    from_right = jnp.where(
        lane_x[None, None, :] < 15, jnp.pad(values, ((0, 0), (0, 0), (0, 1)))[:, :, 1:], 0.0
    )
    beside_all = from_left + exact_dot(ghost_x_low, spread_table(0))
    beside_all = beside_all + from_right + exact_dot(ghost_x_high, spread_table(15))
    beside_all = (
        beside_all
        + jnp.pad(values, ((0, 0), (0, 0), (16, 0)))[:, :, :256]
        + jnp.pad(ghost_y_low, ((0, 0), (0, 0), (0, 240)))
    )
    beside_all = (
        beside_all
        + jnp.pad(values, ((0, 0), (0, 0), (0, 16)))[:, :, 16:]
        + jnp.pad(ghost_y_high, ((0, 0), (0, 0), (240, 0)))
    )
    beside_all = beside_all + jnp.concatenate([ghosts[:, 4][:, None], values[:, :-1]], axis=1)
    beside_all = beside_all + jnp.concatenate([values[:, 1:], ghosts[:, 5][:, None]], axis=1)
    return 6.0 * values - beside_all


def jacobi_sweep(values, forcing, ghosts):
    return values + relax_weight / 6.0 * (forcing - apply_operator(values, ghosts))


def restrict_table():
    lane_y, lane_x = lane_parts()
    target = lane_y // 2 * 8 + lane_x // 2
    return (target[:, None] == jnp.arange(64, dtype=jnp.int32)[None, :]).astype(jnp.float32)


def coarse_table():
    lane_y, lane_x = lane_parts()
    target = lane_y // 4 * 4 + lane_x // 4
    return (target[:, None] == jnp.arange(16, dtype=jnp.int32)[None, :]).astype(jnp.float32)


def place_table():
    source_id = jnp.arange(256, dtype=jnp.int32)
    octant_y = source_id // 128
    octant_x = source_id // 64 % 2
    inner_y = source_id // 8 % 8
    inner_x = source_id % 8
    target = (8 * octant_y + inner_y) * 16 + 8 * octant_x + inner_x
    return (target[:, None] == jnp.arange(256, dtype=jnp.int32)[None, :]).astype(jnp.float32)


def restrict_octants(values):
    blocks = values.shape[0]
    paired = values.reshape(blocks, 8, 2, 256).sum(axis=2)
    return (exact_dot(paired, restrict_table()) * 0.5).reshape(blocks, 512)


def assemble(octant_rows):
    blocks = octant_rows.shape[0]
    arranged = (
        octant_rows.reshape(blocks, 2, 2, 2, 8, 64)
        .transpose(0, 1, 4, 2, 3, 5)
        .reshape(blocks, 16, 256)
    )
    return exact_dot(arranged, place_table())


def coarsen(values):
    blocks = values.shape[0]
    layered = values.reshape(blocks, 4, 4, 256).sum(axis=2)
    return (exact_dot(layered, coarse_table()) * 0.25).reshape(blocks, 64)


def widen_root(coarse):
    blocks = coarse.shape[0]
    flat = exact_dot(coarse.reshape(blocks, 4, 16), coarse_table().T)
    return jnp.repeat(flat, 4, axis=1)


def octant_split(values):
    blocks = values.shape[0]
    moved = exact_dot(values, place_table().T)
    return moved.reshape(blocks, 2, 8, 2, 2, 64).transpose(0, 1, 3, 4, 2, 5).reshape(blocks, 8, 512)


def widen_leaf(octant):
    blocks = octant.shape[0]
    flat = exact_dot(octant.reshape(blocks, 8, 64), restrict_table().T)
    return jnp.repeat(flat, 2, axis=1)


def slot_ranks(range_owners):
    width = range_owners.shape[1]
    same_owner = range_owners[:, :, None] == range_owners[:, None, :]
    earlier = (
        jnp.arange(width, dtype=jnp.int32)[:, None] > jnp.arange(width, dtype=jnp.int32)[None, :]
    )
    return jnp.sum(same_owner & earlier[None], axis=2)


def root_relax(root_values, root_source, row_len):
    plane_len = root_values.shape[1]
    padded_z = jnp.pad(root_values, ((1, 1), (0, 0)))
    padded_row = jnp.pad(root_values, ((0, 0), (row_len, row_len)))
    column_x = jnp.arange(plane_len, dtype=jnp.int32)[None, :] % row_len
    beside_all = padded_z[:-2] + padded_z[2:]
    beside_all = (
        beside_all
        + padded_row[:, :plane_len]
        + padded_row[:, 2 * row_len : 2 * row_len + plane_len]
    )
    beside_all = beside_all + jnp.where(
        column_x > 0, padded_row[:, row_len - 1 : row_len - 1 + plane_len], 0.0
    )
    beside_all = beside_all + jnp.where(
        column_x < row_len - 1, padded_row[:, row_len + 1 : row_len + 1 + plane_len], 0.0
    )
    return root_values + relax_weight / 6.0 * (root_source - (6.0 * root_values - beside_all))


def stack_table(range_faces, outer_faces):
    row_count = range_faces.shape[0]
    return jnp.concatenate(
        [
            range_faces.reshape(row_count * 6, 256),
            outer_faces[0],
            outer_faces[1],
            jnp.zeros((1, 256), jnp.float32),
        ],
        axis=0,
    )


def lookup(face_table, rows_index):
    blocks = rows_index.shape[0]
    return jnp.take(face_table, rows_index.reshape(-1), axis=0).reshape(blocks, 6, 256)


def table_index(neighbours, range_start, range_len):
    opposite = jnp.array([1, 0, 3, 2, 5, 4], dtype=jnp.int32)
    local_id = neighbours - range_start
    inside = (local_id >= 0) & (local_id < range_len)
    from_below = (neighbours >= 0) & (local_id < 0)
    from_above = local_id >= range_len
    rows_index = jnp.where(inside, local_id * 6 + opposite[None, :], range_len * 8)
    rows_index = jnp.where(from_below, range_len * 6 + local_id + range_len, rows_index)
    return jnp.where(from_above, range_len * 7 + local_id - range_len, rows_index)


def leaf_index(neighbours, blk_here, sub_here, sub_count):
    blocks = neighbours.shape[0]
    opposite = jnp.array([1, 0, 3, 2, 5, 4], dtype=jnp.int32)
    clamped = jnp.maximum(neighbours, 0)
    device_id = clamped // blocks
    local_id = clamped % blocks
    other_blk = device_id // sub_count
    other_sub = device_id % sub_count
    present = neighbours >= 0
    same_blk = present & (other_blk == blk_here)
    same_sub = present & (other_sub == sub_here)
    rows_index = jnp.where(same_blk & same_sub, local_id * 6 + opposite[None, :], blocks * 10)
    rows_index = jnp.where(
        same_blk & (other_sub == sub_here - 1), blocks * 6 + local_id, rows_index
    )
    rows_index = jnp.where(
        same_blk & (other_sub == sub_here + 1), blocks * 7 + local_id, rows_index
    )
    rows_index = jnp.where(
        same_sub & (other_blk == blk_here - 1), blocks * 8 + local_id, rows_index
    )
    rows_index = jnp.where(
        same_sub & (other_blk == blk_here + 1), blocks * 9 + local_id, rows_index
    )
    return rows_index


def leaf_table(values):
    face_rows = block_faces(values)
    blocks = face_rows.shape[0]
    side_rows = jnp.stack([face_rows[:, 0], face_rows[:, 1]], axis=0)
    side_wide = extended(side_rows, (("sub", 0),), 1)
    edge_rows = jnp.stack([face_rows[:, 4], face_rows[:, 5]], axis=0)
    edge_wide = extended(edge_rows, (("blk", 0),), 1)
    return jnp.concatenate(
        [
            face_rows.reshape(blocks * 6, 256),
            side_wide[0],
            side_wide[3],
            edge_wide[0],
            edge_wide[3],
            jnp.zeros((1, 256), jnp.float32),
        ],
        axis=0,
    )


def range_table(values):
    face_rows = block_faces(values)
    edge_rows = jnp.stack([face_rows[:, 4], face_rows[:, 5]], axis=0)
    widened = extended(edge_rows, (("blk", 0),), 1)
    return stack_table(face_rows, jnp.stack([widened[0], widened[3]], axis=0))


def general_local(rhs, leaf_neighbors, parent_neighbors, children, owners, parent_places):
    factor = relax_weight / 6.0
    blk_count = lax.axis_size("blk")
    sub_count = lax.axis_size("sub")
    blk_here = lax.axis_index("blk")
    sub_here = lax.axis_index("sub")
    blocks = rhs.shape[0]
    range_len = blocks * sub_count
    parent_len = range_len // 8
    range_start = blk_here * range_len
    parent_start = blk_here * parent_len
    leaf_rows = leaf_index(leaf_neighbors, blk_here, sub_here, sub_count)
    sweep_one = factor * rhs
    second = jacobi_sweep(sweep_one, rhs, lookup(leaf_table(sweep_one), leaf_rows))
    residual = rhs - apply_operator(second, lookup(leaf_table(second), leaf_rows))
    octant_rows = lax.all_gather(restrict_octants(residual), "sub", axis=0, tiled=True)
    range_children = lax.dynamic_slice_in_dim(children, parent_start, parent_len, 0) - range_start
    ranks_all = slot_ranks(owners.reshape(blk_count, parent_len)).reshape(-1)
    range_owners = lax.dynamic_slice_in_dim(owners, parent_start, parent_len, 0)
    range_ranks = lax.dynamic_slice_in_dim(ranks_all, parent_start, parent_len, 0)
    slot_match = (range_owners[None, :] == sub_here) & (
        range_ranks[None, :] == jnp.arange(PMOST, dtype=jnp.int32)[:, None]
    )
    filled = jnp.any(slot_match, axis=1)
    slot_local = jnp.sum(
        jnp.where(slot_match, jnp.arange(parent_len, dtype=jnp.int32)[None, :], 0), axis=1
    )
    filled_gain = filled.astype(jnp.float32)[:, None, None]
    own_local = sub_here * blocks + jnp.arange(blocks, dtype=jnp.int32)
    matches = range_children.reshape(-1)[None, :] == own_local[:, None]
    flat_place = jnp.sum(
        jnp.where(matches, jnp.arange(parent_len * 8, dtype=jnp.int32)[None, :], 0), axis=1
    )
    leaf_parent = flat_place // 8
    leaf_octant = flat_place % 8
    source = assemble(octant_rows[range_children])
    parent_rows = table_index(
        lax.dynamic_slice_in_dim(parent_neighbors, parent_start, parent_len, 0),
        parent_start,
        parent_len,
    )
    global_places = lax.dynamic_slice_in_dim(parent_places, parent_start, parent_len, 0)
    keep_gain = jnp.ones((parent_len, 1, 1), jnp.float32)
    parent_one = factor * source
    parent_two = jacobi_sweep(parent_one, source, lookup(range_table(parent_one), parent_rows))
    parent_rest = source - apply_operator(parent_two, lookup(range_table(parent_two), parent_rows))
    coarse = coarsen(parent_rest)
    root_slab = (
        jnp.zeros((parent_len, 64), jnp.float32).at[global_places - parent_start].set(coarse)
    )
    ordered = lax.all_gather(root_slab, "blk", axis=0, tiled=True)
    side_y = blocks // 4
    side_x = sub_count // 2
    root_source = (
        ordered.reshape(blk_count, side_y, side_x, 4, 4, 4)
        .transpose(0, 3, 1, 4, 2, 5)
        .reshape(4 * blk_count, 16 * side_y * side_x)
    )
    root_source = root_source - jnp.mean(root_source)
    root_values = jnp.zeros_like(root_source)
    for repeat in range(ROOT_SWEEPS):
        root_values = root_relax(root_values, root_source, 4 * side_x)
    root_back = (
        root_values.reshape(blk_count, 4, side_y, 4, side_x, 4)
        .transpose(0, 2, 4, 1, 3, 5)
        .reshape(blk_count * parent_len, 64)[global_places]
    )
    parent_three = parent_two + widen_root(root_back) * keep_gain
    parent_four = jacobi_sweep(parent_three, source, lookup(range_table(parent_three), parent_rows))
    parent_solution = parent_four[slot_local] * filled_gain
    own_parents = parent_four[leaf_parent]
    pieces = octant_split(own_parents)
    chosen = jnp.take_along_axis(pieces, leaf_octant[:, None, None], axis=1)[:, 0]
    leaf_three = second + widen_leaf(chosen)
    leaf_solution = jacobi_sweep(leaf_three, rhs, lookup(leaf_table(leaf_three), leaf_rows))
    return (leaf_solution, parent_solution)


FACTOR = relax_weight / 6.0
SELF = 1.0 - 6.0 * FACTOR
LANES = 128
OWN_ROWS = 64
MSG_ROWS = 32
VMEM_LIMIT = 16 * 1024 * 1024


def lane_iota(shape):
    return lax.broadcasted_iota(jnp.int32, shape, len(shape) - 1)


def row_iota(shape):
    return lax.broadcasted_iota(jnp.int32, shape, len(shape) - 2)


def turn(values, shift, axis):
    size = values.shape[axis]
    shift = shift % size
    if shift == 0:
        return values
    return pltpu.roll(values, shift, axis)


def split_dot(left, table):
    high = left.astype(jnp.bfloat16)
    low = (left - high.astype(jnp.float32)).astype(jnp.bfloat16)
    return jnp.dot(high, table, preferred_element_type=jnp.float32) + jnp.dot(
        low, table, preferred_element_type=jnp.float32
    )


def zero_one(condition, scale=1.0):
    return np.where(condition, scale, 0.0).astype(jnp.bfloat16)


def key_col(rows, columns):
    return np.arange(rows)[:, None], np.arange(columns)[None, :]


def octant_table():
    key, col = key_col(256, LANES)
    key_x = key % 16
    col_x = col % 8
    return zero_one(
        (key // 32 == col % 64 // 8)
        & (
            ((col < 64) & (key_x // 2 == col_x))
            | ((col >= 64) & (col_x == 7) & (key_x == 0))
            | ((col >= 64) & (col_x == 0) & (key_x == 15))
        ),
        0.5,
    )


def face_table():
    key, col = key_col(256, LANES)
    return zero_one(
        (key // 16 == col % 64)
        & (((col < 64) & (key % 16 == 0)) | ((col >= 64) & (key % 16 == 15)))
    )


def root_table(sub_count):
    key, col = key_col(4 * LANES, 16 * sub_count)
    near_x = key % 8 // 4
    row = (key // LANES) % 2 * 4 + key % LANES // 32
    along = np.where(key < 256, near_x + 1, np.where(near_x == 0, 3, 0))
    return zero_one(col == row * (2 * sub_count) + along, 0.25)


def root_spread_table(sub_count):
    key, col = key_col(16 * sub_count, 256)
    return zero_one(key == (col // 32) * (2 * sub_count) + col % 8 // 4)


def parent_table():
    key, col = key_col(256, 256)
    return zero_one(key == (col % 16 // 8) * LANES + (col // 16) * 8 + col % 8)


def leaf_table_of_cells():
    key, col = key_col(256, 256)
    y = col // 16
    x = col % 16
    return zero_one(key == (y % 2 * 2 + x % 2) * 64 + y // 2 * 8 + x // 2)


def push_table():
    key, col = key_col(LANES, 256)
    group = key // 16
    cell = np.select([group == 0, group == 1, group == 4, group == 5], [0, 15, 1, 14], 16)
    return zero_one((key % 16 == col // 16) & (col % 16 == cell))


def beside_x(chunk, width):
    cell = lane_iota(chunk.shape) % width
    low = jnp.where(cell > 0, turn(chunk, 1, 1), 0.0)
    high = jnp.where(cell < width - 1, turn(chunk, -1, 1), 0.0)
    return low + high


def y_pair(chunks, width):
    lane = lane_iota(chunks[0].shape)
    up = [turn(chunk, width, 1) for chunk in chunks]
    down = [turn(chunk, -width, 1) for chunk in chunks]
    zero = jnp.zeros_like(chunks[0])
    lower = []
    upper = []
    for k in range(len(chunks)):
        before = up[k - 1] if k > 0 else zero
        after = down[k + 1] if k + 1 < len(chunks) else zero
        lower.append(jnp.where(lane < width, before, up[k]))
        upper.append(jnp.where(lane >= LANES - width, after, down[k]))
    return lower, upper


def z_pair(chunk):
    rows = chunk.shape[0]
    row = row_iota(chunk.shape)
    lower = jnp.where(row > 0, turn(chunk, 1, 0), 0.0)
    upper = jnp.where(row < rows - 1, turn(chunk, -1, 0), 0.0)
    return lower, upper


def fine_beside(chunks):
    lower, upper = y_pair(chunks, 16)
    in_x = [beside_x(chunk, 16) for chunk in chunks]
    in_y = [a + b for a, b in zip(lower, upper)]
    in_z = []
    for chunk in chunks:
        below, above = z_pair(chunk)
        in_z.append(below + above)
    return in_x, in_y, in_z


def coarse_turns(columns):
    return (
        [[turn(chunk, 8, 1) for chunk in halves] for halves in columns],
        [[turn(chunk, -8, 1) for chunk in halves] for halves in columns],
    )


def coarse_y_pair(up, down):
    lane = lane_iota(up[0].shape)
    zero = jnp.zeros_like(up[0])
    lower = []
    upper = []
    for half in range(2):
        lower.append(jnp.where(lane < 8, up[half - 1] if half > 0 else zero, up[half]))
        upper.append(jnp.where(lane >= LANES - 8, down[half + 1] if half < 1 else zero, down[half]))
    return lower, upper


def coarse_x_pair(columns, up, down, index, half):
    chunk = columns[index][half]
    cell = lane_iota(chunk.shape) % 8
    before = down[index - 1][half] if index > 0 else jnp.zeros_like(chunk)
    after = up[index + 1][half] if index + 1 < len(columns) else jnp.zeros_like(chunk)
    low = turn(jnp.where(cell == 7, before, chunk), 1, 1)
    high = turn(jnp.where(cell == 0, after, chunk), -1, 1)
    return low, high


def coarse_sums(columns):
    up, down = coarse_turns(columns)

    def sums(index):
        lower, upper = coarse_y_pair(up[index], down[index])
        halves = []
        for half in range(2):
            chunk = columns[index][half]
            low, high = coarse_x_pair(columns, up, down, index, half)
            total = low + high + lower[half] + upper[half]
            halves.append(total + turn(chunk, 1, 0) + turn(chunk, -1, 0))
        return halves

    return sums


def as_column(row):
    count = row.shape[1]
    shape = (count, count)
    return jnp.sum(
        jnp.where(row_iota(shape) == lane_iota(shape), row, 0.0), axis=1, keepdims=True
    )


def power_div(values, divisor):
    return lax.shift_right_logical(values, jnp.full_like(values, divisor.bit_length() - 1))


def power_rem(values, divisor):
    return values & (divisor - 1)


def grid_codes(sub_count, wide_y, child_ref, place_ref):
    side_y = wide_y // 2
    side_x = sub_count // 2
    shape = child_ref.shape
    octant = row_iota(shape)
    place = jnp.broadcast_to(place_ref[...], shape)
    cell_z = 2 * power_div(place, side_y * side_x) + power_div(octant, 4)
    cell_y = 2 * power_rem(power_div(place, side_x), side_y) + power_rem(power_div(octant, 2), 2)
    cell_x = 2 * power_rem(place, side_x) + power_rem(octant, 2)
    return (cell_z * wide_y + cell_y) * sub_count + cell_x


def own_codes(sub_count, blocks, child_ref, codes, sub_here, blk_here):
    first = (blk_here * sub_count + sub_here) * blocks
    codes = codes.astype(jnp.float32)
    return [
        jnp.sum(jnp.where(child_ref[...] == first + slot, codes, 0.0)).astype(jnp.int32)
        for slot in range(blocks)
    ]


def lists_agree(sub_count, blk_count, leaf_ref, parent_ref, child_ref, place_ref, codes, own):
    blocks = len(own)
    wide_y = blocks // 2
    side_y = wide_y // 2
    side_x = sub_count // 2
    parents = child_ref.shape[1]
    layer = wide_y * sub_count
    children = child_ref[...]
    device = power_div(codes, 2 * layer) * sub_count + power_rem(codes, sub_count)
    missed = jnp.where(power_div(children, blocks) != device, 1.0, 0.0)
    faults = jnp.int32(0)
    for slot in range(blocks):
        for axis, (stride, length) in enumerate(
            ((1, sub_count), (sub_count, wide_y), (layer, 2 * blk_count))
        ):
            along = lax.rem(lax.div(own[slot], stride), length)
            for sign in (-1, 1):
                listed = leaf_ref[slot, 2 * axis + (sign + 1) // 2]
                exists = (along + sign >= 0) & (along + sign < length)
                hit = (children == listed) & (codes == own[slot] + sign * stride)
                missed = missed - jnp.where(hit, 1.0, 0.0)
                faults = faults + jnp.where(
                    exists, jnp.where(listed >= 0, 1, -100000), jnp.where(listed < 0, 0, -100000)
                )
    wrong = jnp.abs(jnp.sum(missed) + faults.astype(jnp.float32))
    place_row = place_ref[...].astype(jnp.float32)
    place_column = as_column(place_row)
    number = row_iota((parents, parents))
    place = place_ref[...]
    missed = jnp.zeros((1, parents), jnp.float32)
    for axis, (stride, length) in enumerate(((1, side_x), (side_x, side_y), (side_y * side_x, blk_count))):
        along = power_rem(power_div(place, stride), length)
        for sign in (-1, 1):
            face = 2 * axis + (sign + 1) // 2
            listed = parent_ref[face : face + 1, :]
            found = jnp.sum(jnp.where(number == listed, place_column, 0.0), axis=0, keepdims=True)
            exists = (along + sign >= 0) & (along + sign < length)
            wanted = (place + sign * stride).astype(jnp.float32)
            missed = missed + jnp.where(
                exists,
                jnp.where((listed >= 0) & (found == wanted), 0.0, 1.0),
                jnp.where(listed < 0, 0.0, 1.0),
            )
    wrong = wrong + jnp.sum(missed)
    return jnp.where(wrong == 0.0, 1.0, 0.0)


def limits(sub_count, blk_count):
    sub_here = lax.axis_index("sub")
    blk_here = lax.axis_index("blk")

    def gain(condition):
        return jnp.where(condition, 1.0, 0.0).astype(jnp.float32)

    return (
        sub_here,
        blk_here,
        gain(sub_here > 0),
        gain(sub_here < sub_count - 1),
        gain(blk_here > 0),
        gain(blk_here < blk_count - 1),
    )


def placed_chunks(placed, wide_y):
    chunks = []
    for k in range(2 * wide_y):
        lanes = slice(LANES * (k % 2), LANES * (k % 2) + LANES)
        chunks.append(
            jnp.concatenate([placed[k // 2, :, lanes], placed[wide_y + k // 2, :, lanes]], axis=0)
        )
    return chunks


def return_gain(shape, x_low, x_high, z_low, z_high):
    cell = lane_iota(shape) % 16
    row = row_iota(shape)
    return (
        jnp.where(cell == 0, x_low, 0.0)
        + jnp.where(cell == 15, x_high, 0.0)
        + jnp.where(row == 0, z_low, 0.0)
        + jnp.where(row == shape[0] - 1, z_high, 0.0)
    ) * (FACTOR * FACTOR)


def push_kernel(
    sub_count, blk_count, blk_bits,
    leaf_ref, parent_ref, child_ref, place_ref, rhs_ref, table_a_ref, table_r_ref,
    position_ref, own_ref, *rest
):
    msg_refs = rest[:blk_bits]
    placed, rows_s, rows_g, left_a, coarse_s = rest[blk_bits:]
    blocks = rhs_ref.shape[0]
    wide_y = blocks // 2
    f = FACTOR
    f2 = f * f
    sub_here, blk_here, x_low, x_high, z_low, z_high = limits(sub_count, blk_count)
    codes = grid_codes(sub_count, wide_y, child_ref, place_ref)
    own_code = own_codes(sub_count, blocks, child_ref, codes, sub_here, blk_here)
    layer = wide_y * sub_count
    for slot in range(blocks):
        code = own_code[slot]
        position = lax.rem(lax.div(code, layer), 2) * wide_y + lax.rem(
            lax.div(code, sub_count), wide_y
        )
        position_ref[slot] = position
        placed[position] = rhs_ref[slot]
    s = placed_chunks(placed, wide_y)
    shape = s[0].shape
    top = shape[0] - 1
    back = return_gain(shape, x_low, x_high, z_low, z_high)
    sx, sy, sz = fine_beside(s)
    w = [SELF * a + f * (x + y + z) for a, x, y, z in zip(s, sx, sy, sz)]
    wx, wy, wz = fine_beside(w)
    for k in range(2 * wide_y):
        half = slice(LANES * (k % 2), LANES * (k % 2) + LANES)
        rows_s[k] = SELF * w[k] + f * (wx[k] + wy[k] + wz[k]) + back * s[k]
        base = (SELF * f + f2) * s[k] + f * w[k]
        rows_g[k] = base + f2 * (sy[k] + sz[k])
        gz = base + f2 * (sx[k] + sy[k])
        line = 48 * (k // 2)
        left_a[line + 16 : line + 17, half] = gz[0:1]
        left_a[line + 17 : line + 18, half] = gz[top : top + 1]
        left_a[line + 40 : line + 41, half] = (2.0 * f2) * s[k][0:1]
        left_a[line + 41 : line + 42, half] = (2.0 * f2) * s[k][top : top + 1]
        edge = gz + (f - f2) * s[k]
        for bit in range(blk_bits):
            upward = (blk_here // (1 << bit)) % 2 == 0
            msg_refs[bit][16 + k // 2 : 17 + k // 2, half] = jnp.where(
                upward, edge[top : top + 1], edge[0:1]
            )
            msg_refs[bit][16 + wide_y + k // 2 : 17 + wide_y + k // 2, half] = jnp.where(
                upward, s[k][top : top + 1], s[k][0:1]
            )
    for k in range(2 * wide_y):
        half = slice(LANES * (k % 2), LANES * (k % 2) + LANES)
        line = 48 * (k // 2)
        left_a[line : line + 16, half] = (
            rows_s[k, pl.ds(0, 16, stride=2), :] + rows_s[k, pl.ds(1, 16, stride=2), :]
        )
        left_a[line + 24 : line + 40, half] = (
            rows_g[k, pl.ds(0, 16, stride=2), :] + rows_g[k, pl.ds(1, 16, stride=2), :]
        )
    out_a = split_dot(left_a[...], table_a_ref[...])
    good = lists_agree(
        sub_count, blk_count, leaf_ref, parent_ref, child_ref, place_ref, codes, own_code
    )
    lane24 = lane_iota((24, LANES))
    main = []
    side = []
    for half in range(2):
        first = out_a[96 * half : 96 * half + 24]
        second = out_a[96 * half + 48 : 96 * half + 72]
        main.append(jnp.where(lane24 < 64, first, turn(second, 64, 1)))
        first = out_a[96 * half + 24 : 96 * half + 48]
        second = out_a[96 * half + 72 : 96 * half + 96]
        side.append(jnp.where(lane24 < 64, turn(first, 64, 1), second))
    zero3 = jnp.zeros((3, LANES), jnp.float32)
    for half in range(2):
        lanes = slice(LANES * half, LANES * half + LANES)
        for base_row, piece in ((0, main[half]), (24, side[half])):
            own_ref[base_row : base_row + 3, lanes] = zero3
            own_ref[base_row + 3 : base_row + 4, lanes] = piece[16:17] * z_low
            own_ref[base_row + 4 : base_row + 20, lanes] = piece[0:16]
            own_ref[base_row + 20 : base_row + 21, lanes] = piece[17:18] * z_high
            own_ref[base_row + 21 : base_row + 24, lanes] = zero3
    cell8 = lane24 % 8
    row24 = row_iota((24, LANES))
    inside_z = jnp.where(row24 < 4, z_low, jnp.where(row24 >= 20, z_high, 1.0))
    gain = [inside_z * x_low, inside_z, inside_z * x_high]
    main24 = [own_ref[0:24, 0:LANES], own_ref[0:24, LANES:256]]
    side24 = [own_ref[24:48, 0:LANES], own_ref[24:48, LANES:256]]
    columns = [
        [jnp.where(cell8 == 7, piece, 0.0) * x_low for piece in side24],
        main24,
        [jnp.where(cell8 == 0, piece, 0.0) * x_high for piece in side24],
    ]
    sums = coarse_sums(columns)
    wp = []
    for b in range(3):
        near = sums(b)
        wp.append([gain[b] * (SELF * columns[b][h] + f * near[h]) for h in range(2)])
    sums = coarse_sums(wp)
    zero8 = jnp.zeros((8, LANES), jnp.float32)
    for b in range(3):
        near = sums(b)
        for h in range(2):
            coarse_s[2 * b + h, 0:24] = gain[b] * (SELF * wp[b][h] + f * near[h])
            coarse_s[2 * b + h, 24:32] = zero8
    pieces = []
    low_cells = lane_iota((8, LANES)) % 8 < 4
    for k in range(6):
        pieces.append(
            coarse_s[k, pl.ds(0, 8, stride=4), :]
            + coarse_s[k, pl.ds(1, 8, stride=4), :]
            + coarse_s[k, pl.ds(2, 8, stride=4), :]
            + coarse_s[k, pl.ds(3, 8, stride=4), :]
        )
    outer = [jnp.where(low_cells, pieces[4 + h], pieces[h]) for h in range(2)]
    root_left = jnp.concatenate([pieces[2], pieces[3]] + outer, axis=1)
    root_lanes = 16 * sub_count
    root_part = split_dot(root_left, table_r_ref[...])
    root_part = pltpu.roll(root_part, 2 * sub_here + root_lanes - 1, 1)
    root_part = jnp.where(row_iota(root_part.shape) < 6, root_part, 0.0)
    own_ref[48:56, 0:root_lanes] = root_part
    if root_lanes < 256:
        own_ref[48:56, root_lanes:256] = jnp.zeros((8, 256 - root_lanes), jnp.float32)
    flag = jnp.zeros((8, LANES), jnp.float32) + good
    for lanes in (slice(0, LANES), slice(LANES, 256)):
        own_ref[56:64, lanes] = flag
    for bit in range(blk_bits):
        upward = (blk_here // (1 << bit)) % 2 == 0
        ref = msg_refs[bit]
        ref[8:16, :] = own_ref[48:56, :]
        ref[24:32, 0:LANES] = zero8
        ref[24:32, LANES:256] = flag
        for base_row, source in ((0, 0), (4, 24)):
            ref[base_row : base_row + 4, :] = jnp.where(
                upward, own_ref[source + 17 : source + 21, :], own_ref[source + 3 : source + 7, :]
            )


def side_kernel(
    sub_count, blk_count, slots,
    positions, owner_ref, place_ref, rhs_ref, table_ref,
    slot_ref, part_ref, faces_ref,
    placed, left_c
):
    blocks = rhs_ref.shape[0]
    wide_y = blocks // 2
    f = FACTOR
    f2 = f * f
    sub_here, blk_here, x_low, x_high, z_low, z_high = limits(sub_count, blk_count)
    for slot in range(blocks):
        placed[positions[slot]] = rhs_ref[slot]
    s = placed_chunks(placed, wide_y)
    back = return_gain(s[0].shape, x_low, x_high, z_low, z_high)
    sx, sy, sz = fine_beside(s)
    w = [SELF * a + f * (x + y + z) for a, x, y, z in zip(s, sx, sy, sz)]
    wx, wy, wz = fine_beside(w)
    for k in range(2 * wide_y):
        half = slice(LANES * (k % 2), LANES * (k % 2) + LANES)
        r = SELF * w[k] + f * (wx[k] + wy[k] + wz[k]) + back * s[k]
        part = f * (s[k] + w[k] + r)
        part_ref[k // 2, :, half] = part[:16]
        part_ref[wide_y + k // 2, :, half] = part[16:]
        line = 64 * (k // 2)
        left_c[line : line + 32, half] = (
            (SELF * f + f) * s[k] + f * w[k] + f2 * (sy[k] + sz[k])
        )
        left_c[line + 32 : line + 64, half] = s[k]
    out_c = split_dot(left_c[...], table_ref[...])
    faces = out_c[0:64]
    for yy in range(1, wide_y):
        faces = faces + turn(out_c[64 * yy : 64 * yy + 64], 16 * yy, 1)
    faces_ref[...] = faces
    owned = owned_slots(sub_count, blk_count, slots, sub_here, blk_here, owner_ref, place_ref)
    for k in range(slots):
        for j in range(3):
            slot_ref[3 * k + j] = owned[k][j]


def neighbour_pick(blk_here, blk_count, msg_refs):
    spans = []
    step = 1
    while step < blk_count:
        spans.append(step)
        step = 2 * step + 1

    def picker(other):
        choices = [(blk_here ^ other) == d for d in spans]

        def read(rows, lanes):
            value = msg_refs[spans[-1] - 1][rows, lanes]
            for choice, d in zip(choices[:-1], spans[:-1]):
                value = jnp.where(choice, msg_refs[d - 1][rows, lanes], value)
            return value

        return read

    return picker(blk_here - 1), picker(blk_here + 1)


def root_tiles(sub_count, blk_count):
    return (sub_count * blk_count // 16 + 1) // 2


def join_kernel(sub_count, blk_count, own_ref, faces_ref, *rest):
    msg_refs = rest[: blk_count - 1]
    out_ref, lines_ref, root_s = rest[blk_count - 1 :]
    _, blk_here, _, _, z_low, z_high = limits(sub_count, blk_count)
    below, above = neighbour_pick(blk_here, blk_count, msg_refs)
    row8 = row_iota((8, LANES))
    low_rows = (row8 >= 1) & (row8 < 5)
    high_rows = (row8 >= 3) & (row8 < 7)
    good = own_ref[56:64, 0:LANES]
    for ref in msg_refs:
        good = jnp.minimum(good, ref[24:32, LANES:256])
    for half in range(2):
        lanes = slice(LANES * half, LANES * half + LANES)
        low = below(slice(0, 8), lanes) * z_low
        high = above(slice(0, 8), lanes) * z_high
        for base, low_turn, high_turn in ((0, 1, 3), (24, 5, 7)):
            out_ref[base : base + 8, lanes] = own_ref[base : base + 8, lanes] + jnp.where(
                low_rows, turn(low, low_turn, 0), 0.0
            )
            out_ref[base + 8 : base + 16, lanes] = own_ref[base + 8 : base + 16, lanes]
            out_ref[base + 16 : base + 24, lanes] = own_ref[
                base + 16 : base + 24, lanes
            ] + jnp.where(high_rows, turn(high, high_turn, 0), 0.0)
        out_ref[23:24, lanes] = good[0:1]
    root_s[...] = jnp.zeros(root_s.shape, jnp.float32)
    for d in range(blk_count):
        start = 4 * (blk_here ^ d) + 3
        for part in range(root_s.shape[0]):
            lanes = slice(LANES * part, LANES * part + LANES)
            value = own_ref[48:56, lanes] if d == 0 else msg_refs[d - 1][8:16, lanes]
            root_s[part, pl.ds(start, 8), :] = root_s[part, pl.ds(start, 8), :] + value
    tile = 0
    for start in range(0, 4 * blk_count, 8):
        for part in range(root_s.shape[0]):
            row = 48 + 8 * (tile // 2)
            lanes = slice(LANES * (tile % 2), LANES * (tile % 2) + LANES)
            out_ref[row : row + 8, lanes] = root_s[part, 4 + start : 12 + start]
            tile += 1
    row = 48 + 8 * root_tiles(sub_count, blk_count)
    count = lines_ref.shape[0] // 2
    half = count // 2
    low = below(slice(16, 16 + count), slice(0, 256)) * z_low
    high = above(slice(16, 16 + count), slice(0, 256)) * z_high
    lines_ref[0:count] = low
    lines_ref[count : 2 * count] = high
    out_ref[row : row + half, :] = low[half:count]
    out_ref[row + half : row + count, :] = high[half:count]
    out_ref[row + 8 : row + 40, 0:LANES] = faces_ref[0:32]
    out_ref[row + 8 : row + 40, LANES:256] = faces_ref[32:64]


def owned_slots(sub_count, blk_count, slots, sub_here, blk_here, owner_ref, place_ref):
    parents = owner_ref.shape[1]
    parent_len = parents // blk_count
    side_x = sub_count // 2
    side_y = parent_len // side_x
    number = lane_iota((1, parents))
    here = (owner_ref[...] == sub_here) & (lax.div(number, parent_len) == blk_here)
    mine = jnp.where(here, 1.0, 0.0)
    shape = (parents, parents)
    rank = jnp.sum(
        jnp.where(row_iota(shape) < lane_iota(shape), as_column(mine), 0.0), axis=0, keepdims=True
    )
    places = place_ref[...].astype(jnp.float32)
    found = []
    for k in range(slots):
        chosen = jnp.where(rank == float(k), mine, 0.0)
        place = jnp.sum(chosen * places).astype(jnp.int32)
        found.append(
            (
                lax.rem(lax.div(place, side_x), side_y),
                lax.rem(place, side_x),
                jnp.sum(chosen).astype(jnp.int32),
            )
        )
    return found


def solve_kernel(
    sub_count, blk_count, slots,
    positions, owned, all_ref, part_ref, lines_ref, table_w_ref, table_p_ref, table_l_ref, table_x_ref,
    leaf_ref, parent_ref, good_ref,
    placed, par_s, root_s, fine_s, push_s
):
    blocks = part_ref.shape[0]
    wide_y = blocks // 2
    f = FACTOR
    f2 = f * f
    sub_here, blk_here, x_low, x_high, z_low, z_high = limits(sub_count, blk_count)
    row8 = row_iota((8, LANES))
    cell24 = lane_iota((24, LANES)) % 8
    row24 = row_iota((24, LANES))
    good = all_ref[0, 16:24, 0:LANES]
    for c in range(1, sub_count):
        good = jnp.minimum(good, all_ref[c, 16:24, 0:LANES])
    good_ref[0] = jnp.min(jnp.where(row8 == 7, good, 1.0)).astype(jnp.int32)
    source = []
    for c in range(sub_count):
        halves = []
        for half in range(2):
            lanes = slice(LANES * half, LANES * half + LANES)
            value = all_ref[c, 0:24, lanes]
            if c + 1 < sub_count:
                value = value + jnp.where(cell24 == 7, all_ref[c + 1, 24:48, lanes], 0.0)
            if c > 0:
                value = value + jnp.where(cell24 == 0, all_ref[c - 1, 24:48, lanes], 0.0)
            halves.append(value)
        source.append(halves)

    root_lanes = 16 * sub_count
    row_len = 2 * sub_count
    root_rows = 4 * blk_count
    parts = root_lanes // LANES
    tile_rows = []
    tile = 0
    for _ in range(0, root_rows, 8):
        pieces = []
        for part in range(parts):
            row = 48 + 8 * (tile // 2)
            lanes = slice(LANES * (tile % 2), LANES * (tile % 2) + LANES)
            total = all_ref[0, row : row + 8, lanes]
            for c in range(1, sub_count):
                total = total + all_ref[c, row : row + 8, lanes]
            pieces.append(total)
            tile += 1
        tile_rows.append(jnp.concatenate(pieces, axis=1))
    root_source = jnp.concatenate(tile_rows, axis=0)
    root_source = root_source - jnp.sum(root_source) / (root_rows * root_lanes)
    shape = root_source.shape
    lane = lane_iota(shape)
    row = row_iota(shape)

    def root_sweep(values):
        total = jnp.where(lane % row_len > 0, turn(values, 1, 1), 0.0)
        total = total + jnp.where(lane % row_len < row_len - 1, turn(values, -1, 1), 0.0)
        total = total + jnp.where(lane >= row_len, turn(values, row_len, 1), 0.0)
        total = total + jnp.where(lane < root_lanes - row_len, turn(values, -row_len, 1), 0.0)
        total = total + jnp.where(row > 0, turn(values, 1, 0), 0.0)
        total = total + jnp.where(row < root_rows - 1, turn(values, -1, 0), 0.0)
        return SELF * values + f * (root_source + total)

    values = f * root_source
    left_sweeps = ROOT_SWEEPS - 1
    sums = coarse_sums(source)
    two = []
    for c in range(sub_count):
        if left_sweeps > 0:
            values = root_sweep(values)
            left_sweeps -= 1
        near = sums(c)
        two.append(
            [(f + f * SELF) * source[c][half] + f2 * near[half] for half in range(2)]
        )
    for _ in range(left_sweeps):
        values = root_sweep(values)
    root_s[...] = jnp.zeros(root_s.shape, jnp.float32)
    for part in range(parts):
        root_s[part, 4 : 4 + root_rows] = values[:, LANES * part : LANES * part + LANES]
    mine = jnp.concatenate(
        [root_s[part, pl.ds(4 * blk_here + 3, 8), :] for part in range(parts)], axis=1
    )
    left = jnp.concatenate([turn(mine, -2 * c, 1) for c in range(sub_count)], axis=0)
    wide = split_dot(left, table_w_ref[...])

    valid = (
        (row24 >= 2)
        & (row24 < 22)
        & ((row24 >= 4) | (z_low > 0.0))
        & ((row24 < 20) | (z_high > 0.0))
    )
    three = []
    for c in range(sub_count):
        halves = []
        for half in range(2):
            lanes = slice(LANES * half, LANES * half + LANES)
            tiles = []
            for t in range(3):
                first = wide[8 * c + 2 * t : 8 * c + 2 * t + 1, lanes]
                second = wide[8 * c + 2 * t + 1 : 8 * c + 2 * t + 2, lanes]
                tiles.append(
                    jnp.where(
                        row8 < 4,
                        jnp.broadcast_to(first, (8, LANES)),
                        jnp.broadcast_to(second, (8, LANES)),
                    )
                )
            value = two[c][half] + jnp.concatenate(tiles, axis=0)
            halves.append(jnp.where(valid, value, 0.0))
        three.append(halves)
    sums = coarse_sums(three)
    for c in range(sub_count):
        near = sums(c)
        for half in range(2):
            value = SELF * three[c][half] + f * (near[half] + source[c][half])
            par_s[c, half] = jnp.where(valid, value, 0.0)

    pieces = []
    for k in range(slots):
        half = owned[3 * k]
        place_x = owned[3 * k + 1]
        filled = owned[3 * k + 2].astype(jnp.float32)
        pieces.append(
            jnp.concatenate(
                [par_s[2 * place_x, half, 4:20], par_s[2 * place_x + 1, half, 4:20]], axis=1
            )
            * filled
        )
    left = jnp.concatenate(pieces, axis=0)
    moved = split_dot(left, table_p_ref[...])
    for k in range(slots):
        parent_ref[k] = moved[16 * k : 16 * k + 16]

    before = jnp.maximum(sub_here - 1, 0)
    after = jnp.minimum(sub_here + 1, sub_count - 1)
    columns = [
        [par_s[before, half] * x_low for half in range(2)],
        [par_s[sub_here, half] for half in range(2)],
        [par_s[after, half] * x_high for half in range(2)],
    ]
    centre = columns[1]
    up, down = coarse_turns(columns)
    in_y = coarse_y_pair(up[1], down[1])
    lane16 = lane_iota((16, LANES))
    left_rows = []
    in_x = [coarse_x_pair(columns, up, down, 1, half) for half in range(2)]
    blend = {}
    for half in range(2):
        for zp in range(2):
            base = (SELF + 3.0 * f) * centre[half] + f * turn(centre[half], 1 - 2 * zp, 0)
            for yp in range(2):
                for xp in range(2):
                    value = base + f * (in_y[yp][half] + in_x[half][xp])
                    blend[half, zp, 2 * yp + xp] = value[4:20]
    for yy in range(wide_y):
        half = yy // 2
        for zp in range(2):
            pair = []
            for v in (0, 2):
                first = blend[half, zp, v]
                second = blend[half, zp, v + 1]
                if yy % 2 == 0:
                    second = turn(second, 64, 1)
                else:
                    first = turn(first, 64, 1)
                pair.append(jnp.where(lane16 < 64, first, second))
            left_rows.append(jnp.concatenate(pair, axis=1))
    left = jnp.concatenate(left_rows, axis=0)
    spread = split_dot(left, table_l_ref[...])
    for yy in range(wide_y):
        for zp in range(2):
            top = 16 * (2 * yy + zp)
            fine_s[2 * yy, pl.ds(zp, 16, stride=2), :] = spread[top : top + 16, 0:128]
            fine_s[2 * yy + 1, pl.ds(zp, 16, stride=2), :] = spread[top : top + 16, 128:256]

    line = 48 + 8 * root_tiles(sub_count, blk_count)
    lane64 = lane_iota((32, LANES))
    from_low = all_ref[before, line + 8 : line + 40, 0:LANES] * x_low
    low_values = all_ref[before, line + 8 : line + 40, LANES:256] * x_low
    from_high = all_ref[after, line + 8 : line + 40, 0:LANES] * x_high
    high_values = all_ref[after, line + 8 : line + 40, LANES:256] * x_high
    left = jnp.concatenate(
        [
            jnp.where(lane64 < 64, turn(from_low, 64, 1), f2 * low_values),
            jnp.where(lane64 < 64, from_high, f2 * turn(high_values, 64, 1)),
        ],
        axis=1,
    )
    lane128 = lane_iota((32, LANES))
    rows = []
    for yy in range(wide_y):
        rows.append(
            jnp.where(
                lax.rem(lane128, 64) < 16,
                turn(left[:, 0:LANES], -16 * yy, 1),
                turn(left[:, LANES:256], 16 - 16 * yy, 1),
            )
        )
    push = split_dot(jnp.concatenate(rows, axis=0), table_x_ref[...])
    for yy in range(wide_y):
        push_s[:, 256 * yy : 256 * yy + 256] = push[32 * yy : 32 * yy + 32]
    cell = lane_iota((2 * wide_y, 256)) % 16
    across = jnp.where(
        cell == 0, turn(all_ref[before, line : line + 2 * wide_y, :], -15, 1) * x_low, 0.0
    ) + jnp.where(
        cell == 15, turn(all_ref[after, line : line + 2 * wide_y, :], 15, 1) * x_high, 0.0
    )
    across = (2.0 * f2) * across
    count = 2 * wide_y
    for yy in range(wide_y):
        lanes = slice(256 * yy, 256 * yy + 256)
        push_s[0:1, lanes] = push_s[0:1, lanes] + lines_ref[yy : yy + 1] + across[yy : yy + 1]
        push_s[1:2, lanes] = push_s[1:2, lanes] + f2 * lines_ref[wide_y + yy : wide_y + yy + 1]
        push_s[31:32, lanes] = (
            push_s[31:32, lanes]
            + lines_ref[count + yy : count + yy + 1]
            + across[wide_y + yy : wide_y + yy + 1]
        )
        push_s[30:31, lanes] = (
            push_s[30:31, lanes]
            + f2 * lines_ref[count + wide_y + yy : count + wide_y + yy + 1]
        )
    for zz in range(2):
        for yy in range(wide_y):
            rows = slice(16 * zz, 16 * zz + 16)
            lanes = slice(256 * yy, 256 * yy + 256)
            index = zz * wide_y + yy
            fine = jnp.concatenate([fine_s[2 * yy, rows], fine_s[2 * yy + 1, rows]], axis=1)
            placed[index] = part_ref[index] + fine + f * push_s[rows, lanes]
    for slot in range(blocks):
        leaf_ref[slot] = placed[positions[slot]]


def paired(count, step):
    return [(i, i ^ step) for i in range(count)]


def is_power(number):
    return number > 0 and number & (number - 1) == 0


def local(rhs, leaf_neighbors, parent_neighbors, children, owners, parent_places):
    blk_count = lax.axis_size("blk")
    sub_count = lax.axis_size("sub")
    blocks = rhs.shape[0]
    wide_y = blocks // 2
    lists = (leaf_neighbors, parent_neighbors, children, owners, parent_places)
    fits = 32 * blocks == 2 * LANES and 16 * sub_count in (LANES, 2 * LANES)
    if not (fits and blk_count > 1 and is_power(blk_count)):
        return general_local(rhs, *lists)
    blk_bits = blk_count.bit_length() - 1
    f32 = jnp.float32
    vmem = pl.BlockSpec(memory_space=pltpu.VMEM)
    smem = pl.BlockSpec(memory_space=pltpu.SMEM)
    params = pltpu.CompilerParams(vmem_limit_bytes=VMEM_LIMIT)
    owner_row = owners.reshape(1, -1)
    place_row = parent_places.reshape(1, -1)
    outs = pl.pallas_call(
        functools.partial(push_kernel, sub_count, blk_count, blk_bits),
        name="push",
        out_shape=[
            jax.ShapeDtypeStruct((blocks,), jnp.int32),
            jax.ShapeDtypeStruct((OWN_ROWS, 256), f32),
        ]
        + [jax.ShapeDtypeStruct((MSG_ROWS, 256), f32)] * blk_bits,
        in_specs=[smem] + [vmem] * 6,
        out_specs=[smem] + [vmem] * (1 + blk_bits),
        scratch_shapes=[
            pltpu.VMEM((blocks, 16, 256), f32),
            pltpu.VMEM((2 * wide_y, 32, LANES), f32),
            pltpu.VMEM((2 * wide_y, 32, LANES), f32),
            pltpu.VMEM((48 * wide_y, 256), f32),
            pltpu.VMEM((6, 32, LANES), f32),
        ],
        compiler_params=params,
    )(
        leaf_neighbors, parent_neighbors.T, children.T, place_row, rhs,
        jnp.asarray(octant_table()), jnp.asarray(root_table(sub_count)),
    )
    positions, own = outs[:2]
    messages = outs[2:]
    received = [
        lax.ppermute(messages[d.bit_length() - 1], "blk", paired(blk_count, d))
        for d in range(1, blk_count)
    ]
    owned, own_part, faces = pl.pallas_call(
        functools.partial(side_kernel, sub_count, blk_count, PMOST),
        name="side",
        out_shape=[
            jax.ShapeDtypeStruct((3 * PMOST,), jnp.int32),
            jax.ShapeDtypeStruct((blocks, 16, 256), f32),
            jax.ShapeDtypeStruct((64, LANES), f32),
        ],
        in_specs=[smem] + [vmem] * 4,
        out_specs=[smem] + [vmem] * 2,
        scratch_shapes=[
            pltpu.VMEM((blocks, 16, 256), f32),
            pltpu.VMEM((64 * wide_y, 256), f32),
        ],
        compiler_params=params,
    )(positions, owner_row, place_row, rhs, jnp.asarray(face_table()))
    root_parts = 16 * sub_count // LANES
    joined_rows = 48 + 8 * root_tiles(sub_count, blk_count) + 8 + 32
    joined, lines = pl.pallas_call(
        functools.partial(join_kernel, sub_count, blk_count),
        name="join",
        out_shape=[
            jax.ShapeDtypeStruct((joined_rows, 256), f32),
            jax.ShapeDtypeStruct((4 * wide_y, 256), f32),
        ],
        in_specs=[vmem] * (1 + blk_count),
        out_specs=[vmem] * 2,
        scratch_shapes=[pltpu.VMEM((root_parts, 4 * blk_count + 8, LANES), f32)],
        compiler_params=params,
    )(own, faces, *received)
    gathered = lax.all_gather(joined, "sub", axis=0, tiled=False)
    leaf_solution, parent_solution, good = pl.pallas_call(
        functools.partial(solve_kernel, sub_count, blk_count, PMOST),
        name="solve",
        out_shape=[
            jax.ShapeDtypeStruct((blocks, 16, 256), f32),
            jax.ShapeDtypeStruct((PMOST, 16, 256), f32),
            jax.ShapeDtypeStruct((1,), jnp.int32),
        ],
        in_specs=[smem] * 2 + [vmem] * 7,
        out_specs=[vmem] * 2 + [smem],
        scratch_shapes=[
            pltpu.VMEM((blocks, 16, 256), f32),
            pltpu.VMEM((sub_count, 2, 24, LANES), f32),
            pltpu.VMEM((root_parts, 4 * blk_count + 8, LANES), f32),
            pltpu.VMEM((2 * wide_y, 32, LANES), f32),
            pltpu.VMEM((32, 256 * wide_y), f32),
        ],
        compiler_params=params,
    )(
        positions, owned, gathered, own_part, lines,
        jnp.asarray(root_spread_table(sub_count)), jnp.asarray(parent_table()),
        jnp.asarray(leaf_table_of_cells()), jnp.asarray(push_table()),
    )

    def general(state):
        return (*general_local(rhs, *lists), jnp.ones_like(state[2]))

    state = lax.while_loop(
        lambda state: state[2][0] == 0, general, (leaf_solution, parent_solution, good)
    )
    return state[0], state[1]


def solution(mesh):
    in_specs = (P(("blk", "sub"), None, None), P(("blk", "sub"), None), P(), P(), P(), P())
    out_specs = (P(("blk", "sub"), None, None), P(("blk", "sub"), None, None))
    return jax.shard_map(local, mesh=mesh, in_specs=in_specs, out_specs=out_specs, check_vma=False)
```

```python
import functools

import jax
import jax.numpy as jnp
from jax import lax
import numpy as np
from jax.experimental import pallas as pl
from jax.experimental.pallas import tpu as pltpu
from jax.sharding import PartitionSpec as P

ROOT_SWEEPS = 8
PMOST = 3


relax_weight = 0.8


def extended(block, sides, width):
    for axis, dim in sides:
        count = lax.axis_size(axis)
        forward = [(i, i + 1) for i in range(count - 1)]
        backward = [(target, source) for source, target in forward]
        low = lax.ppermute(
            lax.slice_in_dim(block, block.shape[dim] - width, None, axis=dim), axis, forward
        )
        high = lax.ppermute(lax.slice_in_dim(block, 0, width, axis=dim), axis, backward)
        block = jnp.concatenate([low, block, high], axis=dim)
    return block


def lane_parts():
    lanes = jnp.arange(256, dtype=jnp.int32)
    return (lanes // 16, lanes % 16)


def exact_dot(left, table):
    return jnp.einsum("...k,kl->...l", left, table, precision=lax.Precision.HIGHEST)


def spread_table(column):
    lane_y, lane_x = lane_parts()
    picked = (jnp.arange(16, dtype=jnp.int32)[:, None] == lane_y[None, :]) & (
        lane_x[None, :] == column
    )
    return picked.astype(jnp.float32)


def block_faces(values):
    blocks = values.shape[0]
    stacked = jnp.stack(
        [
            values[:, :, 0::16].reshape(blocks, 256),
            values[:, :, 15::16].reshape(blocks, 256),
            values[:, :, 0:16].reshape(blocks, 256),
            values[:, :, 240:256].reshape(blocks, 256),
            values[:, 0],
            values[:, 15],
        ],
        axis=1,
    )
    return stacked


def apply_operator(values, ghosts):
    blocks = values.shape[0]
    lane_y, lane_x = lane_parts()
    ghost_x_low = ghosts[:, 0].reshape(blocks, 16, 16)
    ghost_x_high = ghosts[:, 1].reshape(blocks, 16, 16)
    ghost_y_low = ghosts[:, 2].reshape(blocks, 16, 16)
    ghost_y_high = ghosts[:, 3].reshape(blocks, 16, 16)
    from_left = jnp.where(
        lane_x[None, None, :] > 0, jnp.pad(values, ((0, 0), (0, 0), (1, 0)))[:, :, :256], 0.0
    )
    from_right = jnp.where(
        lane_x[None, None, :] < 15, jnp.pad(values, ((0, 0), (0, 0), (0, 1)))[:, :, 1:], 0.0
    )
    beside_all = from_left + exact_dot(ghost_x_low, spread_table(0))
    beside_all = beside_all + from_right + exact_dot(ghost_x_high, spread_table(15))
    beside_all = (
        beside_all
        + jnp.pad(values, ((0, 0), (0, 0), (16, 0)))[:, :, :256]
        + jnp.pad(ghost_y_low, ((0, 0), (0, 0), (0, 240)))
    )
    beside_all = (
        beside_all
        + jnp.pad(values, ((0, 0), (0, 0), (0, 16)))[:, :, 16:]
        + jnp.pad(ghost_y_high, ((0, 0), (0, 0), (240, 0)))
    )
    beside_all = beside_all + jnp.concatenate([ghosts[:, 4][:, None], values[:, :-1]], axis=1)
    beside_all = beside_all + jnp.concatenate([values[:, 1:], ghosts[:, 5][:, None]], axis=1)
    return 6.0 * values - beside_all


def jacobi_sweep(values, forcing, ghosts):
    return values + relax_weight / 6.0 * (forcing - apply_operator(values, ghosts))


def restrict_table():
    lane_y, lane_x = lane_parts()
    target = lane_y // 2 * 8 + lane_x // 2
    return (target[:, None] == jnp.arange(64, dtype=jnp.int32)[None, :]).astype(jnp.float32)


def coarse_table():
    lane_y, lane_x = lane_parts()
    target = lane_y // 4 * 4 + lane_x // 4
    return (target[:, None] == jnp.arange(16, dtype=jnp.int32)[None, :]).astype(jnp.float32)


def place_table():
    source_id = jnp.arange(256, dtype=jnp.int32)
    octant_y = source_id // 128
    octant_x = source_id // 64 % 2
    inner_y = source_id // 8 % 8
    inner_x = source_id % 8
    target = (8 * octant_y + inner_y) * 16 + 8 * octant_x + inner_x
    return (target[:, None] == jnp.arange(256, dtype=jnp.int32)[None, :]).astype(jnp.float32)


def restrict_octants(values):
    blocks = values.shape[0]
    paired = values.reshape(blocks, 8, 2, 256).sum(axis=2)
    return (exact_dot(paired, restrict_table()) * 0.5).reshape(blocks, 512)


def assemble(octant_rows):
    blocks = octant_rows.shape[0]
    arranged = (
        octant_rows.reshape(blocks, 2, 2, 2, 8, 64)
        .transpose(0, 1, 4, 2, 3, 5)
        .reshape(blocks, 16, 256)
    )
    return exact_dot(arranged, place_table())


def coarsen(values):
    blocks = values.shape[0]
    layered = values.reshape(blocks, 4, 4, 256).sum(axis=2)
    return (exact_dot(layered, coarse_table()) * 0.25).reshape(blocks, 64)


def widen_root(coarse):
    blocks = coarse.shape[0]
    flat = exact_dot(coarse.reshape(blocks, 4, 16), coarse_table().T)
    return jnp.repeat(flat, 4, axis=1)


def octant_split(values):
    blocks = values.shape[0]
    moved = exact_dot(values, place_table().T)
    return moved.reshape(blocks, 2, 8, 2, 2, 64).transpose(0, 1, 3, 4, 2, 5).reshape(blocks, 8, 512)


def widen_leaf(octant):
    blocks = octant.shape[0]
    flat = exact_dot(octant.reshape(blocks, 8, 64), restrict_table().T)
    return jnp.repeat(flat, 2, axis=1)


def slot_ranks(range_owners):
    width = range_owners.shape[1]
    same_owner = range_owners[:, :, None] == range_owners[:, None, :]
    earlier = (
        jnp.arange(width, dtype=jnp.int32)[:, None] > jnp.arange(width, dtype=jnp.int32)[None, :]
    )
    return jnp.sum(same_owner & earlier[None], axis=2)


def root_relax(root_values, root_source, row_len):
    plane_len = root_values.shape[1]
    padded_z = jnp.pad(root_values, ((1, 1), (0, 0)))
    padded_row = jnp.pad(root_values, ((0, 0), (row_len, row_len)))
    column_x = jnp.arange(plane_len, dtype=jnp.int32)[None, :] % row_len
    beside_all = padded_z[:-2] + padded_z[2:]
    beside_all = (
        beside_all
        + padded_row[:, :plane_len]
        + padded_row[:, 2 * row_len : 2 * row_len + plane_len]
    )
    beside_all = beside_all + jnp.where(
        column_x > 0, padded_row[:, row_len - 1 : row_len - 1 + plane_len], 0.0
    )
    beside_all = beside_all + jnp.where(
        column_x < row_len - 1, padded_row[:, row_len + 1 : row_len + 1 + plane_len], 0.0
    )
    return root_values + relax_weight / 6.0 * (root_source - (6.0 * root_values - beside_all))


def stack_table(range_faces, outer_faces):
    row_count = range_faces.shape[0]
    return jnp.concatenate(
        [
            range_faces.reshape(row_count * 6, 256),
            outer_faces[0],
            outer_faces[1],
            jnp.zeros((1, 256), jnp.float32),
        ],
        axis=0,
    )


def lookup(face_table, rows_index):
    blocks = rows_index.shape[0]
    return jnp.take(face_table, rows_index.reshape(-1), axis=0).reshape(blocks, 6, 256)


def table_index(neighbours, range_start, range_len):
    opposite = jnp.array([1, 0, 3, 2, 5, 4], dtype=jnp.int32)
    local_id = neighbours - range_start
    inside = (local_id >= 0) & (local_id < range_len)
    from_below = (neighbours >= 0) & (local_id < 0)
    from_above = local_id >= range_len
    rows_index = jnp.where(inside, local_id * 6 + opposite[None, :], range_len * 8)
    rows_index = jnp.where(from_below, range_len * 6 + local_id + range_len, rows_index)
    return jnp.where(from_above, range_len * 7 + local_id - range_len, rows_index)


def leaf_index(neighbours, blk_here, sub_here, sub_count):
    blocks = neighbours.shape[0]
    opposite = jnp.array([1, 0, 3, 2, 5, 4], dtype=jnp.int32)
    clamped = jnp.maximum(neighbours, 0)
    device_id = clamped // blocks
    local_id = clamped % blocks
    other_blk = device_id // sub_count
    other_sub = device_id % sub_count
    present = neighbours >= 0
    same_blk = present & (other_blk == blk_here)
    same_sub = present & (other_sub == sub_here)
    rows_index = jnp.where(same_blk & same_sub, local_id * 6 + opposite[None, :], blocks * 10)
    rows_index = jnp.where(
        same_blk & (other_sub == sub_here - 1), blocks * 6 + local_id, rows_index
    )
    rows_index = jnp.where(
        same_blk & (other_sub == sub_here + 1), blocks * 7 + local_id, rows_index
    )
    rows_index = jnp.where(
        same_sub & (other_blk == blk_here - 1), blocks * 8 + local_id, rows_index
    )
    rows_index = jnp.where(
        same_sub & (other_blk == blk_here + 1), blocks * 9 + local_id, rows_index
    )
    return rows_index


def leaf_table(values):
    face_rows = block_faces(values)
    blocks = face_rows.shape[0]
    side_rows = jnp.stack([face_rows[:, 0], face_rows[:, 1]], axis=0)
    side_wide = extended(side_rows, (("sub", 0),), 1)
    edge_rows = jnp.stack([face_rows[:, 4], face_rows[:, 5]], axis=0)
    edge_wide = extended(edge_rows, (("blk", 0),), 1)
    return jnp.concatenate(
        [
            face_rows.reshape(blocks * 6, 256),
            side_wide[0],
            side_wide[3],
            edge_wide[0],
            edge_wide[3],
            jnp.zeros((1, 256), jnp.float32),
        ],
        axis=0,
    )


def range_table(values):
    face_rows = block_faces(values)
    edge_rows = jnp.stack([face_rows[:, 4], face_rows[:, 5]], axis=0)
    widened = extended(edge_rows, (("blk", 0),), 1)
    return stack_table(face_rows, jnp.stack([widened[0], widened[3]], axis=0))


def general_local(rhs, leaf_neighbors, parent_neighbors, children, owners, parent_places):
    factor = relax_weight / 6.0
    blk_count = lax.axis_size("blk")
    sub_count = lax.axis_size("sub")
    blk_here = lax.axis_index("blk")
    sub_here = lax.axis_index("sub")
    blocks = rhs.shape[0]
    range_len = blocks * sub_count
    parent_len = range_len // 8
    range_start = blk_here * range_len
    parent_start = blk_here * parent_len
    leaf_rows = leaf_index(leaf_neighbors, blk_here, sub_here, sub_count)
    sweep_one = factor * rhs
    second = jacobi_sweep(sweep_one, rhs, lookup(leaf_table(sweep_one), leaf_rows))
    residual = rhs - apply_operator(second, lookup(leaf_table(second), leaf_rows))
    octant_rows = lax.all_gather(restrict_octants(residual), "sub", axis=0, tiled=True)
    range_children = lax.dynamic_slice_in_dim(children, parent_start, parent_len, 0) - range_start
    ranks_all = slot_ranks(owners.reshape(blk_count, parent_len)).reshape(-1)
    range_owners = lax.dynamic_slice_in_dim(owners, parent_start, parent_len, 0)
    range_ranks = lax.dynamic_slice_in_dim(ranks_all, parent_start, parent_len, 0)
    slot_match = (range_owners[None, :] == sub_here) & (
        range_ranks[None, :] == jnp.arange(PMOST, dtype=jnp.int32)[:, None]
    )
    filled = jnp.any(slot_match, axis=1)
    slot_local = jnp.sum(
        jnp.where(slot_match, jnp.arange(parent_len, dtype=jnp.int32)[None, :], 0), axis=1
    )
    filled_gain = filled.astype(jnp.float32)[:, None, None]
    own_local = sub_here * blocks + jnp.arange(blocks, dtype=jnp.int32)
    matches = range_children.reshape(-1)[None, :] == own_local[:, None]
    flat_place = jnp.sum(
        jnp.where(matches, jnp.arange(parent_len * 8, dtype=jnp.int32)[None, :], 0), axis=1
    )
    leaf_parent = flat_place // 8
    leaf_octant = flat_place % 8
    source = assemble(octant_rows[range_children])
    parent_rows = table_index(
        lax.dynamic_slice_in_dim(parent_neighbors, parent_start, parent_len, 0),
        parent_start,
        parent_len,
    )
    global_places = lax.dynamic_slice_in_dim(parent_places, parent_start, parent_len, 0)
    keep_gain = jnp.ones((parent_len, 1, 1), jnp.float32)
    parent_one = factor * source
    parent_two = jacobi_sweep(parent_one, source, lookup(range_table(parent_one), parent_rows))
    parent_rest = source - apply_operator(parent_two, lookup(range_table(parent_two), parent_rows))
    coarse = coarsen(parent_rest)
    root_slab = (
        jnp.zeros((parent_len, 64), jnp.float32).at[global_places - parent_start].set(coarse)
    )
    ordered = lax.all_gather(root_slab, "blk", axis=0, tiled=True)
    side_y = blocks // 4
    side_x = sub_count // 2
    root_source = (
        ordered.reshape(blk_count, side_y, side_x, 4, 4, 4)
        .transpose(0, 3, 1, 4, 2, 5)
        .reshape(4 * blk_count, 16 * side_y * side_x)
    )
    root_source = root_source - jnp.mean(root_source)
    root_values = jnp.zeros_like(root_source)
    for repeat in range(ROOT_SWEEPS):
        root_values = root_relax(root_values, root_source, 4 * side_x)
    root_back = (
        root_values.reshape(blk_count, 4, side_y, 4, side_x, 4)
        .transpose(0, 2, 4, 1, 3, 5)
        .reshape(blk_count * parent_len, 64)[global_places]
    )
    parent_three = parent_two + widen_root(root_back) * keep_gain
    parent_four = jacobi_sweep(parent_three, source, lookup(range_table(parent_three), parent_rows))
    parent_solution = parent_four[slot_local] * filled_gain
    own_parents = parent_four[leaf_parent]
    pieces = octant_split(own_parents)
    chosen = jnp.take_along_axis(pieces, leaf_octant[:, None, None], axis=1)[:, 0]
    leaf_three = second + widen_leaf(chosen)
    leaf_solution = jacobi_sweep(leaf_three, rhs, lookup(leaf_table(leaf_three), leaf_rows))
    return (leaf_solution, parent_solution)


FACTOR = relax_weight / 6.0
SELF = 1.0 - 6.0 * FACTOR
LANES = 128
OWN_ROWS = 64
MSG_ROWS = 32
VMEM_LIMIT = 16 * 1024 * 1024


def lane_iota(shape):
    return lax.broadcasted_iota(jnp.int32, shape, len(shape) - 1)


def row_iota(shape):
    return lax.broadcasted_iota(jnp.int32, shape, len(shape) - 2)


def turn(values, shift, axis):
    size = values.shape[axis]
    shift = shift % size
    if shift == 0:
        return values
    return pltpu.roll(values, shift, axis)


def split_dot(left, table):
    high = left.astype(jnp.bfloat16)
    low = (left - high.astype(jnp.float32)).astype(jnp.bfloat16)
    return jnp.dot(high, table, preferred_element_type=jnp.float32) + jnp.dot(
        low, table, preferred_element_type=jnp.float32
    )


def zero_one(condition, scale=1.0):
    return np.where(condition, scale, 0.0).astype(jnp.bfloat16)


def key_col(rows, columns):
    return np.arange(rows)[:, None], np.arange(columns)[None, :]


def face_table():
    key, col = key_col(256, LANES)
    return zero_one(
        (key // 16 == col % 64)
        & (((col < 64) & (key % 16 == 0)) | ((col >= 64) & (key % 16 == 15)))
    )


def root_spread_table(sub_count):
    key, col = key_col(16 * sub_count, 256)
    return zero_one(key == (col // 32) * (2 * sub_count) + col % 8 // 4)


def parent_table():
    key, col = key_col(256, 256)
    return zero_one(key == (col % 16 // 8) * LANES + (col // 16) * 8 + col % 8)


def leaf_table_of_cells():
    key, col = key_col(256, 256)
    y = col // 16
    x = col % 16
    return zero_one(key == (y % 2 * 2 + x % 2) * 64 + y // 2 * 8 + x // 2)


def push_table():
    key, col = key_col(LANES, 256)
    group = key // 16
    cell = np.select([group == 0, group == 1, group == 4, group == 5], [0, 15, 1, 14], 16)
    return zero_one((key % 16 == col // 16) & (col % 16 == cell))


def beside_x(chunk, width):
    cell = lane_iota(chunk.shape) % width
    low = jnp.where(cell > 0, turn(chunk, 1, 1), 0.0)
    high = jnp.where(cell < width - 1, turn(chunk, -1, 1), 0.0)
    return low + high


def y_pair(chunks, width):
    lane = lane_iota(chunks[0].shape)
    up = [turn(chunk, width, 1) for chunk in chunks]
    down = [turn(chunk, -width, 1) for chunk in chunks]
    zero = jnp.zeros_like(chunks[0])
    lower = []
    upper = []
    for k in range(len(chunks)):
        before = up[k - 1] if k > 0 else zero
        after = down[k + 1] if k + 1 < len(chunks) else zero
        lower.append(jnp.where(lane < width, before, up[k]))
        upper.append(jnp.where(lane >= LANES - width, after, down[k]))
    return lower, upper


def z_pair(chunk):
    rows = chunk.shape[0]
    row = row_iota(chunk.shape)
    lower = jnp.where(row > 0, turn(chunk, 1, 0), 0.0)
    upper = jnp.where(row < rows - 1, turn(chunk, -1, 0), 0.0)
    return lower, upper


def fine_beside(chunks):
    lower, upper = y_pair(chunks, 16)
    in_x = [beside_x(chunk, 16) for chunk in chunks]
    in_y = [a + b for a, b in zip(lower, upper)]
    in_z = []
    for chunk in chunks:
        below, above = z_pair(chunk)
        in_z.append(below + above)
    return in_x, in_y, in_z


def coarse_turns(columns):
    return (
        [[turn(chunk, 8, 1) for chunk in halves] for halves in columns],
        [[turn(chunk, -8, 1) for chunk in halves] for halves in columns],
    )


def coarse_y_pair(up, down):
    lane = lane_iota(up[0].shape)
    zero = jnp.zeros_like(up[0])
    lower = []
    upper = []
    for half in range(2):
        lower.append(jnp.where(lane < 8, up[half - 1] if half > 0 else zero, up[half]))
        upper.append(jnp.where(lane >= LANES - 8, down[half + 1] if half < 1 else zero, down[half]))
    return lower, upper


def coarse_x_pair(columns, up, down, index, half):
    chunk = columns[index][half]
    cell = lane_iota(chunk.shape) % 8
    before = down[index - 1][half] if index > 0 else jnp.zeros_like(chunk)
    after = up[index + 1][half] if index + 1 < len(columns) else jnp.zeros_like(chunk)
    low = turn(jnp.where(cell == 7, before, chunk), 1, 1)
    high = turn(jnp.where(cell == 0, after, chunk), -1, 1)
    return low, high


def coarse_sums(columns):
    up, down = coarse_turns(columns)

    def sums(index):
        lower, upper = coarse_y_pair(up[index], down[index])
        halves = []
        for half in range(2):
            chunk = columns[index][half]
            low, high = coarse_x_pair(columns, up, down, index, half)
            total = low + high + lower[half] + upper[half]
            halves.append(total + turn(chunk, 1, 0) + turn(chunk, -1, 0))
        return halves

    return sums


def power_div(values, divisor):
    return lax.shift_right_logical(values, jnp.full_like(values, divisor.bit_length() - 1))


def power_rem(values, divisor):
    return values & (divisor - 1)


def octant_table():
    key = row_iota((256, LANES))
    col = lane_iota((256, LANES))
    key_x = power_rem(key, 16)
    col_x = power_rem(col, 8)
    side_x = jnp.where(col_x == 7, 0, jnp.where(col_x == 0, 15, 16))
    right_x = jnp.where(col < 64, power_div(key_x, 2) - col_x, key_x - side_x)
    right_y = power_div(key, 32) - power_div(power_rem(col, 64), 8)
    return jnp.where((right_x | right_y) == 0, 0.5, 0.0).astype(jnp.bfloat16)


def root_table(sub_count):
    shape = (4 * LANES, 16 * sub_count)
    key = row_iota(shape)
    near_x = power_div(power_rem(key, 8), 4)
    row = power_div(power_rem(key, 256), 32)
    along = jnp.where(key < 256, near_x + 1, 3 - 3 * near_x)
    target = row * (2 * sub_count) + along
    return jnp.where(lane_iota(shape) == target, 0.25, 0.0).astype(jnp.bfloat16)


def as_column(row):
    count = row.shape[1]
    shape = (count, count)
    return jnp.sum(
        jnp.where(row_iota(shape) == lane_iota(shape), row, 0.0), axis=1, keepdims=True
    )


def grid_codes(sub_count, wide_y, child_ref, place_ref):
    side_y = wide_y // 2
    side_x = sub_count // 2
    shape = child_ref.shape
    octant = row_iota(shape)
    place = jnp.broadcast_to(place_ref[...], shape)
    cell_z = 2 * power_div(place, side_y * side_x) + power_div(octant, 4)
    cell_y = 2 * power_rem(power_div(place, side_x), side_y) + power_rem(power_div(octant, 2), 2)
    cell_x = 2 * power_rem(place, side_x) + power_rem(octant, 2)
    return (cell_z * wide_y + cell_y) * sub_count + cell_x


def own_codes(sub_count, blocks, child_ref, codes, sub_here, blk_here):
    first = (blk_here * sub_count + sub_here) * blocks
    codes = codes.astype(jnp.float32)
    return [
        jnp.sum(jnp.where(child_ref[...] == first + slot, codes, 0.0)).astype(jnp.int32)
        for slot in range(blocks)
    ]


def own_position(sub_count, wide_y, code):
    return lax.rem(lax.div(code, wide_y * sub_count), 2) * wide_y + lax.rem(
        lax.div(code, sub_count), wide_y
    )


def lists_agree(sub_count, blk_count, leaf_ref, parent_ref, child_ref, place_ref, codes, own):
    blocks = len(own)
    wide_y = blocks // 2
    side_y = wide_y // 2
    side_x = sub_count // 2
    parents = child_ref.shape[1]
    layer = wide_y * sub_count
    children = child_ref[...]
    device = power_div(codes, 2 * layer) * sub_count + power_rem(codes, sub_count)
    missed = jnp.where(power_div(children, blocks) != device, 1.0, 0.0)
    faults = jnp.int32(0)
    for slot in range(blocks):
        for axis, (stride, length) in enumerate(
            ((1, sub_count), (sub_count, wide_y), (layer, 2 * blk_count))
        ):
            along = lax.rem(lax.div(own[slot], stride), length)
            for sign in (-1, 1):
                listed = leaf_ref[slot, 2 * axis + (sign + 1) // 2]
                exists = (along + sign >= 0) & (along + sign < length)
                hit = (children == listed) & (codes == own[slot] + sign * stride)
                missed = missed - jnp.where(hit, 1.0, 0.0)
                faults = faults + jnp.where(
                    exists, jnp.where(listed >= 0, 1, -100000), jnp.where(listed < 0, 0, -100000)
                )
    wrong = jnp.abs(jnp.sum(missed) + faults.astype(jnp.float32))
    place_row = place_ref[...].astype(jnp.float32)
    place_column = as_column(place_row)
    number = row_iota((parents, parents))
    place = place_ref[...]
    missed = jnp.zeros((1, parents), jnp.float32)
    for axis, (stride, length) in enumerate(((1, side_x), (side_x, side_y), (side_y * side_x, blk_count))):
        along = power_rem(power_div(place, stride), length)
        for sign in (-1, 1):
            face = 2 * axis + (sign + 1) // 2
            listed = parent_ref[face : face + 1, :]
            found = jnp.sum(jnp.where(number == listed, place_column, 0.0), axis=0, keepdims=True)
            exists = (along + sign >= 0) & (along + sign < length)
            wanted = (place + sign * stride).astype(jnp.float32)
            missed = missed + jnp.where(
                exists,
                jnp.where((listed >= 0) & (found == wanted), 0.0, 1.0),
                jnp.where(listed < 0, 0.0, 1.0),
            )
    wrong = wrong + jnp.sum(missed)
    return jnp.where(wrong == 0.0, 1.0, 0.0)


def limits(sub_count, blk_count):
    sub_here = lax.axis_index("sub")
    blk_here = lax.axis_index("blk")

    def gain(condition):
        return jnp.where(condition, 1.0, 0.0).astype(jnp.float32)

    return (
        sub_here,
        blk_here,
        gain(sub_here > 0),
        gain(sub_here < sub_count - 1),
        gain(blk_here > 0),
        gain(blk_here < blk_count - 1),
    )


def placed_chunks(placed, wide_y):
    chunks = []
    for k in range(2 * wide_y):
        lanes = slice(LANES * (k % 2), LANES * (k % 2) + LANES)
        chunks.append(
            jnp.concatenate([placed[k // 2, :, lanes], placed[wide_y + k // 2, :, lanes]], axis=0)
        )
    return chunks


def return_gain(shape, x_low, x_high, z_low, z_high):
    cell = lane_iota(shape) % 16
    row = row_iota(shape)
    return (
        jnp.where(cell == 0, x_low, 0.0)
        + jnp.where(cell == 15, x_high, 0.0)
        + jnp.where(row == 0, z_low, 0.0)
        + jnp.where(row == shape[0] - 1, z_high, 0.0)
    ) * (FACTOR * FACTOR)


def push_kernel(
    sub_count, blk_count, blk_bits,
    leaf_hbm, parent_hbm, child_hbm, place_hbm, owner_hbm, rhs_hbm,
    placed, own_ref, leaf_out, parent_ref, child_ref, place_ref, owner_out, *rest
):
    msg_refs = rest[:blk_bits]
    leaf_ref, rhs_ref, rows_s, rows_g, left_a, coarse_s, sems = rest[blk_bits:]
    copies = [
        pltpu.make_async_copy(source, target, sems.at[k])
        for k, (source, target) in enumerate(
            (
                (child_hbm, child_ref),
                (place_hbm, place_ref),
                (rhs_hbm, rhs_ref),
                (leaf_hbm, leaf_ref),
                (parent_hbm, parent_ref),
                (leaf_hbm, leaf_out),
                (owner_hbm, owner_out),
            )
        )
    ]
    for copy in copies:
        copy.start()
    table_a = octant_table()
    table_r = root_table(sub_count)
    blocks = rhs_ref.shape[0]
    wide_y = blocks // 2
    f = FACTOR
    f2 = f * f
    sub_here, blk_here, x_low, x_high, z_low, z_high = limits(sub_count, blk_count)
    copies[0].wait()
    copies[1].wait()
    codes = grid_codes(sub_count, wide_y, child_ref, place_ref)
    own_code = own_codes(sub_count, blocks, child_ref, codes, sub_here, blk_here)
    copies[2].wait()
    for slot in range(blocks):
        placed[own_position(sub_count, wide_y, own_code[slot])] = rhs_ref[slot]
    s = placed_chunks(placed, wide_y)
    shape = s[0].shape
    top = shape[0] - 1
    back = return_gain(shape, x_low, x_high, z_low, z_high)
    sx, sy, sz = fine_beside(s)
    w = [SELF * a + f * (x + y + z) for a, x, y, z in zip(s, sx, sy, sz)]
    wx, wy, wz = fine_beside(w)
    for k in range(2 * wide_y):
        half = slice(LANES * (k % 2), LANES * (k % 2) + LANES)
        rows_s[k] = SELF * w[k] + f * (wx[k] + wy[k] + wz[k]) + back * s[k]
        base = (SELF * f + f2) * s[k] + f * w[k]
        rows_g[k] = base + f2 * (sy[k] + sz[k])
        gz = base + f2 * (sx[k] + sy[k])
        line = 48 * (k // 2)
        left_a[line + 16 : line + 17, half] = gz[0:1]
        left_a[line + 17 : line + 18, half] = gz[top : top + 1]
        left_a[line + 40 : line + 41, half] = (2.0 * f2) * s[k][0:1]
        left_a[line + 41 : line + 42, half] = (2.0 * f2) * s[k][top : top + 1]
        edge = gz + (f - f2) * s[k]
        for bit in range(blk_bits):
            upward = (blk_here // (1 << bit)) % 2 == 0
            msg_refs[bit][16 + k // 2 : 17 + k // 2, half] = jnp.where(
                upward, edge[top : top + 1], edge[0:1]
            )
            msg_refs[bit][16 + wide_y + k // 2 : 17 + wide_y + k // 2, half] = jnp.where(
                upward, s[k][top : top + 1], s[k][0:1]
            )
    for k in range(2 * wide_y):
        half = slice(LANES * (k % 2), LANES * (k % 2) + LANES)
        line = 48 * (k // 2)
        left_a[line : line + 16, half] = (
            rows_s[k, pl.ds(0, 16, stride=2), :] + rows_s[k, pl.ds(1, 16, stride=2), :]
        )
        left_a[line + 24 : line + 40, half] = (
            rows_g[k, pl.ds(0, 16, stride=2), :] + rows_g[k, pl.ds(1, 16, stride=2), :]
        )
    for copy in copies[3:]:
        copy.wait()
    out_a = split_dot(left_a[...], table_a)
    good = lists_agree(
        sub_count, blk_count, leaf_ref, parent_ref, child_ref, place_ref, codes, own_code
    )
    lane24 = lane_iota((24, LANES))
    main = []
    side = []
    for half in range(2):
        first = out_a[96 * half : 96 * half + 24]
        second = out_a[96 * half + 48 : 96 * half + 72]
        main.append(jnp.where(lane24 < 64, first, turn(second, 64, 1)))
        first = out_a[96 * half + 24 : 96 * half + 48]
        second = out_a[96 * half + 72 : 96 * half + 96]
        side.append(jnp.where(lane24 < 64, turn(first, 64, 1), second))
    zero3 = jnp.zeros((3, LANES), jnp.float32)
    for half in range(2):
        lanes = slice(LANES * half, LANES * half + LANES)
        for base_row, piece in ((0, main[half]), (24, side[half])):
            own_ref[base_row : base_row + 3, lanes] = zero3
            own_ref[base_row + 3 : base_row + 4, lanes] = piece[16:17] * z_low
            own_ref[base_row + 4 : base_row + 20, lanes] = piece[0:16]
            own_ref[base_row + 20 : base_row + 21, lanes] = piece[17:18] * z_high
            own_ref[base_row + 21 : base_row + 24, lanes] = zero3
    cell8 = lane24 % 8
    row24 = row_iota((24, LANES))
    inside_z = jnp.where(row24 < 4, z_low, jnp.where(row24 >= 20, z_high, 1.0))
    gain = [inside_z * x_low, inside_z, inside_z * x_high]
    main24 = [own_ref[0:24, 0:LANES], own_ref[0:24, LANES:256]]
    side24 = [own_ref[24:48, 0:LANES], own_ref[24:48, LANES:256]]
    columns = [
        [jnp.where(cell8 == 7, piece, 0.0) * x_low for piece in side24],
        main24,
        [jnp.where(cell8 == 0, piece, 0.0) * x_high for piece in side24],
    ]
    sums = coarse_sums(columns)
    wp = []
    for b in range(3):
        near = sums(b)
        wp.append([gain[b] * (SELF * columns[b][h] + f * near[h]) for h in range(2)])
    sums = coarse_sums(wp)
    zero8 = jnp.zeros((8, LANES), jnp.float32)
    for b in range(3):
        near = sums(b)
        for h in range(2):
            coarse_s[2 * b + h, 0:24] = gain[b] * (SELF * wp[b][h] + f * near[h])
            coarse_s[2 * b + h, 24:32] = zero8
    pieces = []
    low_cells = lane_iota((8, LANES)) % 8 < 4
    for k in range(6):
        pieces.append(
            coarse_s[k, pl.ds(0, 8, stride=4), :]
            + coarse_s[k, pl.ds(1, 8, stride=4), :]
            + coarse_s[k, pl.ds(2, 8, stride=4), :]
            + coarse_s[k, pl.ds(3, 8, stride=4), :]
        )
    outer = [jnp.where(low_cells, pieces[4 + h], pieces[h]) for h in range(2)]
    root_left = jnp.concatenate([pieces[2], pieces[3]] + outer, axis=1)
    root_lanes = 16 * sub_count
    root_part = split_dot(root_left, table_r)
    root_part = pltpu.roll(root_part, 2 * sub_here + root_lanes - 1, 1)
    root_part = jnp.where(row_iota(root_part.shape) < 6, root_part, 0.0)
    own_ref[48:56, 0:root_lanes] = root_part
    if root_lanes < 256:
        own_ref[48:56, root_lanes:256] = jnp.zeros((8, 256 - root_lanes), jnp.float32)
    flag = jnp.zeros((8, LANES), jnp.float32) + good
    for lanes in (slice(0, LANES), slice(LANES, 256)):
        own_ref[56:64, lanes] = flag
    for bit in range(blk_bits):
        upward = (blk_here // (1 << bit)) % 2 == 0
        ref = msg_refs[bit]
        ref[8:16, :] = own_ref[48:56, :]
        ref[24:32, 0:LANES] = zero8
        ref[24:32, LANES:256] = flag
        for base_row, source in ((0, 0), (4, 24)):
            ref[base_row : base_row + 4, :] = jnp.where(
                upward, own_ref[source + 17 : source + 21, :], own_ref[source + 3 : source + 7, :]
            )


def side_kernel(
    sub_count, blk_count, slots,
    child_ref, owner_ref, place_ref, placed, table_ref,
    position_ref, slot_ref, part_ref, faces_ref,
    left_c
):
    blocks = placed.shape[0]
    wide_y = blocks // 2
    f = FACTOR
    f2 = f * f
    sub_here, blk_here, x_low, x_high, z_low, z_high = limits(sub_count, blk_count)
    codes = grid_codes(sub_count, wide_y, child_ref, place_ref)
    own_code = own_codes(sub_count, blocks, child_ref, codes, sub_here, blk_here)
    for slot in range(blocks):
        position_ref[slot] = own_position(sub_count, wide_y, own_code[slot])
    s = placed_chunks(placed, wide_y)
    back = return_gain(s[0].shape, x_low, x_high, z_low, z_high)
    sx, sy, sz = fine_beside(s)
    w = [SELF * a + f * (x + y + z) for a, x, y, z in zip(s, sx, sy, sz)]
    wx, wy, wz = fine_beside(w)
    for k in range(2 * wide_y):
        half = slice(LANES * (k % 2), LANES * (k % 2) + LANES)
        r = SELF * w[k] + f * (wx[k] + wy[k] + wz[k]) + back * s[k]
        part = f * (s[k] + w[k] + r)
        part_ref[k // 2, :, half] = part[:16]
        part_ref[wide_y + k // 2, :, half] = part[16:]
        line = 64 * (k // 2)
        left_c[line : line + 32, half] = (
            (SELF * f + f) * s[k] + f * w[k] + f2 * (sy[k] + sz[k])
        )
        left_c[line + 32 : line + 64, half] = s[k]
    out_c = split_dot(left_c[...], table_ref[...])
    faces = out_c[0:64]
    for yy in range(1, wide_y):
        faces = faces + turn(out_c[64 * yy : 64 * yy + 64], 16 * yy, 1)
    faces_ref[...] = faces
    owned = owned_slots(sub_count, blk_count, slots, sub_here, blk_here, owner_ref, place_ref)
    for k in range(slots):
        for j in range(3):
            slot_ref[3 * k + j] = owned[k][j]


def neighbour_pick(blk_here, blk_count, msg_refs):
    spans = []
    step = 1
    while step < blk_count:
        spans.append(step)
        step = 2 * step + 1

    def picker(other):
        choices = [(blk_here ^ other) == d for d in spans]

        def read(rows, lanes):
            value = msg_refs[spans[-1] - 1][rows, lanes]
            for choice, d in zip(choices[:-1], spans[:-1]):
                value = jnp.where(choice, msg_refs[d - 1][rows, lanes], value)
            return value

        return read

    return picker(blk_here - 1), picker(blk_here + 1)


def root_tiles(sub_count, blk_count):
    return (sub_count * blk_count // 16 + 1) // 2


def join_kernel(sub_count, blk_count, own_ref, faces_ref, *rest):
    msg_refs = rest[: blk_count - 1]
    out_ref, lines_ref, root_s = rest[blk_count - 1 :]
    _, blk_here, _, _, z_low, z_high = limits(sub_count, blk_count)
    below, above = neighbour_pick(blk_here, blk_count, msg_refs)
    row8 = row_iota((8, LANES))
    low_rows = (row8 >= 1) & (row8 < 5)
    high_rows = (row8 >= 3) & (row8 < 7)
    good = own_ref[56:64, 0:LANES]
    for ref in msg_refs:
        good = jnp.minimum(good, ref[24:32, LANES:256])
    for half in range(2):
        lanes = slice(LANES * half, LANES * half + LANES)
        low = below(slice(0, 8), lanes) * z_low
        high = above(slice(0, 8), lanes) * z_high
        for base, low_turn, high_turn in ((0, 1, 3), (24, 5, 7)):
            out_ref[base : base + 8, lanes] = own_ref[base : base + 8, lanes] + jnp.where(
                low_rows, turn(low, low_turn, 0), 0.0
            )
            out_ref[base + 8 : base + 16, lanes] = own_ref[base + 8 : base + 16, lanes]
            out_ref[base + 16 : base + 24, lanes] = own_ref[
                base + 16 : base + 24, lanes
            ] + jnp.where(high_rows, turn(high, high_turn, 0), 0.0)
        out_ref[23:24, lanes] = good[0:1]
    root_s[...] = jnp.zeros(root_s.shape, jnp.float32)
    for d in range(blk_count):
        start = 4 * (blk_here ^ d) + 3
        for part in range(root_s.shape[0]):
            lanes = slice(LANES * part, LANES * part + LANES)
            value = own_ref[48:56, lanes] if d == 0 else msg_refs[d - 1][8:16, lanes]
            root_s[part, pl.ds(start, 8), :] = root_s[part, pl.ds(start, 8), :] + value
    tile = 0
    for start in range(0, 4 * blk_count, 8):
        for part in range(root_s.shape[0]):
            row = 48 + 8 * (tile // 2)
            lanes = slice(LANES * (tile % 2), LANES * (tile % 2) + LANES)
            out_ref[row : row + 8, lanes] = root_s[part, 4 + start : 12 + start]
            tile += 1
    row = 48 + 8 * root_tiles(sub_count, blk_count)
    count = lines_ref.shape[0] // 2
    half = count // 2
    low = below(slice(16, 16 + count), slice(0, 256)) * z_low
    high = above(slice(16, 16 + count), slice(0, 256)) * z_high
    lines_ref[0:count] = low
    lines_ref[count : 2 * count] = high
    out_ref[row : row + half, :] = low[half:count]
    out_ref[row + half : row + count, :] = high[half:count]
    out_ref[row + 8 : row + 40, 0:LANES] = faces_ref[0:32]
    out_ref[row + 8 : row + 40, LANES:256] = faces_ref[32:64]


def owned_slots(sub_count, blk_count, slots, sub_here, blk_here, owner_ref, place_ref):
    parents = owner_ref.shape[1]
    parent_len = parents // blk_count
    side_x = sub_count // 2
    side_y = parent_len // side_x
    number = lane_iota((1, parents))
    here = (owner_ref[...] == sub_here) & (lax.div(number, parent_len) == blk_here)
    mine = jnp.where(here, 1.0, 0.0)
    shape = (parents, parents)
    rank = jnp.sum(
        jnp.where(row_iota(shape) < lane_iota(shape), as_column(mine), 0.0), axis=0, keepdims=True
    )
    places = place_ref[...].astype(jnp.float32)
    found = []
    for k in range(slots):
        chosen = jnp.where(rank == float(k), mine, 0.0)
        place = jnp.sum(chosen * places).astype(jnp.int32)
        found.append(
            (
                lax.rem(lax.div(place, side_x), side_y),
                lax.rem(place, side_x),
                jnp.sum(chosen).astype(jnp.int32),
            )
        )
    return found


def solve_kernel(
    sub_count, blk_count, slots,
    positions, owned, all_ref, part_ref, lines_ref, table_w_ref, table_p_ref, table_l_ref, table_x_ref,
    leaf_ref, parent_ref, good_ref,
    placed, par_s, root_s, fine_s, push_s
):
    blocks = part_ref.shape[0]
    wide_y = blocks // 2
    f = FACTOR
    f2 = f * f
    sub_here, blk_here, x_low, x_high, z_low, z_high = limits(sub_count, blk_count)
    row8 = row_iota((8, LANES))
    cell24 = lane_iota((24, LANES)) % 8
    row24 = row_iota((24, LANES))
    good = all_ref[0, 16:24, 0:LANES]
    for c in range(1, sub_count):
        good = jnp.minimum(good, all_ref[c, 16:24, 0:LANES])
    good_ref[0] = jnp.min(jnp.where(row8 == 7, good, 1.0)).astype(jnp.int32)
    source = []
    for c in range(sub_count):
        halves = []
        for half in range(2):
            lanes = slice(LANES * half, LANES * half + LANES)
            value = all_ref[c, 0:24, lanes]
            if c + 1 < sub_count:
                value = value + jnp.where(cell24 == 7, all_ref[c + 1, 24:48, lanes], 0.0)
            if c > 0:
                value = value + jnp.where(cell24 == 0, all_ref[c - 1, 24:48, lanes], 0.0)
            halves.append(value)
        source.append(halves)

    root_lanes = 16 * sub_count
    row_len = 2 * sub_count
    root_rows = 4 * blk_count
    parts = root_lanes // LANES
    tile_rows = []
    tile = 0
    for _ in range(0, root_rows, 8):
        pieces = []
        for part in range(parts):
            row = 48 + 8 * (tile // 2)
            lanes = slice(LANES * (tile % 2), LANES * (tile % 2) + LANES)
            total = all_ref[0, row : row + 8, lanes]
            for c in range(1, sub_count):
                total = total + all_ref[c, row : row + 8, lanes]
            pieces.append(total)
            tile += 1
        tile_rows.append(jnp.concatenate(pieces, axis=1))
    root_source = jnp.concatenate(tile_rows, axis=0)
    root_source = root_source - jnp.sum(root_source) / (root_rows * root_lanes)
    shape = root_source.shape
    lane = lane_iota(shape)
    row = row_iota(shape)

    def root_sweep(values):
        total = jnp.where(lane % row_len > 0, turn(values, 1, 1), 0.0)
        total = total + jnp.where(lane % row_len < row_len - 1, turn(values, -1, 1), 0.0)
        total = total + jnp.where(lane >= row_len, turn(values, row_len, 1), 0.0)
        total = total + jnp.where(lane < root_lanes - row_len, turn(values, -row_len, 1), 0.0)
        total = total + jnp.where(row > 0, turn(values, 1, 0), 0.0)
        total = total + jnp.where(row < root_rows - 1, turn(values, -1, 0), 0.0)
        return SELF * values + f * (root_source + total)

    values = f * root_source
    left_sweeps = ROOT_SWEEPS - 1
    sums = coarse_sums(source)
    two = []
    for c in range(sub_count):
        if left_sweeps > 0:
            values = root_sweep(values)
            left_sweeps -= 1
        near = sums(c)
        two.append(
            [(f + f * SELF) * source[c][half] + f2 * near[half] for half in range(2)]
        )
    for _ in range(left_sweeps):
        values = root_sweep(values)
    root_s[...] = jnp.zeros(root_s.shape, jnp.float32)
    for part in range(parts):
        root_s[part, 4 : 4 + root_rows] = values[:, LANES * part : LANES * part + LANES]
    mine = jnp.concatenate(
        [root_s[part, pl.ds(4 * blk_here + 3, 8), :] for part in range(parts)], axis=1
    )
    left = jnp.concatenate([turn(mine, -2 * c, 1) for c in range(sub_count)], axis=0)
    wide = split_dot(left, table_w_ref[...])

    valid = (
        (row24 >= 2)
        & (row24 < 22)
        & ((row24 >= 4) | (z_low > 0.0))
        & ((row24 < 20) | (z_high > 0.0))
    )
    three = []
    for c in range(sub_count):
        halves = []
        for half in range(2):
            lanes = slice(LANES * half, LANES * half + LANES)
            tiles = []
            for t in range(3):
                first = wide[8 * c + 2 * t : 8 * c + 2 * t + 1, lanes]
                second = wide[8 * c + 2 * t + 1 : 8 * c + 2 * t + 2, lanes]
                tiles.append(
                    jnp.where(
                        row8 < 4,
                        jnp.broadcast_to(first, (8, LANES)),
                        jnp.broadcast_to(second, (8, LANES)),
                    )
                )
            value = two[c][half] + jnp.concatenate(tiles, axis=0)
            halves.append(jnp.where(valid, value, 0.0))
        three.append(halves)
    sums = coarse_sums(three)
    for c in range(sub_count):
        near = sums(c)
        for half in range(2):
            value = SELF * three[c][half] + f * (near[half] + source[c][half])
            par_s[c, half] = jnp.where(valid, value, 0.0)

    pieces = []
    for k in range(slots):
        half = owned[3 * k]
        place_x = owned[3 * k + 1]
        filled = owned[3 * k + 2].astype(jnp.float32)
        pieces.append(
            jnp.concatenate(
                [par_s[2 * place_x, half, 4:20], par_s[2 * place_x + 1, half, 4:20]], axis=1
            )
            * filled
        )
    left = jnp.concatenate(pieces, axis=0)
    moved = split_dot(left, table_p_ref[...])
    for k in range(slots):
        parent_ref[k] = moved[16 * k : 16 * k + 16]

    before = jnp.maximum(sub_here - 1, 0)
    after = jnp.minimum(sub_here + 1, sub_count - 1)
    columns = [
        [par_s[before, half] * x_low for half in range(2)],
        [par_s[sub_here, half] for half in range(2)],
        [par_s[after, half] * x_high for half in range(2)],
    ]
    centre = columns[1]
    up, down = coarse_turns(columns)
    in_y = coarse_y_pair(up[1], down[1])
    lane16 = lane_iota((16, LANES))
    left_rows = []
    in_x = [coarse_x_pair(columns, up, down, 1, half) for half in range(2)]
    blend = {}
    for half in range(2):
        for zp in range(2):
            base = (SELF + 3.0 * f) * centre[half] + f * turn(centre[half], 1 - 2 * zp, 0)
            for yp in range(2):
                for xp in range(2):
                    value = base + f * (in_y[yp][half] + in_x[half][xp])
                    blend[half, zp, 2 * yp + xp] = value[4:20]
    for yy in range(wide_y):
        half = yy // 2
        for zp in range(2):
            pair = []
            for v in (0, 2):
                first = blend[half, zp, v]
                second = blend[half, zp, v + 1]
                if yy % 2 == 0:
                    second = turn(second, 64, 1)
                else:
                    first = turn(first, 64, 1)
                pair.append(jnp.where(lane16 < 64, first, second))
            left_rows.append(jnp.concatenate(pair, axis=1))
    left = jnp.concatenate(left_rows, axis=0)
    spread = split_dot(left, table_l_ref[...])
    for yy in range(wide_y):
        for zp in range(2):
            top = 16 * (2 * yy + zp)
            fine_s[2 * yy, pl.ds(zp, 16, stride=2), :] = spread[top : top + 16, 0:128]
            fine_s[2 * yy + 1, pl.ds(zp, 16, stride=2), :] = spread[top : top + 16, 128:256]

    line = 48 + 8 * root_tiles(sub_count, blk_count)
    lane64 = lane_iota((32, LANES))
    from_low = all_ref[before, line + 8 : line + 40, 0:LANES] * x_low
    low_values = all_ref[before, line + 8 : line + 40, LANES:256] * x_low
    from_high = all_ref[after, line + 8 : line + 40, 0:LANES] * x_high
    high_values = all_ref[after, line + 8 : line + 40, LANES:256] * x_high
    left = jnp.concatenate(
        [
            jnp.where(lane64 < 64, turn(from_low, 64, 1), f2 * low_values),
            jnp.where(lane64 < 64, from_high, f2 * turn(high_values, 64, 1)),
        ],
        axis=1,
    )
    lane128 = lane_iota((32, LANES))
    rows = []
    for yy in range(wide_y):
        rows.append(
            jnp.where(
                lax.rem(lane128, 64) < 16,
                turn(left[:, 0:LANES], -16 * yy, 1),
                turn(left[:, LANES:256], 16 - 16 * yy, 1),
            )
        )
    push = split_dot(jnp.concatenate(rows, axis=0), table_x_ref[...])
    for yy in range(wide_y):
        push_s[:, 256 * yy : 256 * yy + 256] = push[32 * yy : 32 * yy + 32]
    cell = lane_iota((2 * wide_y, 256)) % 16
    across = jnp.where(
        cell == 0, turn(all_ref[before, line : line + 2 * wide_y, :], -15, 1) * x_low, 0.0
    ) + jnp.where(
        cell == 15, turn(all_ref[after, line : line + 2 * wide_y, :], 15, 1) * x_high, 0.0
    )
    across = (2.0 * f2) * across
    count = 2 * wide_y
    for yy in range(wide_y):
        lanes = slice(256 * yy, 256 * yy + 256)
        push_s[0:1, lanes] = push_s[0:1, lanes] + lines_ref[yy : yy + 1] + across[yy : yy + 1]
        push_s[1:2, lanes] = push_s[1:2, lanes] + f2 * lines_ref[wide_y + yy : wide_y + yy + 1]
        push_s[31:32, lanes] = (
            push_s[31:32, lanes]
            + lines_ref[count + yy : count + yy + 1]
            + across[wide_y + yy : wide_y + yy + 1]
        )
        push_s[30:31, lanes] = (
            push_s[30:31, lanes]
            + f2 * lines_ref[count + wide_y + yy : count + wide_y + yy + 1]
        )
    for zz in range(2):
        for yy in range(wide_y):
            rows = slice(16 * zz, 16 * zz + 16)
            lanes = slice(256 * yy, 256 * yy + 256)
            index = zz * wide_y + yy
            fine = jnp.concatenate([fine_s[2 * yy, rows], fine_s[2 * yy + 1, rows]], axis=1)
            placed[index] = part_ref[index] + fine + f * push_s[rows, lanes]
    for slot in range(blocks):
        leaf_ref[slot] = placed[positions[slot]]


def paired(count, step):
    return [(i, i ^ step) for i in range(count)]


def is_power(number):
    return number > 0 and number & (number - 1) == 0


def local(rhs, leaf_neighbors, parent_neighbors, children, owners, parent_places):
    blk_count = lax.axis_size("blk")
    sub_count = lax.axis_size("sub")
    blocks = rhs.shape[0]
    wide_y = blocks // 2
    lists = (leaf_neighbors, parent_neighbors, children, owners, parent_places)
    fits = 32 * blocks == 2 * LANES and 16 * sub_count in (LANES, 2 * LANES)
    if not (fits and blk_count > 1 and is_power(blk_count)):
        return general_local(rhs, *lists)
    blk_bits = blk_count.bit_length() - 1
    f32 = jnp.float32
    vmem = pl.BlockSpec(memory_space=pltpu.VMEM)
    smem = pl.BlockSpec(memory_space=pltpu.SMEM)
    params = pltpu.CompilerParams(vmem_limit_bytes=VMEM_LIMIT)
    owner_row = owners.reshape(1, -1)
    place_row = parent_places.reshape(1, -1)
    child_rows = children.T
    parent_rows = parent_neighbors.T
    grid_shape = (blocks, 16, 256)
    outs = pl.pallas_call(
        functools.partial(push_kernel, sub_count, blk_count, blk_bits),
        name="push",
        out_shape=[
            jax.ShapeDtypeStruct(grid_shape, f32),
            jax.ShapeDtypeStruct((OWN_ROWS, 256), f32),
        ]
        + [
            jax.ShapeDtypeStruct(array.shape, jnp.int32)
            for array in (leaf_neighbors, parent_rows, child_rows, place_row, owner_row)
        ]
        + [jax.ShapeDtypeStruct((MSG_ROWS, 256), f32)] * blk_bits,
        in_specs=[pl.BlockSpec(memory_space=pltpu.HBM)] * 6,
        out_specs=[vmem] * (7 + blk_bits),
        scratch_shapes=[
            pltpu.SMEM(leaf_neighbors.shape, jnp.int32),
            pltpu.VMEM(grid_shape, f32),
            pltpu.VMEM((2 * wide_y, 32, LANES), f32),
            pltpu.VMEM((2 * wide_y, 32, LANES), f32),
            pltpu.VMEM((48 * wide_y, 256), f32),
            pltpu.VMEM((6, 32, LANES), f32),
            pltpu.SemaphoreType.DMA((7,)),
        ],
        compiler_params=params,
    )(
        *(
            pltpu.with_memory_space_constraint(array, pltpu.HBM)
            for array in (leaf_neighbors, parent_rows, child_rows, place_row, owner_row, rhs)
        )
    )
    placed, own, leaf_neighbors, parent_rows, child_rows, place_row, owner_row = outs[:7]
    messages = outs[7:]
    lists = (
        leaf_neighbors, parent_rows.T, child_rows.T, owner_row.reshape(-1), place_row.reshape(-1),
    )
    received = [
        lax.ppermute(messages[d.bit_length() - 1], "blk", paired(blk_count, d))
        for d in range(1, blk_count)
    ]
    positions, owned, own_part, faces = pl.pallas_call(
        functools.partial(side_kernel, sub_count, blk_count, PMOST),
        name="side",
        out_shape=[
            jax.ShapeDtypeStruct((blocks,), jnp.int32),
            jax.ShapeDtypeStruct((3 * PMOST,), jnp.int32),
            jax.ShapeDtypeStruct(grid_shape, f32),
            jax.ShapeDtypeStruct((64, LANES), f32),
        ],
        in_specs=[vmem] * 5,
        out_specs=[smem] * 2 + [vmem] * 2,
        scratch_shapes=[pltpu.VMEM((64 * wide_y, 256), f32)],
        compiler_params=params,
    )(child_rows, owner_row, place_row, placed, jnp.asarray(face_table()))
    root_parts = 16 * sub_count // LANES
    joined_rows = 48 + 8 * root_tiles(sub_count, blk_count) + 8 + 32
    joined, lines = pl.pallas_call(
        functools.partial(join_kernel, sub_count, blk_count),
        name="join",
        out_shape=[
            jax.ShapeDtypeStruct((joined_rows, 256), f32),
            jax.ShapeDtypeStruct((4 * wide_y, 256), f32),
        ],
        in_specs=[vmem] * (1 + blk_count),
        out_specs=[vmem] * 2,
        scratch_shapes=[pltpu.VMEM((root_parts, 4 * blk_count + 8, LANES), f32)],
        compiler_params=params,
    )(own, faces, *received)
    gathered = lax.all_gather(joined, "sub", axis=0, tiled=False)
    leaf_solution, parent_solution, good = pl.pallas_call(
        functools.partial(solve_kernel, sub_count, blk_count, PMOST),
        name="solve",
        out_shape=[
            jax.ShapeDtypeStruct((blocks, 16, 256), f32),
            jax.ShapeDtypeStruct((PMOST, 16, 256), f32),
            jax.ShapeDtypeStruct((1,), jnp.int32),
        ],
        in_specs=[smem] * 2 + [vmem] * 7,
        out_specs=[vmem] * 2 + [smem],
        scratch_shapes=[
            pltpu.VMEM((blocks, 16, 256), f32),
            pltpu.VMEM((sub_count, 2, 24, LANES), f32),
            pltpu.VMEM((root_parts, 4 * blk_count + 8, LANES), f32),
            pltpu.VMEM((2 * wide_y, 32, LANES), f32),
            pltpu.VMEM((32, 256 * wide_y), f32),
        ],
        compiler_params=params,
    )(
        positions, owned, gathered, own_part, lines,
        jnp.asarray(root_spread_table(sub_count)), jnp.asarray(parent_table()),
        jnp.asarray(leaf_table_of_cells()), jnp.asarray(push_table()),
    )

    def general(state):
        return (*general_local(rhs, *lists), jnp.ones_like(state[2]))

    state = lax.while_loop(
        lambda state: state[2][0] == 0, general, (leaf_solution, parent_solution, good)
    )
    return state[0], state[1]


def solution(mesh):
    in_specs = (P(("blk", "sub"), None, None), P(("blk", "sub"), None), P(), P(), P(), P())
    out_specs = (P(("blk", "sub"), None, None), P(("blk", "sub"), None, None))
    return jax.shard_map(local, mesh=mesh, in_specs=in_specs, out_specs=out_specs, check_vma=False)
```

```python
import functools

import jax
import jax.numpy as jnp
from jax import lax
import numpy as np
from jax.experimental import pallas as pl
from jax.experimental.pallas import tpu as pltpu
from jax.sharding import PartitionSpec as P

ROOT_SWEEPS = 8
PMOST = 3


relax_weight = 0.8


def extended(block, sides, width):
    for axis, dim in sides:
        count = lax.axis_size(axis)
        forward = [(i, i + 1) for i in range(count - 1)]
        backward = [(target, source) for source, target in forward]
        low = lax.ppermute(
            lax.slice_in_dim(block, block.shape[dim] - width, None, axis=dim), axis, forward
        )
        high = lax.ppermute(lax.slice_in_dim(block, 0, width, axis=dim), axis, backward)
        block = jnp.concatenate([low, block, high], axis=dim)
    return block


def lane_parts():
    lanes = jnp.arange(256, dtype=jnp.int32)
    return (lanes // 16, lanes % 16)


def exact_dot(left, table):
    return jnp.einsum("...k,kl->...l", left, table, precision=lax.Precision.HIGHEST)


def spread_table(column):
    lane_y, lane_x = lane_parts()
    picked = (jnp.arange(16, dtype=jnp.int32)[:, None] == lane_y[None, :]) & (
        lane_x[None, :] == column
    )
    return picked.astype(jnp.float32)


def block_faces(values):
    blocks = values.shape[0]
    stacked = jnp.stack(
        [
            values[:, :, 0::16].reshape(blocks, 256),
            values[:, :, 15::16].reshape(blocks, 256),
            values[:, :, 0:16].reshape(blocks, 256),
            values[:, :, 240:256].reshape(blocks, 256),
            values[:, 0],
            values[:, 15],
        ],
        axis=1,
    )
    return stacked


def apply_operator(values, ghosts):
    blocks = values.shape[0]
    _, lane_x = lane_parts()
    ghost_x_low = ghosts[:, 0].reshape(blocks, 16, 16)
    ghost_x_high = ghosts[:, 1].reshape(blocks, 16, 16)
    ghost_y_low = ghosts[:, 2].reshape(blocks, 16, 16)
    ghost_y_high = ghosts[:, 3].reshape(blocks, 16, 16)
    from_left = jnp.where(
        lane_x[None, None, :] > 0, jnp.pad(values, ((0, 0), (0, 0), (1, 0)))[:, :, :256], 0.0
    )
    from_right = jnp.where(
        lane_x[None, None, :] < 15, jnp.pad(values, ((0, 0), (0, 0), (0, 1)))[:, :, 1:], 0.0
    )
    beside_all = from_left + exact_dot(ghost_x_low, spread_table(0))
    beside_all = beside_all + from_right + exact_dot(ghost_x_high, spread_table(15))
    beside_all = (
        beside_all
        + jnp.pad(values, ((0, 0), (0, 0), (16, 0)))[:, :, :256]
        + jnp.pad(ghost_y_low, ((0, 0), (0, 0), (0, 240)))
    )
    beside_all = (
        beside_all
        + jnp.pad(values, ((0, 0), (0, 0), (0, 16)))[:, :, 16:]
        + jnp.pad(ghost_y_high, ((0, 0), (0, 0), (240, 0)))
    )
    beside_all = beside_all + jnp.concatenate([ghosts[:, 4][:, None], values[:, :-1]], axis=1)
    beside_all = beside_all + jnp.concatenate([values[:, 1:], ghosts[:, 5][:, None]], axis=1)
    return 6.0 * values - beside_all


def jacobi_sweep(values, forcing, ghosts):
    return values + relax_weight / 6.0 * (forcing - apply_operator(values, ghosts))


def restrict_table():
    lane_y, lane_x = lane_parts()
    target = lane_y // 2 * 8 + lane_x // 2
    return (target[:, None] == jnp.arange(64, dtype=jnp.int32)[None, :]).astype(jnp.float32)


def coarse_table():
    lane_y, lane_x = lane_parts()
    target = lane_y // 4 * 4 + lane_x // 4
    return (target[:, None] == jnp.arange(16, dtype=jnp.int32)[None, :]).astype(jnp.float32)


def place_table():
    source_id = jnp.arange(256, dtype=jnp.int32)
    octant_y = source_id // 128
    octant_x = source_id // 64 % 2
    inner_y = source_id // 8 % 8
    inner_x = source_id % 8
    target = (8 * octant_y + inner_y) * 16 + 8 * octant_x + inner_x
    return (target[:, None] == jnp.arange(256, dtype=jnp.int32)[None, :]).astype(jnp.float32)


def restrict_octants(values):
    blocks = values.shape[0]
    paired = values.reshape(blocks, 8, 2, 256).sum(axis=2)
    return (exact_dot(paired, restrict_table()) * 0.5).reshape(blocks, 512)


def assemble(octant_rows):
    blocks = octant_rows.shape[0]
    arranged = (
        octant_rows.reshape(blocks, 2, 2, 2, 8, 64)
        .transpose(0, 1, 4, 2, 3, 5)
        .reshape(blocks, 16, 256)
    )
    return exact_dot(arranged, place_table())


def coarsen(values):
    blocks = values.shape[0]
    layered = values.reshape(blocks, 4, 4, 256).sum(axis=2)
    return (exact_dot(layered, coarse_table()) * 0.25).reshape(blocks, 64)


def widen_root(coarse):
    blocks = coarse.shape[0]
    flat = exact_dot(coarse.reshape(blocks, 4, 16), coarse_table().T)
    return jnp.repeat(flat, 4, axis=1)


def octant_split(values):
    blocks = values.shape[0]
    moved = exact_dot(values, place_table().T)
    return moved.reshape(blocks, 2, 8, 2, 2, 64).transpose(0, 1, 3, 4, 2, 5).reshape(blocks, 8, 512)


def widen_leaf(octant):
    blocks = octant.shape[0]
    flat = exact_dot(octant.reshape(blocks, 8, 64), restrict_table().T)
    return jnp.repeat(flat, 2, axis=1)


def slot_ranks(range_owners):
    width = range_owners.shape[1]
    same_owner = range_owners[:, :, None] == range_owners[:, None, :]
    earlier = (
        jnp.arange(width, dtype=jnp.int32)[:, None] > jnp.arange(width, dtype=jnp.int32)[None, :]
    )
    return jnp.sum(same_owner & earlier[None], axis=2)


def root_relax(root_values, root_source, row_len):
    plane_len = root_values.shape[1]
    padded_z = jnp.pad(root_values, ((1, 1), (0, 0)))
    padded_row = jnp.pad(root_values, ((0, 0), (row_len, row_len)))
    column_x = jnp.arange(plane_len, dtype=jnp.int32)[None, :] % row_len
    beside_all = padded_z[:-2] + padded_z[2:]
    beside_all = (
        beside_all
        + padded_row[:, :plane_len]
        + padded_row[:, 2 * row_len : 2 * row_len + plane_len]
    )
    beside_all = beside_all + jnp.where(
        column_x > 0, padded_row[:, row_len - 1 : row_len - 1 + plane_len], 0.0
    )
    beside_all = beside_all + jnp.where(
        column_x < row_len - 1, padded_row[:, row_len + 1 : row_len + 1 + plane_len], 0.0
    )
    return root_values + relax_weight / 6.0 * (root_source - (6.0 * root_values - beside_all))


def stack_table(range_faces, outer_faces):
    row_count = range_faces.shape[0]
    return jnp.concatenate(
        [
            range_faces.reshape(row_count * 6, 256),
            outer_faces[0],
            outer_faces[1],
            jnp.zeros((1, 256), jnp.float32),
        ],
        axis=0,
    )


def lookup(face_table, rows_index):
    blocks = rows_index.shape[0]
    return jnp.take(face_table, rows_index.reshape(-1), axis=0).reshape(blocks, 6, 256)


def table_index(neighbours, range_start, range_len):
    opposite = jnp.array([1, 0, 3, 2, 5, 4], dtype=jnp.int32)
    local_id = neighbours - range_start
    inside = (local_id >= 0) & (local_id < range_len)
    from_below = (neighbours >= 0) & (local_id < 0)
    from_above = local_id >= range_len
    rows_index = jnp.where(inside, local_id * 6 + opposite[None, :], range_len * 8)
    rows_index = jnp.where(from_below, range_len * 6 + local_id + range_len, rows_index)
    return jnp.where(from_above, range_len * 7 + local_id - range_len, rows_index)


def leaf_index(neighbours, blk_here, sub_here, sub_count):
    blocks = neighbours.shape[0]
    opposite = jnp.array([1, 0, 3, 2, 5, 4], dtype=jnp.int32)
    clamped = jnp.maximum(neighbours, 0)
    device_id = clamped // blocks
    local_id = clamped % blocks
    other_blk = device_id // sub_count
    other_sub = device_id % sub_count
    present = neighbours >= 0
    same_blk = present & (other_blk == blk_here)
    same_sub = present & (other_sub == sub_here)
    rows_index = jnp.where(same_blk & same_sub, local_id * 6 + opposite[None, :], blocks * 10)
    rows_index = jnp.where(
        same_blk & (other_sub == sub_here - 1), blocks * 6 + local_id, rows_index
    )
    rows_index = jnp.where(
        same_blk & (other_sub == sub_here + 1), blocks * 7 + local_id, rows_index
    )
    rows_index = jnp.where(
        same_sub & (other_blk == blk_here - 1), blocks * 8 + local_id, rows_index
    )
    rows_index = jnp.where(
        same_sub & (other_blk == blk_here + 1), blocks * 9 + local_id, rows_index
    )
    return rows_index


def leaf_table(values):
    face_rows = block_faces(values)
    blocks = face_rows.shape[0]
    side_rows = jnp.stack([face_rows[:, 0], face_rows[:, 1]], axis=0)
    side_wide = extended(side_rows, (("sub", 0),), 1)
    edge_rows = jnp.stack([face_rows[:, 4], face_rows[:, 5]], axis=0)
    edge_wide = extended(edge_rows, (("blk", 0),), 1)
    return jnp.concatenate(
        [
            face_rows.reshape(blocks * 6, 256),
            side_wide[0],
            side_wide[3],
            edge_wide[0],
            edge_wide[3],
            jnp.zeros((1, 256), jnp.float32),
        ],
        axis=0,
    )


def range_table(values):
    face_rows = block_faces(values)
    edge_rows = jnp.stack([face_rows[:, 4], face_rows[:, 5]], axis=0)
    widened = extended(edge_rows, (("blk", 0),), 1)
    return stack_table(face_rows, jnp.stack([widened[0], widened[3]], axis=0))


def general_local(rhs, leaf_neighbors, parent_neighbors, children, owners, parent_places):
    factor = relax_weight / 6.0
    blk_count = lax.axis_size("blk")
    sub_count = lax.axis_size("sub")
    blk_here = lax.axis_index("blk")
    sub_here = lax.axis_index("sub")
    blocks = rhs.shape[0]
    range_len = blocks * sub_count
    parent_len = range_len // 8
    range_start = blk_here * range_len
    parent_start = blk_here * parent_len
    leaf_rows = leaf_index(leaf_neighbors, blk_here, sub_here, sub_count)
    sweep_one = factor * rhs
    second = jacobi_sweep(sweep_one, rhs, lookup(leaf_table(sweep_one), leaf_rows))
    residual = rhs - apply_operator(second, lookup(leaf_table(second), leaf_rows))
    octant_rows = lax.all_gather(restrict_octants(residual), "sub", axis=0, tiled=True)
    range_children = lax.dynamic_slice_in_dim(children, parent_start, parent_len, 0) - range_start
    ranks_all = slot_ranks(owners.reshape(blk_count, parent_len)).reshape(-1)
    range_owners = lax.dynamic_slice_in_dim(owners, parent_start, parent_len, 0)
    range_ranks = lax.dynamic_slice_in_dim(ranks_all, parent_start, parent_len, 0)
    slot_match = (range_owners[None, :] == sub_here) & (
        range_ranks[None, :] == jnp.arange(PMOST, dtype=jnp.int32)[:, None]
    )
    filled = jnp.any(slot_match, axis=1)
    slot_local = jnp.sum(
        jnp.where(slot_match, jnp.arange(parent_len, dtype=jnp.int32)[None, :], 0), axis=1
    )
    filled_gain = filled.astype(jnp.float32)[:, None, None]
    own_local = sub_here * blocks + jnp.arange(blocks, dtype=jnp.int32)
    matches = range_children.reshape(-1)[None, :] == own_local[:, None]
    flat_place = jnp.sum(
        jnp.where(matches, jnp.arange(parent_len * 8, dtype=jnp.int32)[None, :], 0), axis=1
    )
    leaf_parent = flat_place // 8
    leaf_octant = flat_place % 8
    source = assemble(octant_rows[range_children])
    parent_rows = table_index(
        lax.dynamic_slice_in_dim(parent_neighbors, parent_start, parent_len, 0),
        parent_start,
        parent_len,
    )
    global_places = lax.dynamic_slice_in_dim(parent_places, parent_start, parent_len, 0)
    keep_gain = jnp.ones((parent_len, 1, 1), jnp.float32)
    parent_one = factor * source
    parent_two = jacobi_sweep(parent_one, source, lookup(range_table(parent_one), parent_rows))
    parent_rest = source - apply_operator(parent_two, lookup(range_table(parent_two), parent_rows))
    coarse = coarsen(parent_rest)
    root_slab = (
        jnp.zeros((parent_len, 64), jnp.float32).at[global_places - parent_start].set(coarse)
    )
    ordered = lax.all_gather(root_slab, "blk", axis=0, tiled=True)
    side_y = blocks // 4
    side_x = sub_count // 2
    root_source = (
        ordered.reshape(blk_count, side_y, side_x, 4, 4, 4)
        .transpose(0, 3, 1, 4, 2, 5)
        .reshape(4 * blk_count, 16 * side_y * side_x)
    )
    root_source = root_source - jnp.mean(root_source)
    root_values = jnp.zeros_like(root_source)
    for _ in range(ROOT_SWEEPS):
        root_values = root_relax(root_values, root_source, 4 * side_x)
    root_back = (
        root_values.reshape(blk_count, 4, side_y, 4, side_x, 4)
        .transpose(0, 2, 4, 1, 3, 5)
        .reshape(blk_count * parent_len, 64)[global_places]
    )
    parent_three = parent_two + widen_root(root_back) * keep_gain
    parent_four = jacobi_sweep(parent_three, source, lookup(range_table(parent_three), parent_rows))
    parent_solution = parent_four[slot_local] * filled_gain
    own_parents = parent_four[leaf_parent]
    pieces = octant_split(own_parents)
    chosen = jnp.take_along_axis(pieces, leaf_octant[:, None, None], axis=1)[:, 0]
    leaf_three = second + widen_leaf(chosen)
    leaf_solution = jacobi_sweep(leaf_three, rhs, lookup(leaf_table(leaf_three), leaf_rows))
    return (leaf_solution, parent_solution)


FACTOR = relax_weight / 6.0
SELF = 1.0 - 6.0 * FACTOR
LANES = 128
OWN_ROWS = 64
ROOT_ROW = 32
MSG_ROWS = 32
VMEM_LIMIT = 16 * 1024 * 1024


def lane_iota(shape):
    return lax.broadcasted_iota(jnp.int32, shape, len(shape) - 1)


def row_iota(shape):
    return lax.broadcasted_iota(jnp.int32, shape, len(shape) - 2)


def turn(values, shift, axis):
    size = values.shape[axis]
    shift = shift % size
    if shift == 0:
        return values
    return pltpu.roll(values, shift, axis)


def split_dot(left, table):
    high = left.astype(jnp.bfloat16)
    low = (left - high.astype(jnp.float32)).astype(jnp.bfloat16)
    return jnp.dot(high, table, preferred_element_type=jnp.float32) + jnp.dot(
        low, table, preferred_element_type=jnp.float32
    )


def zero_one(condition, scale=1.0):
    return np.where(condition, scale, 0.0).astype(jnp.bfloat16)


def key_col(rows, columns):
    return np.arange(rows)[:, None], np.arange(columns)[None, :]


def face_table():
    key, col = key_col(256, LANES)
    return zero_one(
        (key // 16 == col % 64)
        & (((col < 64) & (key % 16 == 0)) | ((col >= 64) & (key % 16 == 15)))
    )


def root_spread_table(sub_count):
    key, col = key_col(16 * sub_count, 256)
    return zero_one(key == (col // 32) * (2 * sub_count) + col % 8 // 4)


def parent_table():
    key, col = key_col(256, 256)
    return zero_one(key == (col % 16 // 8) * LANES + (col // 16) * 8 + col % 8)


def leaf_table_of_cells():
    key, col = key_col(256, 256)
    y = col // 16
    x = col % 16
    return zero_one(key == (y % 2 * 2 + x % 2) * 64 + y // 2 * 8 + x // 2)


def push_table():
    key, col = key_col(LANES, 256)
    group = key // 16
    cell = np.select([group == 0, group == 1, group == 4, group == 5], [0, 15, 1, 14], 16)
    return zero_one((key % 16 == col // 16) & (col % 16 == cell))


def beside_x(chunk, width):
    cell = lane_iota(chunk.shape) % width
    low = jnp.where(cell > 0, turn(chunk, 1, 1), 0.0)
    high = jnp.where(cell < width - 1, turn(chunk, -1, 1), 0.0)
    return low + high


def y_pair(chunks, width):
    lane = lane_iota(chunks[0].shape)
    up = [turn(chunk, width, 1) for chunk in chunks]
    down = [turn(chunk, -width, 1) for chunk in chunks]
    zero = jnp.zeros_like(chunks[0])
    lower = []
    upper = []
    for k in range(len(chunks)):
        before = up[k - 1] if k > 0 else zero
        after = down[k + 1] if k + 1 < len(chunks) else zero
        lower.append(jnp.where(lane < width, before, up[k]))
        upper.append(jnp.where(lane >= LANES - width, after, down[k]))
    return lower, upper


def z_pair(chunk):
    rows = chunk.shape[0]
    row = row_iota(chunk.shape)
    lower = jnp.where(row > 0, turn(chunk, 1, 0), 0.0)
    upper = jnp.where(row < rows - 1, turn(chunk, -1, 0), 0.0)
    return lower, upper


def fine_beside(chunks):
    lower, upper = y_pair(chunks, 16)
    in_x = [beside_x(chunk, 16) for chunk in chunks]
    in_y = [a + b for a, b in zip(lower, upper)]
    in_z = []
    for chunk in chunks:
        below, above = z_pair(chunk)
        in_z.append(below + above)
    return in_x, in_y, in_z


def coarse_turns(columns):
    return (
        [[turn(chunk, 8, 1) for chunk in halves] for halves in columns],
        [[turn(chunk, -8, 1) for chunk in halves] for halves in columns],
    )


def coarse_y_pair(up, down):
    lane = lane_iota(up[0].shape)
    zero = jnp.zeros_like(up[0])
    lower = []
    upper = []
    for half in range(2):
        lower.append(jnp.where(lane < 8, up[half - 1] if half > 0 else zero, up[half]))
        upper.append(jnp.where(lane >= LANES - 8, down[half + 1] if half < 1 else zero, down[half]))
    return lower, upper


def coarse_x_pair(columns, up, down, index, half):
    chunk = columns[index][half]
    cell = lane_iota(chunk.shape) % 8
    before = down[index - 1][half] if index > 0 else jnp.zeros_like(chunk)
    after = up[index + 1][half] if index + 1 < len(columns) else jnp.zeros_like(chunk)
    low = turn(jnp.where(cell == 7, before, chunk), 1, 1)
    high = turn(jnp.where(cell == 0, after, chunk), -1, 1)
    return low, high


def coarse_sums(columns):
    up, down = coarse_turns(columns)

    def sums(index):
        lower, upper = coarse_y_pair(up[index], down[index])
        halves = []
        for half in range(2):
            chunk = columns[index][half]
            low, high = coarse_x_pair(columns, up, down, index, half)
            total = low + high + lower[half] + upper[half]
            halves.append(total + turn(chunk, 1, 0) + turn(chunk, -1, 0))
        return halves

    return sums


def power_div(values, divisor):
    return lax.shift_right_logical(values, jnp.full_like(values, divisor.bit_length() - 1))


def power_rem(values, divisor):
    return values & (divisor - 1)


def octant_table():
    key = row_iota((256, LANES))
    col = lane_iota((256, LANES))
    key_x = power_rem(key, 16)
    col_x = power_rem(col, 8)
    side_x = jnp.where(col_x == 7, 0, jnp.where(col_x == 0, 15, 16))
    right_x = jnp.where(col < 64, power_div(key_x, 2) - col_x, key_x - side_x)
    right_y = power_div(key, 32) - power_div(power_rem(col, 64), 8)
    return jnp.where((right_x | right_y) == 0, 0.5, 0.0).astype(jnp.bfloat16)


def root_table(sub_count):
    shape = (4 * LANES, 16 * sub_count)
    key = row_iota(shape)
    near_x = power_div(power_rem(key, 8), 4)
    row = power_div(power_rem(key, 256), 32)
    along = jnp.where(key < 256, near_x + 1, 3 - 3 * near_x)
    target = row * (2 * sub_count) + along
    return jnp.where(lane_iota(shape) == target, 0.25, 0.0).astype(jnp.bfloat16)


def as_column(row):
    count = row.shape[1]
    shape = (count, count)
    return jnp.sum(
        jnp.where(row_iota(shape) == lane_iota(shape), row, 0.0), axis=1, keepdims=True
    )


def grid_codes(sub_count, wide_y, child_ref, place_ref):
    side_y = wide_y // 2
    side_x = sub_count // 2
    shape = child_ref.shape
    octant = row_iota(shape)
    place = jnp.broadcast_to(place_ref[...], shape)
    half_z = power_div(octant, 4)
    cell_z = 2 * power_div(place, side_y * side_x) + half_z
    cell_y = 2 * power_rem(power_div(place, side_x), side_y) + power_rem(power_div(octant, 2), 2)
    cell_x = 2 * power_rem(place, side_x) + power_rem(octant, 2)
    return (cell_z * wide_y + cell_y) * sub_count + cell_x, half_z * wide_y + cell_y


def of_own(child_ref, values, blocks, sub_count, sub_here, blk_here):
    first = (blk_here * sub_count + sub_here) * blocks
    values = values.astype(jnp.float32)
    return [
        jnp.sum(jnp.where(child_ref[...] == first + slot, values, 0.0)).astype(jnp.int32)
        for slot in range(blocks)
    ]


def lists_agree(
    sub_count, blk_count, leaf_ref, leaf_vector, parent_ref, child_ref, place_ref, codes, own
):
    blocks = len(own)
    wide_y = blocks // 2
    side_y = wide_y // 2
    side_x = sub_count // 2
    parents = child_ref.shape[1]
    layer = wide_y * sub_count
    children = child_ref[...]
    device = power_div(codes, 2 * layer) * sub_count + power_rem(codes, sub_count)
    missed = jnp.where(power_div(children, blocks) != device, 1.0, 0.0)
    shape = (blocks, 6)
    row = row_iota(shape)
    own_code = jnp.zeros(shape, jnp.int32)
    for slot in range(blocks):
        own_code = jnp.where(row == slot, own[slot], own_code)
        for face, stride in enumerate((-1, 1, -sub_count, sub_count, -layer, layer)):
            hit = (children == leaf_ref[slot, face]) & (codes == own[slot] + stride)
            missed = missed - jnp.where(hit, 1.0, 0.0)
    face = lane_iota(shape)
    along = jnp.where(
        face < 2,
        power_rem(own_code, sub_count),
        jnp.where(
            face < 4,
            power_rem(power_div(own_code, sub_count), wide_y),
            power_div(own_code, layer),
        ),
    )
    length = jnp.where(face < 2, sub_count, jnp.where(face < 4, wide_y, 2 * blk_count))
    goal = along + 2 * power_rem(face, 2) - 1
    exists = (goal >= 0) & (goal < length)
    listed = leaf_vector[...]
    faults = jnp.sum(
        jnp.where(
            exists,
            jnp.where(listed >= 0, 1.0, -100000.0),
            jnp.where(listed < 0, 0.0, -100000.0),
        )
    )
    wrong = jnp.abs(jnp.sum(missed) + faults)
    place_row = place_ref[...].astype(jnp.float32)
    place_column = as_column(place_row)
    number = row_iota((parents, parents))
    place = place_ref[...]
    missed = jnp.zeros((1, parents), jnp.float32)
    for axis, (stride, length) in enumerate(((1, side_x), (side_x, side_y), (side_y * side_x, blk_count))):
        along = power_rem(power_div(place, stride), length)
        for sign in (-1, 1):
            face = 2 * axis + (sign + 1) // 2
            listed = parent_ref[face : face + 1, :]
            found = jnp.sum(jnp.where(number == listed, place_column, 0.0), axis=0, keepdims=True)
            exists = (along + sign >= 0) & (along + sign < length)
            wanted = (place + sign * stride).astype(jnp.float32)
            missed = missed + jnp.where(
                exists,
                jnp.where((listed >= 0) & (found == wanted), 0.0, 1.0),
                jnp.where(listed < 0, 0.0, 1.0),
            )
    wrong = wrong + jnp.sum(missed)
    return jnp.where(wrong == 0.0, 1.0, 0.0)


def limits(sub_count, blk_count):
    sub_here = lax.axis_index("sub")
    blk_here = lax.axis_index("blk")

    def gain(condition):
        return jnp.where(condition, 1.0, 0.0).astype(jnp.float32)

    return (
        sub_here,
        blk_here,
        gain(sub_here > 0),
        gain(sub_here < sub_count - 1),
        gain(blk_here > 0),
        gain(blk_here < blk_count - 1),
    )


def placed_chunks(placed, wide_y):
    chunks = []
    for k in range(2 * wide_y):
        lanes = slice(LANES * (k % 2), LANES * (k % 2) + LANES)
        chunks.append(
            jnp.concatenate([placed[k // 2, :, lanes], placed[wide_y + k // 2, :, lanes]], axis=0)
        )
    return chunks


def return_gain(shape, x_low, x_high, z_low, z_high):
    cell = lane_iota(shape) % 16
    row = row_iota(shape)
    return (
        jnp.where(cell == 0, x_low, 0.0)
        + jnp.where(cell == 15, x_high, 0.0)
        + jnp.where(row == 0, z_low, 0.0)
        + jnp.where(row == shape[0] - 1, z_high, 0.0)
    ) * (FACTOR * FACTOR)


def push_kernel(
    sub_count, blk_count, blk_bits,
    leaf_hbm, parent_hbm, child_hbm, place_hbm, owner_hbm, rhs_hbm,
    placed, own_ref, leaf_out, parent_ref, child_ref, place_ref, owner_out, *rest
):
    msg_refs = rest[:blk_bits]
    leaf_ref, rhs_ref, rows_s, rows_g, left_a, coarse_s, sems = rest[blk_bits:]
    copies = [
        pltpu.make_async_copy(source, target, sems.at[k])
        for k, (source, target) in enumerate(
            (
                (child_hbm, child_ref),
                (place_hbm, place_ref),
                (rhs_hbm, rhs_ref),
                (leaf_hbm, leaf_ref),
                (parent_hbm, parent_ref),
                (leaf_hbm, leaf_out),
                (owner_hbm, owner_out),
            )
        )
    ]
    for copy in copies:
        copy.start()
    table_a = octant_table()
    table_r = root_table(sub_count)
    blocks = rhs_ref.shape[0]
    wide_y = blocks // 2
    f = FACTOR
    f2 = f * f
    sub_here, blk_here, x_low, x_high, z_low, z_high = limits(sub_count, blk_count)
    copies[0].wait()
    copies[1].wait()
    codes, positions = grid_codes(sub_count, wide_y, child_ref, place_ref)
    positions = of_own(child_ref, positions, blocks, sub_count, sub_here, blk_here)
    copies[2].wait()
    for slot in range(blocks):
        placed[positions[slot]] = rhs_ref[slot]
    s = placed_chunks(placed, wide_y)
    shape = s[0].shape
    top = shape[0] - 1
    back = return_gain(shape, x_low, x_high, z_low, z_high)
    sx, sy, sz = fine_beside(s)
    w = [SELF * a + f * (x + y + z) for a, x, y, z in zip(s, sx, sy, sz)]
    wx, wy, wz = fine_beside(w)
    for k in range(2 * wide_y):
        half = slice(LANES * (k % 2), LANES * (k % 2) + LANES)
        rows_s[k] = SELF * w[k] + f * (wx[k] + wy[k] + wz[k]) + back * s[k]
        base = (SELF * f + f2) * s[k] + f * w[k]
        rows_g[k] = base + f2 * (sy[k] + sz[k])
        gz = base + f2 * (sx[k] + sy[k])
        line = 48 * (k // 2)
        left_a[line + 16 : line + 17, half] = gz[0:1]
        left_a[line + 17 : line + 18, half] = gz[top : top + 1]
        left_a[line + 40 : line + 41, half] = (2.0 * f2) * s[k][0:1]
        left_a[line + 41 : line + 42, half] = (2.0 * f2) * s[k][top : top + 1]
        edge = gz + (f - f2) * s[k]
        for bit in range(blk_bits):
            upward = (blk_here // (1 << bit)) % 2 == 0
            msg_refs[bit][16 + k // 2 : 17 + k // 2, half] = jnp.where(
                upward, edge[top : top + 1], edge[0:1]
            )
            msg_refs[bit][16 + wide_y + k // 2 : 17 + wide_y + k // 2, half] = jnp.where(
                upward, s[k][top : top + 1], s[k][0:1]
            )
    for k in range(2 * wide_y):
        half = slice(LANES * (k % 2), LANES * (k % 2) + LANES)
        line = 48 * (k // 2)
        left_a[line : line + 16, half] = (
            rows_s[k, pl.ds(0, 16, stride=2), :] + rows_s[k, pl.ds(1, 16, stride=2), :]
        )
        left_a[line + 24 : line + 40, half] = (
            rows_g[k, pl.ds(0, 16, stride=2), :] + rows_g[k, pl.ds(1, 16, stride=2), :]
        )
    for copy in copies[3:]:
        copy.wait()
    out_a = split_dot(left_a[...], table_a)
    own_code = of_own(child_ref, codes, blocks, sub_count, sub_here, blk_here)
    good = lists_agree(
        sub_count, blk_count, leaf_ref, leaf_out, parent_ref, child_ref, place_ref, codes, own_code
    )
    lane24 = lane_iota((24, LANES))
    main = []
    side = []
    for half in range(2):
        first = out_a[96 * half : 96 * half + 24]
        second = out_a[96 * half + 48 : 96 * half + 72]
        main.append(jnp.where(lane24 < 64, first, turn(second, 64, 1)))
        first = out_a[96 * half + 24 : 96 * half + 48]
        second = out_a[96 * half + 72 : 96 * half + 96]
        side.append(jnp.where(lane24 < 64, turn(first, 64, 1), second))
    zero3 = jnp.zeros((3, LANES), jnp.float32)
    for half in range(2):
        lanes = slice(LANES * half, LANES * half + LANES)
        for base_row, piece in ((0, main[half]), (24, side[half])):
            own_ref[base_row : base_row + 3, lanes] = zero3
            own_ref[base_row + 3 : base_row + 4, lanes] = piece[16:17] * z_low
            own_ref[base_row + 4 : base_row + 20, lanes] = piece[0:16]
            own_ref[base_row + 20 : base_row + 21, lanes] = piece[17:18] * z_high
            own_ref[base_row + 21 : base_row + 24, lanes] = zero3
    cell8 = lane24 % 8
    row24 = row_iota((24, LANES))
    inside_z = jnp.where(row24 < 4, z_low, jnp.where(row24 >= 20, z_high, 1.0))
    gain = [inside_z * x_low, inside_z, inside_z * x_high]
    main24 = [own_ref[0:24, 0:LANES], own_ref[0:24, LANES:256]]
    side24 = [own_ref[24:48, 0:LANES], own_ref[24:48, LANES:256]]
    columns = [
        [jnp.where(cell8 == 7, piece, 0.0) * x_low for piece in side24],
        main24,
        [jnp.where(cell8 == 0, piece, 0.0) * x_high for piece in side24],
    ]
    sums = coarse_sums(columns)
    wp = []
    for b in range(3):
        near = sums(b)
        wp.append([gain[b] * (SELF * columns[b][h] + f * near[h]) for h in range(2)])
    sums = coarse_sums(wp)
    zero8 = jnp.zeros((8, LANES), jnp.float32)
    for b in range(3):
        near = sums(b)
        for h in range(2):
            coarse_s[2 * b + h, 0:24] = gain[b] * (SELF * wp[b][h] + f * near[h])
            coarse_s[2 * b + h, 24:32] = zero8
    pieces = []
    low_cells = lane_iota((8, LANES)) % 8 < 4
    for k in range(6):
        pieces.append(
            coarse_s[k, pl.ds(0, 8, stride=4), :]
            + coarse_s[k, pl.ds(1, 8, stride=4), :]
            + coarse_s[k, pl.ds(2, 8, stride=4), :]
            + coarse_s[k, pl.ds(3, 8, stride=4), :]
        )
    outer = [jnp.where(low_cells, pieces[4 + h], pieces[h]) for h in range(2)]
    root_left = jnp.concatenate([pieces[2], pieces[3]] + outer, axis=1)
    root_lanes = 16 * sub_count
    root_part = split_dot(root_left, table_r)
    root_part = pltpu.roll(root_part, 2 * sub_here + root_lanes - 1, 1)
    root_part = jnp.where(row_iota(root_part.shape) < 6, root_part, 0.0)
    own_ref[48:56, 0:root_lanes] = root_part
    if root_lanes < 256:
        own_ref[48:56, root_lanes:256] = jnp.zeros((8, 256 - root_lanes), jnp.float32)
    flag = jnp.zeros((8, LANES), jnp.float32) + good
    for lanes in (slice(0, LANES), slice(LANES, 256)):
        own_ref[56:64, lanes] = flag
    for bit in range(blk_bits):
        upward = (blk_here // (1 << bit)) % 2 == 0
        ref = msg_refs[bit]
        ref[8:16, :] = own_ref[48:56, :]
        ref[24:32, 0:LANES] = zero8
        ref[24:32, LANES:256] = flag
        for base_row, source in ((0, 0), (4, 24)):
            ref[base_row : base_row + 4, :] = jnp.where(
                upward, own_ref[source + 17 : source + 21, :], own_ref[source + 3 : source + 7, :]
            )


def side_kernel(
    sub_count, blk_count, slots,
    child_ref, owner_ref, place_ref, placed, table_ref,
    position_ref, slot_ref, part_ref, cross_ref, pair_ref,
    left_c
):
    blocks = placed.shape[0]
    wide_y = blocks // 2
    f = FACTOR
    f2 = f * f
    sub_here, blk_here, x_low, x_high, z_low, z_high = limits(sub_count, blk_count)
    _, positions = grid_codes(sub_count, wide_y, child_ref, place_ref)
    positions = of_own(child_ref, positions, blocks, sub_count, sub_here, blk_here)
    for slot in range(blocks):
        position_ref[slot] = positions[slot]
    s = placed_chunks(placed, wide_y)
    back = return_gain(s[0].shape, x_low, x_high, z_low, z_high)
    sx, sy, sz = fine_beside(s)
    w = [SELF * a + f * (x + y + z) for a, x, y, z in zip(s, sx, sy, sz)]
    wx, wy, wz = fine_beside(w)
    for k in range(2 * wide_y):
        half = slice(LANES * (k % 2), LANES * (k % 2) + LANES)
        r = SELF * w[k] + f * (wx[k] + wy[k] + wz[k]) + back * s[k]
        part = f * (s[k] + w[k] + r)
        part_ref[k // 2, :, half] = part[:16]
        part_ref[wide_y + k // 2, :, half] = part[16:]
        line = 64 * (k // 2)
        left_c[line : line + 32, half] = (
            (SELF * f + f) * s[k] + f * w[k] + f2 * (sy[k] + sz[k])
        )
        left_c[line + 32 : line + 64, half] = s[k]
    out_c = split_dot(left_c[...], table_ref[...])
    faces = out_c[0:64]
    for yy in range(1, wide_y):
        faces = faces + turn(out_c[64 * yy : 64 * yy + 64], 16 * yy, 1)
    lane = lane_iota((32, LANES))
    low = jnp.where(lane < 64, faces[0:32], turn(faces[32:64], 64, 1))
    high = jnp.where(lane < 64, turn(faces[0:32], 64, 1), faces[32:64])
    even = sub_here % 2 == 0
    cross_ref[...] = jnp.where(even, low, high)
    pair_ref[...] = jnp.where(even, high, low)
    owned = owned_slots(sub_count, blk_count, slots, sub_here, blk_here, owner_ref, place_ref)
    for k in range(slots):
        for j in range(3):
            slot_ref[3 * k + j] = owned[k][j]


def neighbour_pick(blk_here, blk_count, msg_refs):
    spans = []
    step = 1
    while step < blk_count:
        spans.append(step)
        step = 2 * step + 1

    def picker(other):
        choices = [(blk_here ^ other) == d for d in spans]

        def read(rows, lanes):
            value = msg_refs[spans[-1] - 1][rows, lanes]
            for choice, d in zip(choices[:-1], spans[:-1]):
                value = jnp.where(choice, msg_refs[d - 1][rows, lanes], value)
            return value

        return read

    return picker(blk_here - 1), picker(blk_here + 1)


def root_tiles(sub_count, blk_count):
    return (sub_count * blk_count // 16 + 1) // 2


def join_kernel(sub_count, blk_count, own_ref, cross_ref, *rest):
    msg_refs = rest[: blk_count - 1]
    out_ref, lines_ref, root_s = rest[blk_count - 1 :]
    _, blk_here, _, _, z_low, z_high = limits(sub_count, blk_count)
    below, above = neighbour_pick(blk_here, blk_count, msg_refs)
    row8 = row_iota((8, LANES))
    cell8 = lane_iota((8, LANES)) % 8
    low_rows = (row8 >= 1) & (row8 < 5)
    high_rows = (row8 >= 3) & (row8 < 7)
    good = own_ref[56:64, 0:LANES]
    for ref in msg_refs:
        good = jnp.minimum(good, ref[24:32, LANES:256])
    for half in range(2):
        lanes = slice(LANES * half, LANES * half + LANES)
        low = below(slice(0, 8), lanes) * z_low
        high = above(slice(0, 8), lanes) * z_high
        tiles = []
        for base, low_turn, high_turn in ((0, 1, 3), (24, 5, 7)):
            tiles.append(
                (
                    own_ref[base : base + 8, lanes]
                    + jnp.where(low_rows, turn(low, low_turn, 0), 0.0),
                    own_ref[base + 8 : base + 16, lanes],
                    own_ref[base + 16 : base + 24, lanes]
                    + jnp.where(high_rows, turn(high, high_turn, 0), 0.0),
                )
            )
        packed = tiles[1][0]
        for g in range(3):
            out_ref[8 * g : 8 * g + 8, lanes] = tiles[0][g]
            if g > 0:
                packed = packed + turn(jnp.where(cell8 == 0, tiles[1][g], 0.0), g, 1)
                packed = packed + turn(jnp.where(cell8 == 7, tiles[1][g], 0.0), -g, 1)
        out_ref[24:32, lanes] = packed
        out_ref[23:24, lanes] = good[0:1]
    root_s[...] = jnp.zeros(root_s.shape, jnp.float32)
    for d in range(blk_count):
        start = 4 * (blk_here ^ d) + 3
        for part in range(root_s.shape[0]):
            lanes = slice(LANES * part, LANES * part + LANES)
            value = own_ref[48:56, lanes] if d == 0 else msg_refs[d - 1][8:16, lanes]
            root_s[part, pl.ds(start, 8), :] = root_s[part, pl.ds(start, 8), :] + value
    tile = 0
    for start in range(0, 4 * blk_count, 8):
        for part in range(root_s.shape[0]):
            row = ROOT_ROW + 8 * (tile // 2)
            lanes = slice(LANES * (tile % 2), LANES * (tile % 2) + LANES)
            out_ref[row : row + 8, lanes] = root_s[part, 4 + start : 12 + start]
            tile += 1
    row = ROOT_ROW + 8 * root_tiles(sub_count, blk_count)
    count = lines_ref.shape[0] // 2
    half = count // 2
    low = below(slice(16, 16 + count), slice(0, 256)) * z_low
    high = above(slice(16, 16 + count), slice(0, 256)) * z_high
    lines_ref[0:count] = low
    lines_ref[count : 2 * count] = high
    out_ref[row : row + half, :] = low[half:count]
    out_ref[row + half : row + count, :] = high[half:count]
    out_ref[row + 8 : row + 24, 0:LANES] = cross_ref[0:16]
    out_ref[row + 8 : row + 24, LANES:256] = cross_ref[16:32]


def owned_slots(sub_count, blk_count, slots, sub_here, blk_here, owner_ref, place_ref):
    parents = owner_ref.shape[1]
    parent_len = parents // blk_count
    side_x = sub_count // 2
    side_y = parent_len // side_x
    number = lane_iota((1, parents))
    here = (owner_ref[...] == sub_here) & (lax.div(number, parent_len) == blk_here)
    mine = jnp.where(here, 1.0, 0.0)
    shape = (parents, parents)
    rank = jnp.sum(
        jnp.where(row_iota(shape) < lane_iota(shape), as_column(mine), 0.0), axis=0, keepdims=True
    )
    places = place_ref[...].astype(jnp.float32)
    found = []
    for k in range(slots):
        chosen = jnp.where(rank == float(k), mine, 0.0)
        place = jnp.sum(chosen * places).astype(jnp.int32)
        found.append(
            (
                lax.rem(lax.div(place, side_x), side_y),
                lax.rem(place, side_x),
                jnp.sum(chosen).astype(jnp.int32),
            )
        )
    return found


def exchange_slot(sub_count, distance):
    return lax.shift_right_logical(distance, 1) + (distance & 1) * (sub_count // 2)


def solve_kernel(
    sub_count, blk_count, slots,
    positions, owned, all_ref, pair_ref, part_ref, lines_ref, table_w_ref, table_p_ref, table_l_ref, table_x_ref,
    leaf_ref, parent_ref, good_ref,
    placed, par_s, root_s, fine_s, push_s
):
    blocks = part_ref.shape[0]
    wide_y = blocks // 2
    f = FACTOR
    f2 = f * f
    sub_here, blk_here, x_low, x_high, z_low, z_high = limits(sub_count, blk_count)
    slot_of = [exchange_slot(sub_count, sub_here ^ c) for c in range(sub_count)]
    row8 = row_iota((8, LANES))
    cell24 = lane_iota((24, LANES)) % 8
    row24 = row_iota((24, LANES))
    good = all_ref[0, 16:24, 0:LANES]
    for c in range(1, sub_count):
        good = jnp.minimum(good, all_ref[c, 16:24, 0:LANES])
    good_ref[0] = jnp.min(jnp.where(row8 == 7, good, 1.0)).astype(jnp.int32)
    cell8 = lane_iota((8, LANES)) % 8
    sides = []
    for c in range(sub_count):
        halves = []
        for half in range(2):
            packed = all_ref[slot_of[c], 24:32, LANES * half : LANES * half + LANES]
            halves.append(
                (
                    jnp.concatenate(
                        [jnp.where(cell8 == 7, turn(packed, g, 1), 0.0) for g in range(3)], axis=0
                    ),
                    jnp.concatenate(
                        [jnp.where(cell8 == 0, turn(packed, -g, 1), 0.0) for g in range(3)], axis=0
                    ),
                )
            )
        sides.append(halves)
    source = []
    for c in range(sub_count):
        halves = []
        for half in range(2):
            value = all_ref[slot_of[c], 0:24, LANES * half : LANES * half + LANES]
            if c + 1 < sub_count:
                value = value + sides[c + 1][half][0]
            if c > 0:
                value = value + sides[c - 1][half][1]
            halves.append(value)
        source.append(halves)

    root_lanes = 16 * sub_count
    row_len = 2 * sub_count
    root_rows = 4 * blk_count
    parts = root_lanes // LANES
    tile_rows = []
    tile = 0
    for _ in range(0, root_rows, 8):
        pieces = []
        for _ in range(parts):
            row = ROOT_ROW + 8 * (tile // 2)
            lanes = slice(LANES * (tile % 2), LANES * (tile % 2) + LANES)
            total = all_ref[0, row : row + 8, lanes]
            for c in range(1, sub_count):
                total = total + all_ref[c, row : row + 8, lanes]
            pieces.append(total)
            tile += 1
        tile_rows.append(jnp.concatenate(pieces, axis=1))
    root_source = jnp.concatenate(tile_rows, axis=0)
    root_source = root_source - jnp.sum(root_source) / (root_rows * root_lanes)
    shape = root_source.shape
    lane = lane_iota(shape)
    row = row_iota(shape)

    def root_sweep(values):
        total = jnp.where(lane % row_len > 0, turn(values, 1, 1), 0.0)
        total = total + jnp.where(lane % row_len < row_len - 1, turn(values, -1, 1), 0.0)
        total = total + jnp.where(lane >= row_len, turn(values, row_len, 1), 0.0)
        total = total + jnp.where(lane < root_lanes - row_len, turn(values, -row_len, 1), 0.0)
        total = total + jnp.where(row > 0, turn(values, 1, 0), 0.0)
        total = total + jnp.where(row < root_rows - 1, turn(values, -1, 0), 0.0)
        return SELF * values + f * (root_source + total)

    values = f * root_source
    left_sweeps = ROOT_SWEEPS - 1
    sums = coarse_sums(source)
    two = []
    for c in range(sub_count):
        if left_sweeps > 0:
            values = root_sweep(values)
            left_sweeps -= 1
        near = sums(c)
        two.append(
            [(f + f * SELF) * source[c][half] + f2 * near[half] for half in range(2)]
        )
    for _ in range(left_sweeps):
        values = root_sweep(values)
    root_s[...] = jnp.zeros(root_s.shape, jnp.float32)
    for part in range(parts):
        root_s[part, 4 : 4 + root_rows] = values[:, LANES * part : LANES * part + LANES]
    mine = jnp.concatenate(
        [root_s[part, pl.ds(4 * blk_here + 3, 8), :] for part in range(parts)], axis=1
    )
    left = jnp.concatenate([turn(mine, -2 * c, 1) for c in range(sub_count)], axis=0)
    wide = split_dot(left, table_w_ref[...])

    valid = (
        (row24 >= 2)
        & (row24 < 22)
        & ((row24 >= 4) | (z_low > 0.0))
        & ((row24 < 20) | (z_high > 0.0))
    )
    three = []
    for c in range(sub_count):
        halves = []
        for half in range(2):
            lanes = slice(LANES * half, LANES * half + LANES)
            tiles = []
            for t in range(3):
                first = wide[8 * c + 2 * t : 8 * c + 2 * t + 1, lanes]
                second = wide[8 * c + 2 * t + 1 : 8 * c + 2 * t + 2, lanes]
                tiles.append(
                    jnp.where(
                        row8 < 4,
                        jnp.broadcast_to(first, (8, LANES)),
                        jnp.broadcast_to(second, (8, LANES)),
                    )
                )
            value = two[c][half] + jnp.concatenate(tiles, axis=0)
            halves.append(jnp.where(valid, value, 0.0))
        three.append(halves)
    sums = coarse_sums(three)
    for c in range(sub_count):
        near = sums(c)
        for half in range(2):
            value = SELF * three[c][half] + f * (near[half] + source[c][half])
            par_s[c, half] = jnp.where(valid, value, 0.0)

    pieces = []
    for k in range(slots):
        half = owned[3 * k]
        place_x = owned[3 * k + 1]
        filled = owned[3 * k + 2].astype(jnp.float32)
        pieces.append(
            jnp.concatenate(
                [par_s[2 * place_x, half, 4:20], par_s[2 * place_x + 1, half, 4:20]], axis=1
            )
            * filled
        )
    left = jnp.concatenate(pieces, axis=0)
    moved = split_dot(left, table_p_ref[...])
    for k in range(slots):
        parent_ref[k] = moved[16 * k : 16 * k + 16]

    before = jnp.maximum(sub_here - 1, 0)
    after = jnp.minimum(sub_here + 1, sub_count - 1)
    columns = [
        [par_s[before, half] * x_low for half in range(2)],
        [par_s[sub_here, half] for half in range(2)],
        [par_s[after, half] * x_high for half in range(2)],
    ]
    centre = columns[1]
    up, down = coarse_turns(columns)
    in_y = coarse_y_pair(up[1], down[1])
    lane16 = lane_iota((16, LANES))
    left_rows = []
    in_x = [coarse_x_pair(columns, up, down, 1, half) for half in range(2)]
    blend = {}
    for half in range(2):
        for zp in range(2):
            base = (SELF + 3.0 * f) * centre[half] + f * turn(centre[half], 1 - 2 * zp, 0)
            for yp in range(2):
                for xp in range(2):
                    value = base + f * (in_y[yp][half] + in_x[half][xp])
                    blend[half, zp, 2 * yp + xp] = value[4:20]
    for yy in range(wide_y):
        half = yy // 2
        for zp in range(2):
            pair = []
            for v in (0, 2):
                first = blend[half, zp, v]
                second = blend[half, zp, v + 1]
                if yy % 2 == 0:
                    second = turn(second, 64, 1)
                else:
                    first = turn(first, 64, 1)
                pair.append(jnp.where(lane16 < 64, first, second))
            left_rows.append(jnp.concatenate(pair, axis=1))
    left = jnp.concatenate(left_rows, axis=0)
    spread = split_dot(left, table_l_ref[...])
    for yy in range(wide_y):
        for zp in range(2):
            top = 16 * (2 * yy + zp)
            fine_s[2 * yy, pl.ds(zp, 16, stride=2), :] = spread[top : top + 16, 0:128]
            fine_s[2 * yy + 1, pl.ds(zp, 16, stride=2), :] = spread[top : top + 16, 128:256]

    slot_before = exchange_slot(sub_count, sub_here ^ before)
    slot_after = exchange_slot(sub_count, sub_here ^ after)
    line = ROOT_ROW + 8 * root_tiles(sub_count, blk_count)
    even = sub_here % 2 == 0

    def crossed(slot):
        rows = all_ref[slot, line + 8 : line + 24, :]
        return jnp.concatenate([rows[:, 0:LANES], rows[:, LANES:256]], axis=0)

    pair = pair_ref[...]
    from_low = jnp.where(even, crossed(slot_before), pair) * x_low
    from_high = jnp.where(even, pair, crossed(slot_after)) * x_high
    behind = jnp.where(lane_iota((32, LANES)) < 64, 1.0, f2)
    left = [from_low * behind, from_high * behind]
    lane128 = lane_iota((32, LANES))
    rows = []
    for yy in range(wide_y):
        rows.append(
            jnp.where(
                lax.rem(lane128, 64) < 16,
                turn(left[0], -16 * yy, 1),
                turn(left[1], 16 - 16 * yy, 1),
            )
        )
    push = split_dot(jnp.concatenate(rows, axis=0), table_x_ref[...])
    for yy in range(wide_y):
        push_s[:, 256 * yy : 256 * yy + 256] = push[32 * yy : 32 * yy + 32]
    cell = lane_iota((2 * wide_y, 256)) % 16
    across = jnp.where(
        cell == 0, turn(all_ref[slot_before, line : line + 2 * wide_y, :], -15, 1) * x_low, 0.0
    ) + jnp.where(
        cell == 15, turn(all_ref[slot_after, line : line + 2 * wide_y, :], 15, 1) * x_high, 0.0
    )
    across = (2.0 * f2) * across
    count = 2 * wide_y
    for yy in range(wide_y):
        lanes = slice(256 * yy, 256 * yy + 256)
        push_s[0:1, lanes] = push_s[0:1, lanes] + lines_ref[yy : yy + 1] + across[yy : yy + 1]
        push_s[1:2, lanes] = push_s[1:2, lanes] + f2 * lines_ref[wide_y + yy : wide_y + yy + 1]
        push_s[31:32, lanes] = (
            push_s[31:32, lanes]
            + lines_ref[count + yy : count + yy + 1]
            + across[wide_y + yy : wide_y + yy + 1]
        )
        push_s[30:31, lanes] = (
            push_s[30:31, lanes]
            + f2 * lines_ref[count + wide_y + yy : count + wide_y + yy + 1]
        )
    for zz in range(2):
        for yy in range(wide_y):
            rows = slice(16 * zz, 16 * zz + 16)
            lanes = slice(256 * yy, 256 * yy + 256)
            index = zz * wide_y + yy
            fine = jnp.concatenate([fine_s[2 * yy, rows], fine_s[2 * yy + 1, rows]], axis=1)
            placed[index] = part_ref[index] + fine + f * push_s[rows, lanes]
    for slot in range(blocks):
        leaf_ref[slot] = placed[positions[slot]]


def paired(count, step):
    return [(i, i ^ step) for i in range(count)]


def is_power(number):
    return number > 0 and number & (number - 1) == 0


def local(rhs, leaf_neighbors, parent_neighbors, children, owners, parent_places):
    blk_count = lax.axis_size("blk")
    sub_count = lax.axis_size("sub")
    blocks = rhs.shape[0]
    wide_y = blocks // 2
    lists = (leaf_neighbors, parent_neighbors, children, owners, parent_places)
    fits = 32 * blocks == 2 * LANES and 16 * sub_count in (LANES, 2 * LANES)
    if not (fits and blk_count > 1 and is_power(blk_count)):
        return general_local(rhs, *lists)
    blk_bits = blk_count.bit_length() - 1
    f32 = jnp.float32
    vmem = pl.BlockSpec(memory_space=pltpu.VMEM)
    smem = pl.BlockSpec(memory_space=pltpu.SMEM)
    params = pltpu.CompilerParams(vmem_limit_bytes=VMEM_LIMIT)
    owner_row = owners.reshape(1, -1)
    place_row = parent_places.reshape(1, -1)
    child_rows = children.T
    parent_rows = parent_neighbors.T
    grid_shape = (blocks, 16, 256)
    outs = pl.pallas_call(
        functools.partial(push_kernel, sub_count, blk_count, blk_bits),
        name="push",
        out_shape=[
            jax.ShapeDtypeStruct(grid_shape, f32),
            jax.ShapeDtypeStruct((OWN_ROWS, 256), f32),
        ]
        + [
            jax.ShapeDtypeStruct(array.shape, jnp.int32)
            for array in (leaf_neighbors, parent_rows, child_rows, place_row, owner_row)
        ]
        + [jax.ShapeDtypeStruct((MSG_ROWS, 256), f32)] * blk_bits,
        in_specs=[pl.BlockSpec(memory_space=pltpu.HBM)] * 6,
        out_specs=[vmem] * (7 + blk_bits),
        scratch_shapes=[
            pltpu.SMEM(leaf_neighbors.shape, jnp.int32),
            pltpu.VMEM(grid_shape, f32),
            pltpu.VMEM((2 * wide_y, 32, LANES), f32),
            pltpu.VMEM((2 * wide_y, 32, LANES), f32),
            pltpu.VMEM((48 * wide_y, 256), f32),
            pltpu.VMEM((6, 32, LANES), f32),
            pltpu.SemaphoreType.DMA((7,)),
        ],
        compiler_params=params,
    )(
        *(
            pltpu.with_memory_space_constraint(array, pltpu.HBM)
            for array in (leaf_neighbors, parent_rows, child_rows, place_row, owner_row, rhs)
        )
    )
    placed, own, leaf_neighbors, parent_rows, child_rows, place_row, owner_row = outs[:7]
    messages = outs[7:]
    lists = (
        leaf_neighbors, parent_rows.T, child_rows.T, owner_row.reshape(-1), place_row.reshape(-1),
    )
    received = []
    for d in range(1, blk_count):
        received.append(
            lax.ppermute(messages[d.bit_length() - 1], "blk", paired(blk_count, d))
        )
    positions, owned, own_part, cross_faces, pair_faces = pl.pallas_call(
        functools.partial(side_kernel, sub_count, blk_count, PMOST),
        name="side",
        out_shape=[
            jax.ShapeDtypeStruct((blocks,), jnp.int32),
            jax.ShapeDtypeStruct((3 * PMOST,), jnp.int32),
            jax.ShapeDtypeStruct(grid_shape, f32),
        ]
        + [jax.ShapeDtypeStruct((32, LANES), f32)] * 2,
        in_specs=[vmem] * 5,
        out_specs=[smem] * 2 + [vmem] * 3,
        scratch_shapes=[pltpu.VMEM((64 * wide_y, 256), f32)],
        compiler_params=params,
    )(child_rows, owner_row, place_row, placed, jnp.asarray(face_table()))
    pair_faces = lax.ppermute(pair_faces, "sub", paired(sub_count, 1))
    root_parts = 16 * sub_count // LANES
    joined_rows = ROOT_ROW + 8 * root_tiles(sub_count, blk_count) + 8 + 16
    joined, lines = pl.pallas_call(
        functools.partial(join_kernel, sub_count, blk_count),
        name="join",
        out_shape=[
            jax.ShapeDtypeStruct((joined_rows, 256), f32),
            jax.ShapeDtypeStruct((4 * wide_y, 256), f32),
        ],
        in_specs=[vmem] * (1 + blk_count),
        out_specs=[vmem] * 2,
        scratch_shapes=[pltpu.VMEM((root_parts, 4 * blk_count + 8, LANES), f32)],
        compiler_params=params,
    )(own, cross_faces, *received)
    block = [joined]
    for d in range(2, sub_count, 2):
        block.append(lax.ppermute(joined, "sub", paired(sub_count, d)))
    block = jnp.stack(block)
    other = lax.ppermute(block, "sub", paired(sub_count, 1))
    gathered = jnp.concatenate([block, other], axis=0)
    leaf_solution, parent_solution, good = pl.pallas_call(
        functools.partial(solve_kernel, sub_count, blk_count, PMOST),
        name="solve",
        out_shape=[
            jax.ShapeDtypeStruct((blocks, 16, 256), f32),
            jax.ShapeDtypeStruct((PMOST, 16, 256), f32),
            jax.ShapeDtypeStruct((1,), jnp.int32),
        ],
        in_specs=[smem] * 2 + [vmem] * 8,
        out_specs=[vmem] * 2 + [smem],
        scratch_shapes=[
            pltpu.VMEM((blocks, 16, 256), f32),
            pltpu.VMEM((sub_count, 2, 24, LANES), f32),
            pltpu.VMEM((root_parts, 4 * blk_count + 8, LANES), f32),
            pltpu.VMEM((2 * wide_y, 32, LANES), f32),
            pltpu.VMEM((32, 256 * wide_y), f32),
        ],
        compiler_params=params,
    )(
        positions, owned, gathered, pair_faces, own_part, lines,
        jnp.asarray(root_spread_table(sub_count)), jnp.asarray(parent_table()),
        jnp.asarray(leaf_table_of_cells()), jnp.asarray(push_table()),
    )

    def general(state):
        return (*general_local(rhs, *lists), jnp.ones_like(state[2]))

    state = lax.while_loop(
        lambda state: state[2][0] == 0, general, (leaf_solution, parent_solution, good)
    )
    return state[0], state[1]


def solution(mesh):
    in_specs = (P(("blk", "sub"), None, None), P(("blk", "sub"), None), P(), P(), P(), P())
    out_specs = (P(("blk", "sub"), None, None), P(("blk", "sub"), None, None))
    return jax.shard_map(local, mesh=mesh, in_specs=in_specs, out_specs=out_specs, check_vma=False)
```

```python
import functools

import jax
import jax.numpy as jnp
from jax import lax
import numpy as np
from jax.experimental import pallas as pl
from jax.experimental.pallas import tpu as pltpu
from jax.sharding import PartitionSpec as P

ROOT_SWEEPS = 8
PMOST = 3


relax_weight = 0.8


def extended(block, sides, width):
    for axis, dim in sides:
        count = lax.axis_size(axis)
        forward = [(i, i + 1) for i in range(count - 1)]
        backward = [(target, source) for source, target in forward]
        low = lax.ppermute(
            lax.slice_in_dim(block, block.shape[dim] - width, None, axis=dim), axis, forward
        )
        high = lax.ppermute(lax.slice_in_dim(block, 0, width, axis=dim), axis, backward)
        block = jnp.concatenate([low, block, high], axis=dim)
    return block


def lane_parts():
    lanes = jnp.arange(256, dtype=jnp.int32)
    return (lanes // 16, lanes % 16)


def exact_dot(left, table):
    return jnp.einsum("...k,kl->...l", left, table, precision=lax.Precision.HIGHEST)


def spread_table(column):
    lane_y, lane_x = lane_parts()
    picked = (jnp.arange(16, dtype=jnp.int32)[:, None] == lane_y[None, :]) & (
        lane_x[None, :] == column
    )
    return picked.astype(jnp.float32)


def block_faces(values):
    blocks = values.shape[0]
    stacked = jnp.stack(
        [
            values[:, :, 0::16].reshape(blocks, 256),
            values[:, :, 15::16].reshape(blocks, 256),
            values[:, :, 0:16].reshape(blocks, 256),
            values[:, :, 240:256].reshape(blocks, 256),
            values[:, 0],
            values[:, 15],
        ],
        axis=1,
    )
    return stacked


def apply_operator(values, ghosts):
    blocks = values.shape[0]
    _, lane_x = lane_parts()
    ghost_x_low = ghosts[:, 0].reshape(blocks, 16, 16)
    ghost_x_high = ghosts[:, 1].reshape(blocks, 16, 16)
    ghost_y_low = ghosts[:, 2].reshape(blocks, 16, 16)
    ghost_y_high = ghosts[:, 3].reshape(blocks, 16, 16)
    from_left = jnp.where(
        lane_x[None, None, :] > 0, jnp.pad(values, ((0, 0), (0, 0), (1, 0)))[:, :, :256], 0.0
    )
    from_right = jnp.where(
        lane_x[None, None, :] < 15, jnp.pad(values, ((0, 0), (0, 0), (0, 1)))[:, :, 1:], 0.0
    )
    beside_all = from_left + exact_dot(ghost_x_low, spread_table(0))
    beside_all = beside_all + from_right + exact_dot(ghost_x_high, spread_table(15))
    beside_all = (
        beside_all
        + jnp.pad(values, ((0, 0), (0, 0), (16, 0)))[:, :, :256]
        + jnp.pad(ghost_y_low, ((0, 0), (0, 0), (0, 240)))
    )
    beside_all = (
        beside_all
        + jnp.pad(values, ((0, 0), (0, 0), (0, 16)))[:, :, 16:]
        + jnp.pad(ghost_y_high, ((0, 0), (0, 0), (240, 0)))
    )
    beside_all = beside_all + jnp.concatenate([ghosts[:, 4][:, None], values[:, :-1]], axis=1)
    beside_all = beside_all + jnp.concatenate([values[:, 1:], ghosts[:, 5][:, None]], axis=1)
    return 6.0 * values - beside_all


def jacobi_sweep(values, forcing, ghosts):
    return values + relax_weight / 6.0 * (forcing - apply_operator(values, ghosts))


def restrict_table():
    lane_y, lane_x = lane_parts()
    target = lane_y // 2 * 8 + lane_x // 2
    return (target[:, None] == jnp.arange(64, dtype=jnp.int32)[None, :]).astype(jnp.float32)


def coarse_table():
    lane_y, lane_x = lane_parts()
    target = lane_y // 4 * 4 + lane_x // 4
    return (target[:, None] == jnp.arange(16, dtype=jnp.int32)[None, :]).astype(jnp.float32)


def place_table():
    source_id = jnp.arange(256, dtype=jnp.int32)
    octant_y = source_id // 128
    octant_x = source_id // 64 % 2
    inner_y = source_id // 8 % 8
    inner_x = source_id % 8
    target = (8 * octant_y + inner_y) * 16 + 8 * octant_x + inner_x
    return (target[:, None] == jnp.arange(256, dtype=jnp.int32)[None, :]).astype(jnp.float32)


def restrict_octants(values):
    blocks = values.shape[0]
    paired = values.reshape(blocks, 8, 2, 256).sum(axis=2)
    return (exact_dot(paired, restrict_table()) * 0.5).reshape(blocks, 512)


def assemble(octant_rows):
    blocks = octant_rows.shape[0]
    arranged = (
        octant_rows.reshape(blocks, 2, 2, 2, 8, 64)
        .transpose(0, 1, 4, 2, 3, 5)
        .reshape(blocks, 16, 256)
    )
    return exact_dot(arranged, place_table())


def coarsen(values):
    blocks = values.shape[0]
    layered = values.reshape(blocks, 4, 4, 256).sum(axis=2)
    return (exact_dot(layered, coarse_table()) * 0.25).reshape(blocks, 64)


def widen_root(coarse):
    blocks = coarse.shape[0]
    flat = exact_dot(coarse.reshape(blocks, 4, 16), coarse_table().T)
    return jnp.repeat(flat, 4, axis=1)


def octant_split(values):
    blocks = values.shape[0]
    moved = exact_dot(values, place_table().T)
    return moved.reshape(blocks, 2, 8, 2, 2, 64).transpose(0, 1, 3, 4, 2, 5).reshape(blocks, 8, 512)


def widen_leaf(octant):
    blocks = octant.shape[0]
    flat = exact_dot(octant.reshape(blocks, 8, 64), restrict_table().T)
    return jnp.repeat(flat, 2, axis=1)


def slot_ranks(range_owners):
    width = range_owners.shape[1]
    same_owner = range_owners[:, :, None] == range_owners[:, None, :]
    earlier = (
        jnp.arange(width, dtype=jnp.int32)[:, None] > jnp.arange(width, dtype=jnp.int32)[None, :]
    )
    return jnp.sum(same_owner & earlier[None], axis=2)


def root_relax(root_values, root_source, row_len):
    plane_len = root_values.shape[1]
    padded_z = jnp.pad(root_values, ((1, 1), (0, 0)))
    padded_row = jnp.pad(root_values, ((0, 0), (row_len, row_len)))
    column_x = jnp.arange(plane_len, dtype=jnp.int32)[None, :] % row_len
    beside_all = padded_z[:-2] + padded_z[2:]
    beside_all = (
        beside_all
        + padded_row[:, :plane_len]
        + padded_row[:, 2 * row_len : 2 * row_len + plane_len]
    )
    beside_all = beside_all + jnp.where(
        column_x > 0, padded_row[:, row_len - 1 : row_len - 1 + plane_len], 0.0
    )
    beside_all = beside_all + jnp.where(
        column_x < row_len - 1, padded_row[:, row_len + 1 : row_len + 1 + plane_len], 0.0
    )
    return root_values + relax_weight / 6.0 * (root_source - (6.0 * root_values - beside_all))


def stack_table(range_faces, outer_faces):
    row_count = range_faces.shape[0]
    return jnp.concatenate(
        [
            range_faces.reshape(row_count * 6, 256),
            outer_faces[0],
            outer_faces[1],
            jnp.zeros((1, 256), jnp.float32),
        ],
        axis=0,
    )


def lookup(face_table, rows_index):
    blocks = rows_index.shape[0]
    return jnp.take(face_table, rows_index.reshape(-1), axis=0).reshape(blocks, 6, 256)


def table_index(neighbours, range_start, range_len):
    opposite = jnp.array([1, 0, 3, 2, 5, 4], dtype=jnp.int32)
    local_id = neighbours - range_start
    inside = (local_id >= 0) & (local_id < range_len)
    from_below = (neighbours >= 0) & (local_id < 0)
    from_above = local_id >= range_len
    rows_index = jnp.where(inside, local_id * 6 + opposite[None, :], range_len * 8)
    rows_index = jnp.where(from_below, range_len * 6 + local_id + range_len, rows_index)
    return jnp.where(from_above, range_len * 7 + local_id - range_len, rows_index)


def leaf_index(neighbours, blk_here, sub_here, sub_count):
    blocks = neighbours.shape[0]
    opposite = jnp.array([1, 0, 3, 2, 5, 4], dtype=jnp.int32)
    clamped = jnp.maximum(neighbours, 0)
    device_id = clamped // blocks
    local_id = clamped % blocks
    other_blk = device_id // sub_count
    other_sub = device_id % sub_count
    present = neighbours >= 0
    same_blk = present & (other_blk == blk_here)
    same_sub = present & (other_sub == sub_here)
    rows_index = jnp.where(same_blk & same_sub, local_id * 6 + opposite[None, :], blocks * 10)
    rows_index = jnp.where(
        same_blk & (other_sub == sub_here - 1), blocks * 6 + local_id, rows_index
    )
    rows_index = jnp.where(
        same_blk & (other_sub == sub_here + 1), blocks * 7 + local_id, rows_index
    )
    rows_index = jnp.where(
        same_sub & (other_blk == blk_here - 1), blocks * 8 + local_id, rows_index
    )
    rows_index = jnp.where(
        same_sub & (other_blk == blk_here + 1), blocks * 9 + local_id, rows_index
    )
    return rows_index


def leaf_table(values):
    face_rows = block_faces(values)
    blocks = face_rows.shape[0]
    side_rows = jnp.stack([face_rows[:, 0], face_rows[:, 1]], axis=0)
    side_wide = extended(side_rows, (("sub", 0),), 1)
    edge_rows = jnp.stack([face_rows[:, 4], face_rows[:, 5]], axis=0)
    edge_wide = extended(edge_rows, (("blk", 0),), 1)
    return jnp.concatenate(
        [
            face_rows.reshape(blocks * 6, 256),
            side_wide[0],
            side_wide[3],
            edge_wide[0],
            edge_wide[3],
            jnp.zeros((1, 256), jnp.float32),
        ],
        axis=0,
    )


def range_table(values):
    face_rows = block_faces(values)
    edge_rows = jnp.stack([face_rows[:, 4], face_rows[:, 5]], axis=0)
    widened = extended(edge_rows, (("blk", 0),), 1)
    return stack_table(face_rows, jnp.stack([widened[0], widened[3]], axis=0))


def general_local(rhs, leaf_neighbors, parent_neighbors, children, owners, parent_places):
    factor = relax_weight / 6.0
    blk_count = lax.axis_size("blk")
    sub_count = lax.axis_size("sub")
    blk_here = lax.axis_index("blk")
    sub_here = lax.axis_index("sub")
    blocks = rhs.shape[0]
    range_len = blocks * sub_count
    parent_len = range_len // 8
    range_start = blk_here * range_len
    parent_start = blk_here * parent_len
    leaf_rows = leaf_index(leaf_neighbors, blk_here, sub_here, sub_count)
    sweep_one = factor * rhs
    second = jacobi_sweep(sweep_one, rhs, lookup(leaf_table(sweep_one), leaf_rows))
    residual = rhs - apply_operator(second, lookup(leaf_table(second), leaf_rows))
    octant_rows = lax.all_gather(restrict_octants(residual), "sub", axis=0, tiled=True)
    range_children = lax.dynamic_slice_in_dim(children, parent_start, parent_len, 0) - range_start
    ranks_all = slot_ranks(owners.reshape(blk_count, parent_len)).reshape(-1)
    range_owners = lax.dynamic_slice_in_dim(owners, parent_start, parent_len, 0)
    range_ranks = lax.dynamic_slice_in_dim(ranks_all, parent_start, parent_len, 0)
    slot_match = (range_owners[None, :] == sub_here) & (
        range_ranks[None, :] == jnp.arange(PMOST, dtype=jnp.int32)[:, None]
    )
    filled = jnp.any(slot_match, axis=1)
    slot_local = jnp.sum(
        jnp.where(slot_match, jnp.arange(parent_len, dtype=jnp.int32)[None, :], 0), axis=1
    )
    filled_gain = filled.astype(jnp.float32)[:, None, None]
    own_local = sub_here * blocks + jnp.arange(blocks, dtype=jnp.int32)
    matches = range_children.reshape(-1)[None, :] == own_local[:, None]
    flat_place = jnp.sum(
        jnp.where(matches, jnp.arange(parent_len * 8, dtype=jnp.int32)[None, :], 0), axis=1
    )
    leaf_parent = flat_place // 8
    leaf_octant = flat_place % 8
    source = assemble(octant_rows[range_children])
    parent_rows = table_index(
        lax.dynamic_slice_in_dim(parent_neighbors, parent_start, parent_len, 0),
        parent_start,
        parent_len,
    )
    global_places = lax.dynamic_slice_in_dim(parent_places, parent_start, parent_len, 0)
    keep_gain = jnp.ones((parent_len, 1, 1), jnp.float32)
    parent_one = factor * source
    parent_two = jacobi_sweep(parent_one, source, lookup(range_table(parent_one), parent_rows))
    parent_rest = source - apply_operator(parent_two, lookup(range_table(parent_two), parent_rows))
    coarse = coarsen(parent_rest)
    root_slab = (
        jnp.zeros((parent_len, 64), jnp.float32).at[global_places - parent_start].set(coarse)
    )
    ordered = lax.all_gather(root_slab, "blk", axis=0, tiled=True)
    side_y = blocks // 4
    side_x = sub_count // 2
    root_source = (
        ordered.reshape(blk_count, side_y, side_x, 4, 4, 4)
        .transpose(0, 3, 1, 4, 2, 5)
        .reshape(4 * blk_count, 16 * side_y * side_x)
    )
    root_source = root_source - jnp.mean(root_source)
    root_values = jnp.zeros_like(root_source)
    for _ in range(ROOT_SWEEPS):
        root_values = root_relax(root_values, root_source, 4 * side_x)
    root_back = (
        root_values.reshape(blk_count, 4, side_y, 4, side_x, 4)
        .transpose(0, 2, 4, 1, 3, 5)
        .reshape(blk_count * parent_len, 64)[global_places]
    )
    parent_three = parent_two + widen_root(root_back) * keep_gain
    parent_four = jacobi_sweep(parent_three, source, lookup(range_table(parent_three), parent_rows))
    parent_solution = parent_four[slot_local] * filled_gain
    own_parents = parent_four[leaf_parent]
    pieces = octant_split(own_parents)
    chosen = jnp.take_along_axis(pieces, leaf_octant[:, None, None], axis=1)[:, 0]
    leaf_three = second + widen_leaf(chosen)
    leaf_solution = jacobi_sweep(leaf_three, rhs, lookup(leaf_table(leaf_three), leaf_rows))
    return (leaf_solution, parent_solution)


FACTOR = relax_weight / 6.0
SELF = 1.0 - 6.0 * FACTOR
LANES = 128
OWN_ROWS = 56
ROOT_ROW = 32
MSG_ROWS = 24
VMEM_LIMIT = 16 * 1024 * 1024


def lane_iota(shape):
    return lax.broadcasted_iota(jnp.int32, shape, len(shape) - 1)


def row_iota(shape):
    return lax.broadcasted_iota(jnp.int32, shape, len(shape) - 2)


def turn(values, shift, axis):
    size = values.shape[axis]
    shift = shift % size
    if shift == 0:
        return values
    return pltpu.roll(values, shift, axis)


def split_dot(left, table):
    high = left.astype(jnp.bfloat16)
    low = (left - high.astype(jnp.float32)).astype(jnp.bfloat16)
    return jnp.dot(high, table, preferred_element_type=jnp.float32) + jnp.dot(
        low, table, preferred_element_type=jnp.float32
    )


def zero_one(condition, scale=1.0):
    return np.where(condition, scale, 0.0).astype(jnp.bfloat16)


def key_col(rows, columns):
    return np.arange(rows)[:, None], np.arange(columns)[None, :]


def face_table():
    key, col = key_col(256, LANES)
    return zero_one(
        (key // 16 == col % 64)
        & (((col < 64) & (key % 16 == 0)) | ((col >= 64) & (key % 16 == 15)))
    )


def root_spread_table(sub_count):
    key, col = key_col(16 * sub_count, 256)
    return zero_one(key == (col // 32) * (2 * sub_count) + col % 8 // 4)


def parent_table():
    key, col = key_col(256, 256)
    return zero_one(key == (col % 16 // 8) * LANES + (col // 16) * 8 + col % 8)


def leaf_table_of_cells():
    key, col = key_col(256, 256)
    y = col // 16
    x = col % 16
    return zero_one(key == (y % 2 * 2 + x % 2) * 64 + y // 2 * 8 + x // 2)


def push_table():
    key, col = key_col(LANES, 256)
    group = key // 16
    cell = np.select([group == 0, group == 1, group == 4, group == 5], [0, 15, 1, 14], 16)
    return zero_one((key % 16 == col // 16) & (col % 16 == cell))


def beside_x(chunk, width):
    cell = lane_iota(chunk.shape) % width
    low = jnp.where(cell > 0, turn(chunk, 1, 1), 0.0)
    high = jnp.where(cell < width - 1, turn(chunk, -1, 1), 0.0)
    return low + high


def y_pair(chunks, width):
    lane = lane_iota(chunks[0].shape)
    up = [turn(chunk, width, 1) for chunk in chunks]
    down = [turn(chunk, -width, 1) for chunk in chunks]
    zero = jnp.zeros_like(chunks[0])
    lower = []
    upper = []
    for k in range(len(chunks)):
        before = up[k - 1] if k > 0 else zero
        after = down[k + 1] if k + 1 < len(chunks) else zero
        lower.append(jnp.where(lane < width, before, up[k]))
        upper.append(jnp.where(lane >= LANES - width, after, down[k]))
    return lower, upper


def z_pair(chunk):
    rows = chunk.shape[0]
    row = row_iota(chunk.shape)
    lower = jnp.where(row > 0, turn(chunk, 1, 0), 0.0)
    upper = jnp.where(row < rows - 1, turn(chunk, -1, 0), 0.0)
    return lower, upper


def fine_beside(chunks):
    lower, upper = y_pair(chunks, 16)
    in_x = [beside_x(chunk, 16) for chunk in chunks]
    in_y = [a + b for a, b in zip(lower, upper)]
    in_z = []
    for chunk in chunks:
        below, above = z_pair(chunk)
        in_z.append(below + above)
    return in_x, in_y, in_z


def coarse_turns(columns):
    return (
        [[turn(chunk, 8, 1) for chunk in halves] for halves in columns],
        [[turn(chunk, -8, 1) for chunk in halves] for halves in columns],
    )


def coarse_y_pair(up, down):
    lane = lane_iota(up[0].shape)
    zero = jnp.zeros_like(up[0])
    lower = []
    upper = []
    for half in range(2):
        lower.append(jnp.where(lane < 8, up[half - 1] if half > 0 else zero, up[half]))
        upper.append(jnp.where(lane >= LANES - 8, down[half + 1] if half < 1 else zero, down[half]))
    return lower, upper


def coarse_x_pair(columns, up, down, index, half, ring=False):
    chunk = columns[index][half]
    cell = lane_iota(chunk.shape) % 8
    count = len(columns)
    zero = jnp.zeros_like(chunk)
    before = down[(index - 1) % count][half] if ring or index > 0 else zero
    after = up[(index + 1) % count][half] if ring or index + 1 < count else zero
    low = turn(jnp.where(cell == 7, before, chunk), 1, 1)
    high = turn(jnp.where(cell == 0, after, chunk), -1, 1)
    return low, high


def coarse_sums(columns, ring=False):
    up, down = coarse_turns(columns)

    def sums(index):
        lower, upper = coarse_y_pair(up[index], down[index])
        halves = []
        for half in range(2):
            chunk = columns[index][half]
            low, high = coarse_x_pair(columns, up, down, index, half, ring)
            total = low + high + lower[half] + upper[half]
            halves.append(total + turn(chunk, 1, 0) + turn(chunk, -1, 0))
        return halves

    return sums


def power_div(values, divisor):
    return lax.shift_right_logical(values, jnp.full_like(values, divisor.bit_length() - 1))


def power_rem(values, divisor):
    return values & (divisor - 1)


def octant_table():
    key = row_iota((256, LANES))
    col = lane_iota((256, LANES))
    key_x = power_rem(key, 16)
    col_x = power_rem(col, 8)
    side_x = jnp.where(col_x == 7, 0, jnp.where(col_x == 0, 15, 16))
    right_x = jnp.where(col < 64, power_div(key_x, 2) - col_x, key_x - side_x)
    right_y = power_div(key, 32) - power_div(power_rem(col, 64), 8)
    return jnp.where((right_x | right_y) == 0, 0.5, 0.0).astype(jnp.bfloat16)


def root_table(sub_count):
    shape = (4 * LANES, 16 * sub_count)
    key = row_iota(shape)
    near_x = power_div(power_rem(key, 8), 4)
    row = power_div(power_rem(key, 256), 32)
    along = jnp.where(key < 256, near_x + 1, 3 - 3 * near_x)
    target = row * (2 * sub_count) + along
    return jnp.where(lane_iota(shape) == target, 0.25, 0.0).astype(jnp.bfloat16)


def as_column(row):
    count = row.shape[1]
    shape = (count, count)
    return jnp.sum(
        jnp.where(row_iota(shape) == lane_iota(shape), row, 0.0), axis=1, keepdims=True
    )


def grid_codes(sub_count, wide_y, child_ref, place_ref):
    side_y = wide_y // 2
    side_x = sub_count // 2
    shape = child_ref.shape
    octant = row_iota(shape)
    place = jnp.broadcast_to(place_ref[...], shape)
    half_z = power_div(octant, 4)
    cell_z = 2 * power_div(place, side_y * side_x) + half_z
    cell_y = 2 * power_rem(power_div(place, side_x), side_y) + power_rem(power_div(octant, 2), 2)
    cell_x = 2 * power_rem(place, side_x) + power_rem(octant, 2)
    return (cell_z * wide_y + cell_y) * sub_count + cell_x, half_z * wide_y + cell_y


def of_own(child_ref, values, blocks, sub_count, sub_here, blk_here):
    first = (blk_here * sub_count + sub_here) * blocks
    values = values.astype(jnp.float32)
    return [
        jnp.sum(jnp.where(child_ref[...] == first + slot, values, 0.0)).astype(jnp.int32)
        for slot in range(blocks)
    ]


def lists_agree(
    sub_count, blk_count, leaf_ref, leaf_vector, parent_ref, child_ref, place_ref, codes, own
):
    blocks = len(own)
    wide_y = blocks // 2
    side_y = wide_y // 2
    side_x = sub_count // 2
    parents = child_ref.shape[1]
    layer = wide_y * sub_count
    children = child_ref[...]
    device = power_div(codes, 2 * layer) * sub_count + power_rem(codes, sub_count)
    missed = jnp.where(power_div(children, blocks) != device, 1.0, 0.0)
    shape = (blocks, 6)
    row = row_iota(shape)
    own_code = jnp.zeros(shape, jnp.int32)
    for slot in range(blocks):
        own_code = jnp.where(row == slot, own[slot], own_code)
        for face, stride in enumerate((-1, 1, -sub_count, sub_count, -layer, layer)):
            hit = (children == leaf_ref[slot, face]) & (codes == own[slot] + stride)
            missed = missed - jnp.where(hit, 1.0, 0.0)
    face = lane_iota(shape)
    along = jnp.where(
        face < 2,
        power_rem(own_code, sub_count),
        jnp.where(
            face < 4,
            power_rem(power_div(own_code, sub_count), wide_y),
            power_div(own_code, layer),
        ),
    )
    length = jnp.where(face < 2, sub_count, jnp.where(face < 4, wide_y, 2 * blk_count))
    goal = along + 2 * power_rem(face, 2) - 1
    exists = (goal >= 0) & (goal < length)
    listed = leaf_vector[...]
    faults = jnp.sum(
        jnp.where(
            exists,
            jnp.where(listed >= 0, 1.0, -100000.0),
            jnp.where(listed < 0, 0.0, -100000.0),
        )
    )
    wrong = jnp.abs(jnp.sum(missed) + faults)
    place_row = place_ref[...].astype(jnp.float32)
    place_column = as_column(place_row)
    number = row_iota((parents, parents))
    place = place_ref[...]
    missed = jnp.zeros((1, parents), jnp.float32)
    for axis, (stride, length) in enumerate(((1, side_x), (side_x, side_y), (side_y * side_x, blk_count))):
        along = power_rem(power_div(place, stride), length)
        for sign in (-1, 1):
            face = 2 * axis + (sign + 1) // 2
            listed = parent_ref[face : face + 1, :]
            found = jnp.sum(jnp.where(number == listed, place_column, 0.0), axis=0, keepdims=True)
            exists = (along + sign >= 0) & (along + sign < length)
            wanted = (place + sign * stride).astype(jnp.float32)
            missed = missed + jnp.where(
                exists,
                jnp.where((listed >= 0) & (found == wanted), 0.0, 1.0),
                jnp.where(listed < 0, 0.0, 1.0),
            )
    wrong = wrong + jnp.sum(missed)
    return jnp.where(wrong == 0.0, 1.0, 0.0)


def limits(sub_count, blk_count):
    sub_here = lax.axis_index("sub")
    blk_here = lax.axis_index("blk")

    def gain(condition):
        return jnp.where(condition, 1.0, 0.0).astype(jnp.float32)

    return (
        sub_here,
        blk_here,
        gain(sub_here > 0),
        gain(sub_here < sub_count - 1),
        gain(blk_here > 0),
        gain(blk_here < blk_count - 1),
    )


def placed_chunks(placed, wide_y):
    chunks = []
    for k in range(2 * wide_y):
        lanes = slice(LANES * (k % 2), LANES * (k % 2) + LANES)
        chunks.append(
            jnp.concatenate([placed[k // 2, :, lanes], placed[wide_y + k // 2, :, lanes]], axis=0)
        )
    return chunks


def return_gain(shape, x_low, x_high, z_low, z_high):
    cell = lane_iota(shape) % 16
    row = row_iota(shape)
    return (
        jnp.where(cell == 0, x_low, 0.0)
        + jnp.where(cell == 15, x_high, 0.0)
        + jnp.where(row == 0, z_low, 0.0)
        + jnp.where(row == shape[0] - 1, z_high, 0.0)
    ) * (FACTOR * FACTOR)


def push_kernel(
    sub_count, blk_count, blk_bits,
    leaf_hbm, parent_hbm, child_hbm, place_hbm, owner_hbm, rhs_hbm,
    placed, own_ref, root_ref, leaf_out, parent_ref, child_ref, place_ref, owner_out, *rest
):
    msg_refs = rest[:blk_bits]
    leaf_ref, rhs_ref, rows_s, rows_g, left_a, coarse_s, sems = rest[blk_bits:]
    copies = [
        pltpu.make_async_copy(source, target, sems.at[k])
        for k, (source, target) in enumerate(
            (
                (child_hbm, child_ref),
                (place_hbm, place_ref),
                (rhs_hbm, rhs_ref),
                (leaf_hbm, leaf_ref),
                (parent_hbm, parent_ref),
                (leaf_hbm, leaf_out),
                (owner_hbm, owner_out),
            )
        )
    ]
    for copy in copies:
        copy.start()
    table_a = octant_table()
    table_r = root_table(sub_count)
    blocks = rhs_ref.shape[0]
    wide_y = blocks // 2
    f = FACTOR
    f2 = f * f
    sub_here, blk_here, x_low, x_high, z_low, z_high = limits(sub_count, blk_count)
    copies[0].wait()
    copies[1].wait()
    codes, positions = grid_codes(sub_count, wide_y, child_ref, place_ref)
    positions = of_own(child_ref, positions, blocks, sub_count, sub_here, blk_here)
    copies[2].wait()
    for slot in range(blocks):
        placed[positions[slot]] = rhs_ref[slot]
    s = placed_chunks(placed, wide_y)
    shape = s[0].shape
    top = shape[0] - 1
    back = return_gain(shape, x_low, x_high, z_low, z_high)
    sx, sy, sz = fine_beside(s)
    w = [SELF * a + f * (x + y + z) for a, x, y, z in zip(s, sx, sy, sz)]
    wx, wy, wz = fine_beside(w)
    for k in range(2 * wide_y):
        half = slice(LANES * (k % 2), LANES * (k % 2) + LANES)
        rows_s[k] = SELF * w[k] + f * (wx[k] + wy[k] + wz[k]) + back * s[k]
        base = (SELF * f + f2) * s[k] + f * w[k]
        rows_g[k] = base + f2 * (sy[k] + sz[k])
        gz = base + f2 * (sx[k] + sy[k])
        line = 48 * (k // 2)
        left_a[line + 16 : line + 17, half] = gz[0:1]
        left_a[line + 17 : line + 18, half] = gz[top : top + 1]
        left_a[line + 40 : line + 41, half] = (2.0 * f2) * s[k][0:1]
        left_a[line + 41 : line + 42, half] = (2.0 * f2) * s[k][top : top + 1]
        edge = gz + (f - f2) * s[k]
        for bit in range(blk_bits):
            upward = (blk_here // (1 << bit)) % 2 == 0
            msg_refs[bit][16 + k // 2 : 17 + k // 2, half] = jnp.where(
                upward, edge[top : top + 1], edge[0:1]
            )
            msg_refs[bit][16 + wide_y + k // 2 : 17 + wide_y + k // 2, half] = jnp.where(
                upward, s[k][top : top + 1], s[k][0:1]
            )
    for k in range(2 * wide_y):
        half = slice(LANES * (k % 2), LANES * (k % 2) + LANES)
        line = 48 * (k // 2)
        left_a[line : line + 16, half] = (
            rows_s[k, pl.ds(0, 16, stride=2), :] + rows_s[k, pl.ds(1, 16, stride=2), :]
        )
        left_a[line + 24 : line + 40, half] = (
            rows_g[k, pl.ds(0, 16, stride=2), :] + rows_g[k, pl.ds(1, 16, stride=2), :]
        )
    for copy in copies[3:]:
        copy.wait()
    out_a = split_dot(left_a[...], table_a)
    lane24 = lane_iota((24, LANES))
    main = []
    side = []
    for half in range(2):
        first = out_a[96 * half : 96 * half + 24]
        second = out_a[96 * half + 48 : 96 * half + 72]
        main.append(jnp.where(lane24 < 64, first, turn(second, 64, 1)))
        first = out_a[96 * half + 24 : 96 * half + 48]
        second = out_a[96 * half + 72 : 96 * half + 96]
        side.append(jnp.where(lane24 < 64, turn(first, 64, 1), second))
    zero3 = jnp.zeros((3, LANES), jnp.float32)
    for half in range(2):
        lanes = slice(LANES * half, LANES * half + LANES)
        for base_row, piece in ((0, main[half]), (24, side[half])):
            own_ref[base_row : base_row + 3, lanes] = zero3
            own_ref[base_row + 3 : base_row + 4, lanes] = piece[16:17] * z_low
            own_ref[base_row + 4 : base_row + 20, lanes] = piece[0:16]
            own_ref[base_row + 20 : base_row + 21, lanes] = piece[17:18] * z_high
            own_ref[base_row + 21 : base_row + 24, lanes] = zero3
    cell8 = lane24 % 8
    row24 = row_iota((24, LANES))
    inside_z = jnp.where(row24 < 4, z_low, jnp.where(row24 >= 20, z_high, 1.0))
    main24 = [own_ref[0:24, 0:LANES], own_ref[0:24, LANES:256]]
    side24 = [own_ref[24:48, 0:LANES], own_ref[24:48, LANES:256]]
    gain = [inside_z, inside_z * jnp.where(cell8 < 4, x_high, x_low)]
    columns = [main24, [gain[1] * piece for piece in side24]]
    sums = coarse_sums(columns, ring=True)
    wp = []
    for b in range(2):
        near = sums(b)
        wp.append([gain[b] * (SELF * columns[b][h] + f * near[h]) for h in range(2)])
    sums = coarse_sums(wp, ring=True)
    zero8 = jnp.zeros((8, LANES), jnp.float32)
    pieces = []
    for b in range(2):
        near = sums(b)
        for h in range(2):
            k = 2 * b + h
            coarse_s[k, 0:24] = gain[b] * (SELF * wp[b][h] + f * near[h])
            coarse_s[k, 24:32] = zero8
    for k in range(4):
        pieces.append(
            coarse_s[k, pl.ds(0, 8, stride=4), :]
            + coarse_s[k, pl.ds(1, 8, stride=4), :]
            + coarse_s[k, pl.ds(2, 8, stride=4), :]
            + coarse_s[k, pl.ds(3, 8, stride=4), :]
        )
    root_left = jnp.concatenate(pieces, axis=1)
    root_lanes = 16 * sub_count
    root_part = split_dot(root_left, table_r)
    root_part = pltpu.roll(root_part, 2 * sub_here + root_lanes - 1, 1)
    own_code = of_own(child_ref, codes, blocks, sub_count, sub_here, blk_here)
    good = lists_agree(
        sub_count, blk_count, leaf_ref, leaf_out, parent_ref, child_ref, place_ref, codes, own_code
    )
    if root_lanes < 256:
        root_part = jnp.concatenate(
            [root_part, jnp.zeros((8, 256 - root_lanes), jnp.float32)], axis=1
        )
    root_part = jnp.where(row_iota(root_part.shape) < 6, root_part, good)
    own_ref[48:56, :] = root_part
    root_ref[...] = root_part
    for bit in range(blk_bits):
        upward = (blk_here // (1 << bit)) % 2 == 0
        ref = msg_refs[bit]
        ref[8:16, :] = root_part
        for base_row, source in ((0, 0), (4, 24)):
            ref[base_row : base_row + 4, :] = jnp.where(
                upward, own_ref[source + 17 : source + 21, :], own_ref[source + 3 : source + 7, :]
            )


def side_kernel(
    sub_count, blk_count, slots,
    child_ref, owner_ref, place_ref, placed, table_ref,
    position_ref, slot_ref, part_ref, cross_ref, pair_ref,
    left_c
):
    blocks = placed.shape[0]
    wide_y = blocks // 2
    f = FACTOR
    f2 = f * f
    sub_here, blk_here, x_low, x_high, z_low, z_high = limits(sub_count, blk_count)
    _, positions = grid_codes(sub_count, wide_y, child_ref, place_ref)
    positions = of_own(child_ref, positions, blocks, sub_count, sub_here, blk_here)
    for slot in range(blocks):
        position_ref[slot] = positions[slot]
    s = placed_chunks(placed, wide_y)
    back = return_gain(s[0].shape, x_low, x_high, z_low, z_high)
    sx, sy, sz = fine_beside(s)
    w = [SELF * a + f * (x + y + z) for a, x, y, z in zip(s, sx, sy, sz)]
    wx, wy, wz = fine_beside(w)
    for k in range(2 * wide_y):
        half = slice(LANES * (k % 2), LANES * (k % 2) + LANES)
        r = SELF * w[k] + f * (wx[k] + wy[k] + wz[k]) + back * s[k]
        part = f * (s[k] + w[k] + r)
        part_ref[k // 2, :, half] = part[:16]
        part_ref[wide_y + k // 2, :, half] = part[16:]
        line = 64 * (k // 2)
        left_c[line : line + 32, half] = (
            (SELF * f + f) * s[k] + f * w[k] + f2 * (sy[k] + sz[k])
        )
        left_c[line + 32 : line + 64, half] = s[k]
    out_c = split_dot(left_c[...], table_ref[...])
    faces = out_c[0:64]
    for yy in range(1, wide_y):
        faces = faces + turn(out_c[64 * yy : 64 * yy + 64], 16 * yy, 1)
    lane = lane_iota((32, LANES))
    low = jnp.where(lane < 64, faces[0:32], turn(faces[32:64], 64, 1))
    high = jnp.where(lane < 64, turn(faces[0:32], 64, 1), faces[32:64])
    even = sub_here % 2 == 0
    cross_ref[...] = jnp.where(even, low, high)
    pair_ref[...] = jnp.where(even, high, low)
    owned = owned_slots(sub_count, blk_count, slots, sub_here, blk_here, owner_ref, place_ref)
    for k in range(slots):
        for j in range(3):
            slot_ref[3 * k + j] = owned[k][j]


def neighbour_pick(blk_here, blk_count, msg_refs):
    spans = []
    step = 1
    while step < blk_count:
        spans.append(step)
        step = 2 * step + 1

    def picker(other):
        choices = [(blk_here ^ other) == d for d in spans]

        def read(rows, lanes):
            value = msg_refs[spans[-1] - 1][rows, lanes]
            for choice, d in zip(choices[:-1], spans[:-1]):
                value = jnp.where(choice, msg_refs[d - 1][rows, lanes], value)
            return value

        return read

    return picker(blk_here - 1), picker(blk_here + 1)


def root_tiles(sub_count, blk_count):
    return (sub_count * blk_count // 16 + 1) // 2


def join_kernel(sub_count, blk_count, own_ref, cross_ref, *rest):
    msg_refs = rest[: blk_count - 1]
    out_ref, lines_ref, root_s = rest[blk_count - 1 :]
    _, blk_here, _, _, z_low, z_high = limits(sub_count, blk_count)
    below, above = neighbour_pick(blk_here, blk_count, msg_refs)
    row8 = row_iota((8, LANES))
    cell8 = lane_iota((8, LANES)) % 8
    low_rows = (row8 >= 1) & (row8 < 5)
    high_rows = (row8 >= 3) & (row8 < 7)

    def root_rows(d, lanes):
        if d == 0:
            return own_ref[48:56, lanes]
        ref = msg_refs[d - 1]
        return ref[0:8, lanes] if ref.shape[0] == 8 else ref[8:16, lanes]

    good = root_rows(0, slice(0, LANES))
    for d in range(1, blk_count):
        good = jnp.minimum(good, root_rows(d, slice(0, LANES)))
    for half in range(2):
        lanes = slice(LANES * half, LANES * half + LANES)
        low = below(slice(0, 8), lanes) * z_low
        high = above(slice(0, 8), lanes) * z_high
        tiles = []
        for base, low_turn, high_turn in ((0, 1, 3), (24, 5, 7)):
            tiles.append(
                (
                    own_ref[base : base + 8, lanes]
                    + jnp.where(low_rows, turn(low, low_turn, 0), 0.0),
                    own_ref[base + 8 : base + 16, lanes],
                    own_ref[base + 16 : base + 24, lanes]
                    + jnp.where(high_rows, turn(high, high_turn, 0), 0.0),
                )
            )
        packed = tiles[1][0]
        for g in range(3):
            out_ref[8 * g : 8 * g + 8, lanes] = tiles[0][g]
            if g > 0:
                packed = packed + turn(jnp.where(cell8 == 0, tiles[1][g], 0.0), g, 1)
                packed = packed + turn(jnp.where(cell8 == 7, tiles[1][g], 0.0), -g, 1)
        out_ref[24:32, lanes] = packed
        out_ref[23:24, lanes] = good[7:8]
    root_s[...] = jnp.zeros(root_s.shape, jnp.float32)
    for d in range(blk_count):
        start = 4 * (blk_here ^ d) + 3
        for part in range(root_s.shape[0]):
            lanes = slice(LANES * part, LANES * part + LANES)
            value = jnp.where(row8 < 6, root_rows(d, lanes), 0.0)
            root_s[part, pl.ds(start, 8), :] = root_s[part, pl.ds(start, 8), :] + value
    tile = 0
    for start in range(0, 4 * blk_count, 8):
        for part in range(root_s.shape[0]):
            row = ROOT_ROW + 8 * (tile // 2)
            lanes = slice(LANES * (tile % 2), LANES * (tile % 2) + LANES)
            out_ref[row : row + 8, lanes] = root_s[part, 4 + start : 12 + start]
            tile += 1
    row = ROOT_ROW + 8 * root_tiles(sub_count, blk_count)
    count = lines_ref.shape[0] // 2
    half = count // 2
    low = below(slice(16, 16 + count), slice(0, 256)) * z_low
    high = above(slice(16, 16 + count), slice(0, 256)) * z_high
    lines_ref[0:count] = low
    lines_ref[count : 2 * count] = high
    out_ref[row : row + half, :] = low[half:count]
    out_ref[row + half : row + count, :] = high[half:count]
    out_ref[row + 8 : row + 24, 0:LANES] = cross_ref[0:16]
    out_ref[row + 8 : row + 24, LANES:256] = cross_ref[16:32]


def owned_slots(sub_count, blk_count, slots, sub_here, blk_here, owner_ref, place_ref):
    parents = owner_ref.shape[1]
    parent_len = parents // blk_count
    side_x = sub_count // 2
    side_y = parent_len // side_x
    number = lane_iota((1, parents))
    here = (owner_ref[...] == sub_here) & (lax.div(number, parent_len) == blk_here)
    mine = jnp.where(here, 1.0, 0.0)
    shape = (parents, parents)
    rank = jnp.sum(
        jnp.where(row_iota(shape) < lane_iota(shape), as_column(mine), 0.0), axis=0, keepdims=True
    )
    places = place_ref[...].astype(jnp.float32)
    found = []
    for k in range(slots):
        chosen = jnp.where(rank == float(k), mine, 0.0)
        place = jnp.sum(chosen * places).astype(jnp.int32)
        found.append(
            (
                lax.rem(lax.div(place, side_x), side_y),
                lax.rem(place, side_x),
                jnp.sum(chosen).astype(jnp.int32),
            )
        )
    return found


def exchange_slot(sub_count, distance):
    return lax.shift_right_logical(distance, 1) + (distance & 1) * (sub_count // 2)


def solve_kernel(
    sub_count, blk_count, slots,
    positions_in, owned_in, all_ref, pair_ref, part_ref, lines_ref, table_w_ref, table_p_ref, table_l_ref, table_x_ref,
    leaf_ref, parent_ref, good_ref,
    placed, par_s, root_s, fine_s, push_s, positions, owned, sems
):
    position_copy = pltpu.make_async_copy(positions_in, positions, sems.at[0])
    owned_copy = pltpu.make_async_copy(owned_in, owned, sems.at[1])
    position_copy.start()
    owned_copy.start()
    blocks = part_ref.shape[0]
    wide_y = blocks // 2
    f = FACTOR
    f2 = f * f
    sub_here, blk_here, x_low, x_high, z_low, z_high = limits(sub_count, blk_count)
    slot_of = [exchange_slot(sub_count, sub_here ^ c) for c in range(sub_count)]
    row8 = row_iota((8, LANES))
    cell24 = lane_iota((24, LANES)) % 8
    row24 = row_iota((24, LANES))
    good = all_ref[0, 16:24, 0:LANES]
    for c in range(1, sub_count):
        good = jnp.minimum(good, all_ref[c, 16:24, 0:LANES])
    good_ref[0] = jnp.min(jnp.where(row8 == 7, good, 1.0)).astype(jnp.int32)
    cell8 = lane_iota((8, LANES)) % 8
    sides = []
    for c in range(sub_count):
        halves = []
        for half in range(2):
            packed = all_ref[slot_of[c], 24:32, LANES * half : LANES * half + LANES]
            halves.append(
                (
                    jnp.concatenate(
                        [jnp.where(cell8 == 7, turn(packed, g, 1), 0.0) for g in range(3)], axis=0
                    ),
                    jnp.concatenate(
                        [jnp.where(cell8 == 0, turn(packed, -g, 1), 0.0) for g in range(3)], axis=0
                    ),
                )
            )
        sides.append(halves)
    source = []
    for c in range(sub_count):
        halves = []
        for half in range(2):
            value = all_ref[slot_of[c], 0:24, LANES * half : LANES * half + LANES]
            if c + 1 < sub_count:
                value = value + sides[c + 1][half][0]
            if c > 0:
                value = value + sides[c - 1][half][1]
            halves.append(value)
        source.append(halves)

    root_lanes = 16 * sub_count
    row_len = 2 * sub_count
    root_rows = 4 * blk_count
    parts = root_lanes // LANES
    tile_rows = []
    tile = 0
    for _ in range(0, root_rows, 8):
        pieces = []
        for _ in range(parts):
            row = ROOT_ROW + 8 * (tile // 2)
            lanes = slice(LANES * (tile % 2), LANES * (tile % 2) + LANES)
            total = all_ref[0, row : row + 8, lanes]
            for c in range(1, sub_count):
                total = total + all_ref[c, row : row + 8, lanes]
            pieces.append(total)
            tile += 1
        tile_rows.append(jnp.concatenate(pieces, axis=1))
    root_source = jnp.concatenate(tile_rows, axis=0)
    root_source = root_source - jnp.sum(root_source) / (root_rows * root_lanes)
    shape = root_source.shape
    lane = lane_iota(shape)
    row = row_iota(shape)

    def root_sweep(values):
        total = jnp.where(lane % row_len > 0, turn(values, 1, 1), 0.0)
        total = total + jnp.where(lane % row_len < row_len - 1, turn(values, -1, 1), 0.0)
        total = total + jnp.where(lane >= row_len, turn(values, row_len, 1), 0.0)
        total = total + jnp.where(lane < root_lanes - row_len, turn(values, -row_len, 1), 0.0)
        total = total + jnp.where(row > 0, turn(values, 1, 0), 0.0)
        total = total + jnp.where(row < root_rows - 1, turn(values, -1, 0), 0.0)
        return SELF * values + f * (root_source + total)

    before = jnp.maximum(sub_here - 1, 0)
    after = jnp.minimum(sub_here + 1, sub_count - 1)
    slot_before = exchange_slot(sub_count, sub_here ^ before)
    slot_after = exchange_slot(sub_count, sub_here ^ after)
    line = ROOT_ROW + 8 * root_tiles(sub_count, blk_count)
    even = sub_here % 2 == 0

    def crossed(slot):
        rows = all_ref[slot, line + 8 : line + 24, :]
        return jnp.concatenate([rows[:, 0:LANES], rows[:, LANES:256]], axis=0)

    pair = pair_ref[...]
    from_low = jnp.where(even, crossed(slot_before), pair) * x_low
    from_high = jnp.where(even, pair, crossed(slot_after)) * x_high
    behind = jnp.where(lane_iota((32, LANES)) < 64, 1.0, f2)
    left = [from_low * behind, from_high * behind]
    lane128 = lane_iota((32, LANES))
    rows = []
    for yy in range(wide_y):
        rows.append(
            jnp.where(
                lax.rem(lane128, 64) < 16,
                turn(left[0], -16 * yy, 1),
                turn(left[1], 16 - 16 * yy, 1),
            )
        )
    push = split_dot(jnp.concatenate(rows, axis=0), table_x_ref[...])
    for yy in range(wide_y):
        push_s[:, 256 * yy : 256 * yy + 256] = push[32 * yy : 32 * yy + 32]
    cell = lane_iota((2 * wide_y, 256)) % 16
    across = jnp.where(
        cell == 0, turn(all_ref[slot_before, line : line + 2 * wide_y, :], -15, 1) * x_low, 0.0
    ) + jnp.where(
        cell == 15, turn(all_ref[slot_after, line : line + 2 * wide_y, :], 15, 1) * x_high, 0.0
    )
    across = (2.0 * f2) * across
    count = 2 * wide_y
    for yy in range(wide_y):
        lanes = slice(256 * yy, 256 * yy + 256)
        push_s[0:1, lanes] = push_s[0:1, lanes] + lines_ref[yy : yy + 1] + across[yy : yy + 1]
        push_s[1:2, lanes] = push_s[1:2, lanes] + f2 * lines_ref[wide_y + yy : wide_y + yy + 1]
        push_s[31:32, lanes] = (
            push_s[31:32, lanes]
            + lines_ref[count + yy : count + yy + 1]
            + across[wide_y + yy : wide_y + yy + 1]
        )
        push_s[30:31, lanes] = (
            push_s[30:31, lanes]
            + f2 * lines_ref[count + wide_y + yy : count + wide_y + yy + 1]
        )
    values = f * root_source
    left_sweeps = ROOT_SWEEPS - 1
    sums = coarse_sums(source)
    two = []
    for c in range(sub_count):
        if left_sweeps > 0:
            values = root_sweep(values)
            left_sweeps -= 1
        near = sums(c)
        two.append(
            [(f + f * SELF) * source[c][half] + f2 * near[half] for half in range(2)]
        )
    for _ in range(left_sweeps):
        values = root_sweep(values)
    root_s[...] = jnp.zeros(root_s.shape, jnp.float32)
    for part in range(parts):
        root_s[part, 4 : 4 + root_rows] = values[:, LANES * part : LANES * part + LANES]
    mine = jnp.concatenate(
        [root_s[part, pl.ds(4 * blk_here + 3, 8), :] for part in range(parts)], axis=1
    )
    left = jnp.concatenate([turn(mine, -2 * c, 1) for c in range(sub_count)], axis=0)
    wide = split_dot(left, table_w_ref[...])

    valid = (
        (row24 >= 2)
        & (row24 < 22)
        & ((row24 >= 4) | (z_low > 0.0))
        & ((row24 < 20) | (z_high > 0.0))
    )
    three = []
    for c in range(sub_count):
        halves = []
        for half in range(2):
            lanes = slice(LANES * half, LANES * half + LANES)
            tiles = []
            for t in range(3):
                first = wide[8 * c + 2 * t : 8 * c + 2 * t + 1, lanes]
                second = wide[8 * c + 2 * t + 1 : 8 * c + 2 * t + 2, lanes]
                tiles.append(
                    jnp.where(
                        row8 < 4,
                        jnp.broadcast_to(first, (8, LANES)),
                        jnp.broadcast_to(second, (8, LANES)),
                    )
                )
            value = two[c][half] + jnp.concatenate(tiles, axis=0)
            halves.append(jnp.where(valid, value, 0.0))
        three.append(halves)
    sums = coarse_sums(three)
    for c in range(sub_count):
        near = sums(c)
        for half in range(2):
            value = SELF * three[c][half] + f * (near[half] + source[c][half])
            par_s[c, half] = jnp.where(valid, value, 0.0)

    owned_copy.wait()
    pieces = []
    for k in range(slots):
        half = owned[3 * k]
        place_x = owned[3 * k + 1]
        filled = owned[3 * k + 2].astype(jnp.float32)
        pieces.append(
            jnp.concatenate(
                [par_s[2 * place_x, half, 4:20], par_s[2 * place_x + 1, half, 4:20]], axis=1
            )
            * filled
        )
    left = jnp.concatenate(pieces, axis=0)
    moved = split_dot(left, table_p_ref[...])
    for k in range(slots):
        parent_ref[k] = moved[16 * k : 16 * k + 16]

    columns = [
        [par_s[before, half] * x_low for half in range(2)],
        [par_s[sub_here, half] for half in range(2)],
        [par_s[after, half] * x_high for half in range(2)],
    ]
    centre = columns[1]
    up, down = coarse_turns(columns)
    in_y = coarse_y_pair(up[1], down[1])
    lane16 = lane_iota((16, LANES))
    left_rows = []
    in_x = [coarse_x_pair(columns, up, down, 1, half) for half in range(2)]
    blend = {}
    for half in range(2):
        for zp in range(2):
            base = (SELF + 3.0 * f) * centre[half] + f * turn(centre[half], 1 - 2 * zp, 0)
            for yp in range(2):
                for xp in range(2):
                    value = base + f * (in_y[yp][half] + in_x[half][xp])
                    blend[half, zp, 2 * yp + xp] = value[4:20]
    for yy in range(wide_y):
        half = yy // 2
        for zp in range(2):
            pair = []
            for v in (0, 2):
                first = blend[half, zp, v]
                second = blend[half, zp, v + 1]
                if yy % 2 == 0:
                    second = turn(second, 64, 1)
                else:
                    first = turn(first, 64, 1)
                pair.append(jnp.where(lane16 < 64, first, second))
            left_rows.append(jnp.concatenate(pair, axis=1))
    left = jnp.concatenate(left_rows, axis=0)
    spread = split_dot(left, table_l_ref[...])
    for yy in range(wide_y):
        for zp in range(2):
            top = 16 * (2 * yy + zp)
            fine_s[2 * yy, pl.ds(zp, 16, stride=2), :] = spread[top : top + 16, 0:128]
            fine_s[2 * yy + 1, pl.ds(zp, 16, stride=2), :] = spread[top : top + 16, 128:256]

    for zz in range(2):
        for yy in range(wide_y):
            rows = slice(16 * zz, 16 * zz + 16)
            lanes = slice(256 * yy, 256 * yy + 256)
            index = zz * wide_y + yy
            fine = jnp.concatenate([fine_s[2 * yy, rows], fine_s[2 * yy + 1, rows]], axis=1)
            placed[index] = part_ref[index] + fine + f * push_s[rows, lanes]
    position_copy.wait()
    for slot in range(blocks):
        leaf_ref[slot] = placed[positions[slot]]


def paired(count, step):
    return [(i, i ^ step) for i in range(count)]


def is_power(number):
    return number > 0 and number & (number - 1) == 0


def local(rhs, leaf_neighbors, parent_neighbors, children, owners, parent_places):
    blk_count = lax.axis_size("blk")
    sub_count = lax.axis_size("sub")
    blocks = rhs.shape[0]
    wide_y = blocks // 2
    lists = (leaf_neighbors, parent_neighbors, children, owners, parent_places)
    fits = 32 * blocks == 2 * LANES and 16 * sub_count in (LANES, 2 * LANES)
    if not (fits and blk_count > 1 and is_power(blk_count)):
        return general_local(rhs, *lists)
    blk_bits = blk_count.bit_length() - 1
    f32 = jnp.float32
    vmem = pl.BlockSpec(memory_space=pltpu.VMEM)
    smem = pl.BlockSpec(memory_space=pltpu.SMEM)
    params = pltpu.CompilerParams(vmem_limit_bytes=VMEM_LIMIT)
    owner_row = owners.reshape(1, -1)
    place_row = parent_places.reshape(1, -1)
    child_rows = children.T
    parent_rows = parent_neighbors.T
    grid_shape = (blocks, 16, 256)
    outs = pl.pallas_call(
        functools.partial(push_kernel, sub_count, blk_count, blk_bits),
        name="push",
        out_shape=[
            jax.ShapeDtypeStruct(grid_shape, f32),
            jax.ShapeDtypeStruct((OWN_ROWS, 256), f32),
            jax.ShapeDtypeStruct((8, 256), f32),
        ]
        + [
            jax.ShapeDtypeStruct(array.shape, jnp.int32)
            for array in (leaf_neighbors, parent_rows, child_rows, place_row, owner_row)
        ]
        + [jax.ShapeDtypeStruct((MSG_ROWS, 256), f32)] * blk_bits,
        in_specs=[pl.BlockSpec(memory_space=pltpu.HBM)] * 6,
        out_specs=[vmem] * (8 + blk_bits),
        scratch_shapes=[
            pltpu.SMEM(leaf_neighbors.shape, jnp.int32),
            pltpu.VMEM(grid_shape, f32),
            pltpu.VMEM((2 * wide_y, 32, LANES), f32),
            pltpu.VMEM((2 * wide_y, 32, LANES), f32),
            pltpu.VMEM((48 * wide_y, 256), f32),
            pltpu.VMEM((4, 32, LANES), f32),
            pltpu.SemaphoreType.DMA((7,)),
        ],
        compiler_params=params,
    )(
        *(
            pltpu.with_memory_space_constraint(array, pltpu.HBM)
            for array in (leaf_neighbors, parent_rows, child_rows, place_row, owner_row, rhs)
        )
    )
    placed, own, root_tile, leaf_neighbors, parent_rows, child_rows, place_row, owner_row = outs[:8]
    messages = outs[8:]
    lists = (
        leaf_neighbors, parent_rows.T, child_rows.T, owner_row.reshape(-1), place_row.reshape(-1),
    )
    received = []
    for d in range(1, blk_count):
        message = messages[d.bit_length() - 1] if is_power(d + 1) else root_tile
        received.append(lax.ppermute(message, "blk", paired(blk_count, d)))
    positions, owned, own_part, cross_faces, pair_faces = pl.pallas_call(
        functools.partial(side_kernel, sub_count, blk_count, PMOST),
        name="side",
        out_shape=[
            jax.ShapeDtypeStruct((blocks,), jnp.int32),
            jax.ShapeDtypeStruct((3 * PMOST,), jnp.int32),
            jax.ShapeDtypeStruct(grid_shape, f32),
        ]
        + [jax.ShapeDtypeStruct((32, LANES), f32)] * 2,
        in_specs=[vmem] * 5,
        out_specs=[smem] * 2 + [vmem] * 3,
        scratch_shapes=[pltpu.VMEM((64 * wide_y, 256), f32)],
        compiler_params=params,
    )(child_rows, owner_row, place_row, placed, jnp.asarray(face_table()))
    pair_faces = lax.ppermute(pair_faces, "sub", paired(sub_count, 1))
    root_parts = 16 * sub_count // LANES
    joined_rows = ROOT_ROW + 8 * root_tiles(sub_count, blk_count) + 8 + 16
    joined, lines = pl.pallas_call(
        functools.partial(join_kernel, sub_count, blk_count),
        name="join",
        out_shape=[
            jax.ShapeDtypeStruct((joined_rows, 256), f32),
            jax.ShapeDtypeStruct((4 * wide_y, 256), f32),
        ],
        in_specs=[vmem] * (1 + blk_count),
        out_specs=[vmem] * 2,
        scratch_shapes=[pltpu.VMEM((root_parts, 4 * blk_count + 8, LANES), f32)],
        compiler_params=params,
    )(own, cross_faces, *received)
    block = [joined]
    for d in range(2, sub_count, 2):
        block.append(lax.ppermute(joined, "sub", paired(sub_count, d)))
    block = jnp.stack(block)
    other = lax.ppermute(block, "sub", paired(sub_count, 1))
    gathered = jnp.concatenate([block, other], axis=0)
    leaf_solution, parent_solution, good = pl.pallas_call(
        functools.partial(solve_kernel, sub_count, blk_count, PMOST),
        name="solve",
        out_shape=[
            jax.ShapeDtypeStruct((blocks, 16, 256), f32),
            jax.ShapeDtypeStruct((PMOST, 16, 256), f32),
            jax.ShapeDtypeStruct((1,), jnp.int32),
        ],
        in_specs=[pl.BlockSpec(memory_space=pl.ANY)] * 2 + [vmem] * 8,
        out_specs=[vmem] * 2 + [smem],
        scratch_shapes=[
            pltpu.VMEM((blocks, 16, 256), f32),
            pltpu.VMEM((sub_count, 2, 24, LANES), f32),
            pltpu.VMEM((root_parts, 4 * blk_count + 8, LANES), f32),
            pltpu.VMEM((2 * wide_y, 32, LANES), f32),
            pltpu.VMEM((32, 256 * wide_y), f32),
            pltpu.SMEM((blocks,), jnp.int32),
            pltpu.SMEM((3 * PMOST,), jnp.int32),
            pltpu.SemaphoreType.DMA((2,)),
        ],
        compiler_params=params,
    )(
        positions, owned, gathered, pair_faces, own_part, lines,
        jnp.asarray(root_spread_table(sub_count)), jnp.asarray(parent_table()),
        jnp.asarray(leaf_table_of_cells()), jnp.asarray(push_table()),
    )

    def general(state):
        return (*general_local(rhs, *lists), jnp.ones_like(state[2]))

    state = lax.while_loop(
        lambda state: state[2][0] == 0, general, (leaf_solution, parent_solution, good)
    )
    return state[0], state[1]


def solution(mesh):
    in_specs = (P(("blk", "sub"), None, None), P(("blk", "sub"), None), P(), P(), P(), P())
    out_specs = (P(("blk", "sub"), None, None), P(("blk", "sub"), None, None))
    return jax.shard_map(local, mesh=mesh, in_specs=in_specs, out_specs=out_specs, check_vma=False)
```

```python
import functools

import jax
import jax.numpy as jnp
from jax import lax
import numpy as np
from jax.experimental import pallas as pl
from jax.experimental.pallas import tpu as pltpu
from jax.sharding import PartitionSpec as P

ROOT_SWEEPS = 8
PMOST = 3


relax_weight = 0.8


def extended(block, sides, width):
    for axis, dim in sides:
        count = lax.axis_size(axis)
        forward = [(i, i + 1) for i in range(count - 1)]
        backward = [(target, source) for source, target in forward]
        low = lax.ppermute(
            lax.slice_in_dim(block, block.shape[dim] - width, None, axis=dim), axis, forward
        )
        high = lax.ppermute(lax.slice_in_dim(block, 0, width, axis=dim), axis, backward)
        block = jnp.concatenate([low, block, high], axis=dim)
    return block


def lane_parts():
    lanes = jnp.arange(256, dtype=jnp.int32)
    return (lanes // 16, lanes % 16)


def exact_dot(left, table):
    return jnp.einsum("...k,kl->...l", left, table, precision=lax.Precision.HIGHEST)


def spread_table(column):
    lane_y, lane_x = lane_parts()
    picked = (jnp.arange(16, dtype=jnp.int32)[:, None] == lane_y[None, :]) & (
        lane_x[None, :] == column
    )
    return picked.astype(jnp.float32)


def block_faces(values):
    blocks = values.shape[0]
    stacked = jnp.stack(
        [
            values[:, :, 0::16].reshape(blocks, 256),
            values[:, :, 15::16].reshape(blocks, 256),
            values[:, :, 0:16].reshape(blocks, 256),
            values[:, :, 240:256].reshape(blocks, 256),
            values[:, 0],
            values[:, 15],
        ],
        axis=1,
    )
    return stacked


def apply_operator(values, ghosts):
    blocks = values.shape[0]
    _, lane_x = lane_parts()
    ghost_x_low = ghosts[:, 0].reshape(blocks, 16, 16)
    ghost_x_high = ghosts[:, 1].reshape(blocks, 16, 16)
    ghost_y_low = ghosts[:, 2].reshape(blocks, 16, 16)
    ghost_y_high = ghosts[:, 3].reshape(blocks, 16, 16)
    from_left = jnp.where(
        lane_x[None, None, :] > 0, jnp.pad(values, ((0, 0), (0, 0), (1, 0)))[:, :, :256], 0.0
    )
    from_right = jnp.where(
        lane_x[None, None, :] < 15, jnp.pad(values, ((0, 0), (0, 0), (0, 1)))[:, :, 1:], 0.0
    )
    beside_all = from_left + exact_dot(ghost_x_low, spread_table(0))
    beside_all = beside_all + from_right + exact_dot(ghost_x_high, spread_table(15))
    beside_all = (
        beside_all
        + jnp.pad(values, ((0, 0), (0, 0), (16, 0)))[:, :, :256]
        + jnp.pad(ghost_y_low, ((0, 0), (0, 0), (0, 240)))
    )
    beside_all = (
        beside_all
        + jnp.pad(values, ((0, 0), (0, 0), (0, 16)))[:, :, 16:]
        + jnp.pad(ghost_y_high, ((0, 0), (0, 0), (240, 0)))
    )
    beside_all = beside_all + jnp.concatenate([ghosts[:, 4][:, None], values[:, :-1]], axis=1)
    beside_all = beside_all + jnp.concatenate([values[:, 1:], ghosts[:, 5][:, None]], axis=1)
    return 6.0 * values - beside_all


def jacobi_sweep(values, forcing, ghosts):
    return values + relax_weight / 6.0 * (forcing - apply_operator(values, ghosts))


def restrict_table():
    lane_y, lane_x = lane_parts()
    target = lane_y // 2 * 8 + lane_x // 2
    return (target[:, None] == jnp.arange(64, dtype=jnp.int32)[None, :]).astype(jnp.float32)


def coarse_table():
    lane_y, lane_x = lane_parts()
    target = lane_y // 4 * 4 + lane_x // 4
    return (target[:, None] == jnp.arange(16, dtype=jnp.int32)[None, :]).astype(jnp.float32)


def place_table():
    source_id = jnp.arange(256, dtype=jnp.int32)
    octant_y = source_id // 128
    octant_x = source_id // 64 % 2
    inner_y = source_id // 8 % 8
    inner_x = source_id % 8
    target = (8 * octant_y + inner_y) * 16 + 8 * octant_x + inner_x
    return (target[:, None] == jnp.arange(256, dtype=jnp.int32)[None, :]).astype(jnp.float32)


def restrict_octants(values):
    blocks = values.shape[0]
    paired = values.reshape(blocks, 8, 2, 256).sum(axis=2)
    return (exact_dot(paired, restrict_table()) * 0.5).reshape(blocks, 512)


def assemble(octant_rows):
    blocks = octant_rows.shape[0]
    arranged = (
        octant_rows.reshape(blocks, 2, 2, 2, 8, 64)
        .transpose(0, 1, 4, 2, 3, 5)
        .reshape(blocks, 16, 256)
    )
    return exact_dot(arranged, place_table())


def coarsen(values):
    blocks = values.shape[0]
    layered = values.reshape(blocks, 4, 4, 256).sum(axis=2)
    return (exact_dot(layered, coarse_table()) * 0.25).reshape(blocks, 64)


def widen_root(coarse):
    blocks = coarse.shape[0]
    flat = exact_dot(coarse.reshape(blocks, 4, 16), coarse_table().T)
    return jnp.repeat(flat, 4, axis=1)


def octant_split(values):
    blocks = values.shape[0]
    moved = exact_dot(values, place_table().T)
    return moved.reshape(blocks, 2, 8, 2, 2, 64).transpose(0, 1, 3, 4, 2, 5).reshape(blocks, 8, 512)


def widen_leaf(octant):
    blocks = octant.shape[0]
    flat = exact_dot(octant.reshape(blocks, 8, 64), restrict_table().T)
    return jnp.repeat(flat, 2, axis=1)


def slot_ranks(range_owners):
    width = range_owners.shape[1]
    same_owner = range_owners[:, :, None] == range_owners[:, None, :]
    earlier = (
        jnp.arange(width, dtype=jnp.int32)[:, None] > jnp.arange(width, dtype=jnp.int32)[None, :]
    )
    return jnp.sum(same_owner & earlier[None], axis=2)


def root_relax(root_values, root_source, row_len):
    plane_len = root_values.shape[1]
    padded_z = jnp.pad(root_values, ((1, 1), (0, 0)))
    padded_row = jnp.pad(root_values, ((0, 0), (row_len, row_len)))
    column_x = jnp.arange(plane_len, dtype=jnp.int32)[None, :] % row_len
    beside_all = padded_z[:-2] + padded_z[2:]
    beside_all = (
        beside_all
        + padded_row[:, :plane_len]
        + padded_row[:, 2 * row_len : 2 * row_len + plane_len]
    )
    beside_all = beside_all + jnp.where(
        column_x > 0, padded_row[:, row_len - 1 : row_len - 1 + plane_len], 0.0
    )
    beside_all = beside_all + jnp.where(
        column_x < row_len - 1, padded_row[:, row_len + 1 : row_len + 1 + plane_len], 0.0
    )
    return root_values + relax_weight / 6.0 * (root_source - (6.0 * root_values - beside_all))


def stack_table(range_faces, outer_faces):
    row_count = range_faces.shape[0]
    return jnp.concatenate(
        [
            range_faces.reshape(row_count * 6, 256),
            outer_faces[0],
            outer_faces[1],
            jnp.zeros((1, 256), jnp.float32),
        ],
        axis=0,
    )


def lookup(face_table, rows_index):
    blocks = rows_index.shape[0]
    return jnp.take(face_table, rows_index.reshape(-1), axis=0).reshape(blocks, 6, 256)


def table_index(neighbours, range_start, range_len):
    opposite = jnp.array([1, 0, 3, 2, 5, 4], dtype=jnp.int32)
    local_id = neighbours - range_start
    inside = (local_id >= 0) & (local_id < range_len)
    from_below = (neighbours >= 0) & (local_id < 0)
    from_above = local_id >= range_len
    rows_index = jnp.where(inside, local_id * 6 + opposite[None, :], range_len * 8)
    rows_index = jnp.where(from_below, range_len * 6 + local_id + range_len, rows_index)
    return jnp.where(from_above, range_len * 7 + local_id - range_len, rows_index)


def leaf_index(neighbours, blk_here, sub_here, sub_count):
    blocks = neighbours.shape[0]
    opposite = jnp.array([1, 0, 3, 2, 5, 4], dtype=jnp.int32)
    clamped = jnp.maximum(neighbours, 0)
    device_id = clamped // blocks
    local_id = clamped % blocks
    other_blk = device_id // sub_count
    other_sub = device_id % sub_count
    present = neighbours >= 0
    same_blk = present & (other_blk == blk_here)
    same_sub = present & (other_sub == sub_here)
    rows_index = jnp.where(same_blk & same_sub, local_id * 6 + opposite[None, :], blocks * 10)
    rows_index = jnp.where(
        same_blk & (other_sub == sub_here - 1), blocks * 6 + local_id, rows_index
    )
    rows_index = jnp.where(
        same_blk & (other_sub == sub_here + 1), blocks * 7 + local_id, rows_index
    )
    rows_index = jnp.where(
        same_sub & (other_blk == blk_here - 1), blocks * 8 + local_id, rows_index
    )
    rows_index = jnp.where(
        same_sub & (other_blk == blk_here + 1), blocks * 9 + local_id, rows_index
    )
    return rows_index


def leaf_table(values):
    face_rows = block_faces(values)
    blocks = face_rows.shape[0]
    side_rows = jnp.stack([face_rows[:, 0], face_rows[:, 1]], axis=0)
    side_wide = extended(side_rows, (("sub", 0),), 1)
    edge_rows = jnp.stack([face_rows[:, 4], face_rows[:, 5]], axis=0)
    edge_wide = extended(edge_rows, (("blk", 0),), 1)
    return jnp.concatenate(
        [
            face_rows.reshape(blocks * 6, 256),
            side_wide[0],
            side_wide[3],
            edge_wide[0],
            edge_wide[3],
            jnp.zeros((1, 256), jnp.float32),
        ],
        axis=0,
    )


def range_table(values):
    face_rows = block_faces(values)
    edge_rows = jnp.stack([face_rows[:, 4], face_rows[:, 5]], axis=0)
    widened = extended(edge_rows, (("blk", 0),), 1)
    return stack_table(face_rows, jnp.stack([widened[0], widened[3]], axis=0))


def general_local(rhs, leaf_neighbors, parent_neighbors, children, owners, parent_places):
    factor = relax_weight / 6.0
    blk_count = lax.axis_size("blk")
    sub_count = lax.axis_size("sub")
    blk_here = lax.axis_index("blk")
    sub_here = lax.axis_index("sub")
    blocks = rhs.shape[0]
    range_len = blocks * sub_count
    parent_len = range_len // 8
    range_start = blk_here * range_len
    parent_start = blk_here * parent_len
    leaf_rows = leaf_index(leaf_neighbors, blk_here, sub_here, sub_count)
    sweep_one = factor * rhs
    second = jacobi_sweep(sweep_one, rhs, lookup(leaf_table(sweep_one), leaf_rows))
    residual = rhs - apply_operator(second, lookup(leaf_table(second), leaf_rows))
    octant_rows = lax.all_gather(restrict_octants(residual), "sub", axis=0, tiled=True)
    range_children = lax.dynamic_slice_in_dim(children, parent_start, parent_len, 0) - range_start
    ranks_all = slot_ranks(owners.reshape(blk_count, parent_len)).reshape(-1)
    range_owners = lax.dynamic_slice_in_dim(owners, parent_start, parent_len, 0)
    range_ranks = lax.dynamic_slice_in_dim(ranks_all, parent_start, parent_len, 0)
    slot_match = (range_owners[None, :] == sub_here) & (
        range_ranks[None, :] == jnp.arange(PMOST, dtype=jnp.int32)[:, None]
    )
    filled = jnp.any(slot_match, axis=1)
    slot_local = jnp.sum(
        jnp.where(slot_match, jnp.arange(parent_len, dtype=jnp.int32)[None, :], 0), axis=1
    )
    filled_gain = filled.astype(jnp.float32)[:, None, None]
    own_local = sub_here * blocks + jnp.arange(blocks, dtype=jnp.int32)
    matches = range_children.reshape(-1)[None, :] == own_local[:, None]
    flat_place = jnp.sum(
        jnp.where(matches, jnp.arange(parent_len * 8, dtype=jnp.int32)[None, :], 0), axis=1
    )
    leaf_parent = flat_place // 8
    leaf_octant = flat_place % 8
    source = assemble(octant_rows[range_children])
    parent_rows = table_index(
        lax.dynamic_slice_in_dim(parent_neighbors, parent_start, parent_len, 0),
        parent_start,
        parent_len,
    )
    global_places = lax.dynamic_slice_in_dim(parent_places, parent_start, parent_len, 0)
    keep_gain = jnp.ones((parent_len, 1, 1), jnp.float32)
    parent_one = factor * source
    parent_two = jacobi_sweep(parent_one, source, lookup(range_table(parent_one), parent_rows))
    parent_rest = source - apply_operator(parent_two, lookup(range_table(parent_two), parent_rows))
    coarse = coarsen(parent_rest)
    root_slab = (
        jnp.zeros((parent_len, 64), jnp.float32).at[global_places - parent_start].set(coarse)
    )
    ordered = lax.all_gather(root_slab, "blk", axis=0, tiled=True)
    side_y = blocks // 4
    side_x = sub_count // 2
    root_source = (
        ordered.reshape(blk_count, side_y, side_x, 4, 4, 4)
        .transpose(0, 3, 1, 4, 2, 5)
        .reshape(4 * blk_count, 16 * side_y * side_x)
    )
    root_source = root_source - jnp.mean(root_source)
    root_values = jnp.zeros_like(root_source)
    for _ in range(ROOT_SWEEPS):
        root_values = root_relax(root_values, root_source, 4 * side_x)
    root_back = (
        root_values.reshape(blk_count, 4, side_y, 4, side_x, 4)
        .transpose(0, 2, 4, 1, 3, 5)
        .reshape(blk_count * parent_len, 64)[global_places]
    )
    parent_three = parent_two + widen_root(root_back) * keep_gain
    parent_four = jacobi_sweep(parent_three, source, lookup(range_table(parent_three), parent_rows))
    parent_solution = parent_four[slot_local] * filled_gain
    own_parents = parent_four[leaf_parent]
    pieces = octant_split(own_parents)
    chosen = jnp.take_along_axis(pieces, leaf_octant[:, None, None], axis=1)[:, 0]
    leaf_three = second + widen_leaf(chosen)
    leaf_solution = jacobi_sweep(leaf_three, rhs, lookup(leaf_table(leaf_three), leaf_rows))
    return (leaf_solution, parent_solution)


FACTOR = relax_weight / 6.0
SELF = 1.0 - 6.0 * FACTOR
LANES = 128
OWN_ROWS = 56
ROOT_ROW = 32
MSG_ROWS = 24
VMEM_LIMIT = 16 * 1024 * 1024


def lane_iota(shape):
    return lax.broadcasted_iota(jnp.int32, shape, len(shape) - 1)


def row_iota(shape):
    return lax.broadcasted_iota(jnp.int32, shape, len(shape) - 2)


def turn(values, shift, axis):
    size = values.shape[axis]
    shift = shift % size
    if shift == 0:
        return values
    return pltpu.roll(values, shift, axis)


def split_dot(left, table):
    high = left.astype(jnp.bfloat16)
    low = (left - high.astype(jnp.float32)).astype(jnp.bfloat16)
    return jnp.dot(high, table, preferred_element_type=jnp.float32) + jnp.dot(
        low, table, preferred_element_type=jnp.float32
    )


def zero_one(condition, scale=1.0):
    return np.where(condition, scale, 0.0).astype(jnp.bfloat16)


def key_col(rows, columns):
    return np.arange(rows)[:, None], np.arange(columns)[None, :]


def face_table():
    key, col = key_col(256, LANES)
    return zero_one(
        (key // 16 == col % 64)
        & (((col < 64) & (key % 16 == 0)) | ((col >= 64) & (key % 16 == 15)))
    )


def root_spread_table(sub_count):
    key, col = key_col(16 * sub_count, 256)
    return zero_one(key == (col // 32) * (2 * sub_count) + col % 8 // 4)


def parent_table():
    key, col = key_col(256, 256)
    return zero_one(key == (col % 16 // 8) * LANES + (col // 16) * 8 + col % 8)


def leaf_table_of_cells():
    key, col = key_col(256, 256)
    y = col // 16
    x = col % 16
    return zero_one(key == (y % 2 * 2 + x % 2) * 64 + y // 2 * 8 + x // 2)


def push_table():
    key, col = key_col(LANES, 256)
    group = key // 16
    cell = np.select([group == 0, group == 1, group == 4, group == 5], [0, 15, 1, 14], 16)
    return zero_one((key % 16 == col // 16) & (col % 16 == cell))


def beside_x(chunk, width):
    cell = lane_iota(chunk.shape) % width
    low = jnp.where(cell > 0, turn(chunk, 1, 1), 0.0)
    high = jnp.where(cell < width - 1, turn(chunk, -1, 1), 0.0)
    return low + high


def y_pair(chunks, width):
    lane = lane_iota(chunks[0].shape)
    up = [turn(chunk, width, 1) for chunk in chunks]
    down = [turn(chunk, -width, 1) for chunk in chunks]
    zero = jnp.zeros_like(chunks[0])
    lower = []
    upper = []
    for k in range(len(chunks)):
        before = up[k - 1] if k > 0 else zero
        after = down[k + 1] if k + 1 < len(chunks) else zero
        lower.append(jnp.where(lane < width, before, up[k]))
        upper.append(jnp.where(lane >= LANES - width, after, down[k]))
    return lower, upper


def z_pair(chunk):
    rows = chunk.shape[0]
    row = row_iota(chunk.shape)
    lower = jnp.where(row > 0, turn(chunk, 1, 0), 0.0)
    upper = jnp.where(row < rows - 1, turn(chunk, -1, 0), 0.0)
    return lower, upper


def fine_beside(chunks):
    lower, upper = y_pair(chunks, 16)
    in_x = [beside_x(chunk, 16) for chunk in chunks]
    in_y = [a + b for a, b in zip(lower, upper)]
    in_z = []
    for chunk in chunks:
        below, above = z_pair(chunk)
        in_z.append(below + above)
    return in_x, in_y, in_z


def coarse_turns(columns):
    return (
        [[turn(chunk, 8, 1) for chunk in halves] for halves in columns],
        [[turn(chunk, -8, 1) for chunk in halves] for halves in columns],
    )


def coarse_y_pair(up, down):
    lane = lane_iota(up[0].shape)
    zero = jnp.zeros_like(up[0])
    lower = []
    upper = []
    for half in range(2):
        lower.append(jnp.where(lane < 8, up[half - 1] if half > 0 else zero, up[half]))
        upper.append(jnp.where(lane >= LANES - 8, down[half + 1] if half < 1 else zero, down[half]))
    return lower, upper


def coarse_x_pair(columns, up, down, index, half, ring=False):
    chunk = columns[index][half]
    cell = lane_iota(chunk.shape) % 8
    count = len(columns)
    zero = jnp.zeros_like(chunk)
    before = down[(index - 1) % count][half] if ring or index > 0 else zero
    after = up[(index + 1) % count][half] if ring or index + 1 < count else zero
    low = turn(jnp.where(cell == 7, before, chunk), 1, 1)
    high = turn(jnp.where(cell == 0, after, chunk), -1, 1)
    return low, high


def coarse_sums(columns, ring=False):
    up, down = coarse_turns(columns)

    def sums(index):
        lower, upper = coarse_y_pair(up[index], down[index])
        halves = []
        for half in range(2):
            chunk = columns[index][half]
            low, high = coarse_x_pair(columns, up, down, index, half, ring)
            total = low + high + lower[half] + upper[half]
            halves.append(total + turn(chunk, 1, 0) + turn(chunk, -1, 0))
        return halves

    return sums


def power_div(values, divisor):
    return lax.shift_right_logical(values, jnp.full_like(values, divisor.bit_length() - 1))


def power_rem(values, divisor):
    return values & (divisor - 1)


def octant_table():
    key = row_iota((256, LANES))
    col = lane_iota((256, LANES))
    key_x = power_rem(key, 16)
    col_x = power_rem(col, 8)
    side_x = jnp.where(col_x == 7, 0, jnp.where(col_x == 0, 15, 16))
    right_x = jnp.where(col < 64, power_div(key_x, 2) - col_x, key_x - side_x)
    right_y = power_div(key, 32) - power_div(power_rem(col, 64), 8)
    return jnp.where((right_x | right_y) == 0, 0.5, 0.0).astype(jnp.bfloat16)


def root_table(sub_count):
    shape = (4 * LANES, 16 * sub_count)
    key = row_iota(shape)
    near_x = power_div(power_rem(key, 8), 4)
    row = power_div(power_rem(key, 256), 32)
    along = jnp.where(key < 256, near_x + 1, 3 - 3 * near_x)
    target = row * (2 * sub_count) + along
    return jnp.where(lane_iota(shape) == target, 0.25, 0.0).astype(jnp.bfloat16)


def as_column(row):
    count = row.shape[1]
    shape = (count, count)
    return jnp.sum(
        jnp.where(row_iota(shape) == lane_iota(shape), row, 0.0), axis=1, keepdims=True
    )


def grid_codes(sub_count, wide_y, child_ref, place_ref):
    side_y = wide_y // 2
    side_x = sub_count // 2
    shape = child_ref.shape
    octant = row_iota(shape)
    place = jnp.broadcast_to(place_ref[...], shape)
    half_z = power_div(octant, 4)
    cell_z = 2 * power_div(place, side_y * side_x) + half_z
    cell_y = 2 * power_rem(power_div(place, side_x), side_y) + power_rem(power_div(octant, 2), 2)
    cell_x = 2 * power_rem(place, side_x) + power_rem(octant, 2)
    return (cell_z * wide_y + cell_y) * sub_count + cell_x, half_z * wide_y + cell_y


def of_own(child_ref, values, blocks, sub_count, sub_here, blk_here):
    first = (blk_here * sub_count + sub_here) * blocks
    values = values.astype(jnp.float32)
    return [
        jnp.sum(jnp.where(child_ref[...] == first + slot, values, 0.0)).astype(jnp.int32)
        for slot in range(blocks)
    ]


def lists_agree(
    sub_count, blk_count, leaf_ref, leaf_vector, parent_ref, child_ref, place_ref, codes, own
):
    blocks = len(own)
    wide_y = blocks // 2
    side_y = wide_y // 2
    side_x = sub_count // 2
    parents = child_ref.shape[1]
    layer = wide_y * sub_count
    children = child_ref[...]
    device = power_div(codes, 2 * layer) * sub_count + power_rem(codes, sub_count)
    missed = jnp.where(power_div(children, blocks) != device, 1.0, 0.0)
    shape = (blocks, 6)
    row = row_iota(shape)
    own_code = jnp.zeros(shape, jnp.int32)
    for slot in range(blocks):
        own_code = jnp.where(row == slot, own[slot], own_code)
        for face, stride in enumerate((-1, 1, -sub_count, sub_count, -layer, layer)):
            hit = (children == leaf_ref[slot, face]) & (codes == own[slot] + stride)
            missed = missed - jnp.where(hit, 1.0, 0.0)
    face = lane_iota(shape)
    along = jnp.where(
        face < 2,
        power_rem(own_code, sub_count),
        jnp.where(
            face < 4,
            power_rem(power_div(own_code, sub_count), wide_y),
            power_div(own_code, layer),
        ),
    )
    length = jnp.where(face < 2, sub_count, jnp.where(face < 4, wide_y, 2 * blk_count))
    goal = along + 2 * power_rem(face, 2) - 1
    exists = (goal >= 0) & (goal < length)
    listed = leaf_vector[...]
    faults = jnp.sum(
        jnp.where(
            exists,
            jnp.where(listed >= 0, 1.0, -100000.0),
            jnp.where(listed < 0, 0.0, -100000.0),
        )
    )
    wrong = jnp.abs(jnp.sum(missed) + faults)
    place_row = place_ref[...].astype(jnp.float32)
    place_column = as_column(place_row)
    number = row_iota((parents, parents))
    place = place_ref[...]
    missed = jnp.zeros((1, parents), jnp.float32)
    for axis, (stride, length) in enumerate(((1, side_x), (side_x, side_y), (side_y * side_x, blk_count))):
        along = power_rem(power_div(place, stride), length)
        for sign in (-1, 1):
            face = 2 * axis + (sign + 1) // 2
            listed = parent_ref[face : face + 1, :]
            found = jnp.sum(jnp.where(number == listed, place_column, 0.0), axis=0, keepdims=True)
            exists = (along + sign >= 0) & (along + sign < length)
            wanted = (place + sign * stride).astype(jnp.float32)
            missed = missed + jnp.where(
                exists,
                jnp.where((listed >= 0) & (found == wanted), 0.0, 1.0),
                jnp.where(listed < 0, 0.0, 1.0),
            )
    wrong = wrong + jnp.sum(missed)
    return jnp.where(wrong == 0.0, 1.0, 0.0)


def limits(sub_count, blk_count):
    sub_here = lax.axis_index("sub")
    blk_here = lax.axis_index("blk")

    def gain(condition):
        return jnp.where(condition, 1.0, 0.0).astype(jnp.float32)

    return (
        sub_here,
        blk_here,
        gain(sub_here > 0),
        gain(sub_here < sub_count - 1),
        gain(blk_here > 0),
        gain(blk_here < blk_count - 1),
    )


def placed_chunks(placed, wide_y):
    chunks = []
    for k in range(2 * wide_y):
        lanes = slice(LANES * (k % 2), LANES * (k % 2) + LANES)
        chunks.append(
            jnp.concatenate([placed[k // 2, :, lanes], placed[wide_y + k // 2, :, lanes]], axis=0)
        )
    return chunks


def return_gain(shape, x_low, x_high, z_low, z_high):
    cell = lane_iota(shape) % 16
    row = row_iota(shape)
    return (
        jnp.where(cell == 0, x_low, 0.0)
        + jnp.where(cell == 15, x_high, 0.0)
        + jnp.where(row == 0, z_low, 0.0)
        + jnp.where(row == shape[0] - 1, z_high, 0.0)
    ) * (FACTOR * FACTOR)


def push_kernel(
    sub_count, blk_count, blk_bits,
    leaf_hbm, parent_hbm, child_hbm, place_hbm, owner_hbm, rhs_hbm,
    placed, own_ref, root_ref, leaf_out, parent_ref, child_ref, place_ref, owner_out, *rest
):
    msg_refs = rest[:blk_bits]
    leaf_ref, rhs_ref, rows_s, rows_g, left_a, coarse_s, sems = rest[blk_bits:]
    copies = [
        pltpu.make_async_copy(source, target, sems.at[k])
        for k, (source, target) in enumerate(
            (
                (child_hbm, child_ref),
                (place_hbm, place_ref),
                (rhs_hbm, rhs_ref),
                (leaf_hbm, leaf_ref),
                (parent_hbm, parent_ref),
                (leaf_hbm, leaf_out),
                (owner_hbm, owner_out),
            )
        )
    ]
    for copy in copies:
        copy.start()
    table_a = octant_table()
    table_r = root_table(sub_count)
    blocks = rhs_ref.shape[0]
    wide_y = blocks // 2
    f = FACTOR
    f2 = f * f
    sub_here, blk_here, x_low, x_high, z_low, z_high = limits(sub_count, blk_count)
    copies[0].wait()
    copies[1].wait()
    codes, positions = grid_codes(sub_count, wide_y, child_ref, place_ref)
    positions = of_own(child_ref, positions, blocks, sub_count, sub_here, blk_here)
    copies[2].wait()
    for slot in range(blocks):
        placed[positions[slot]] = rhs_ref[slot]
    s = placed_chunks(placed, wide_y)
    shape = s[0].shape
    top = shape[0] - 1
    back = return_gain(shape, x_low, x_high, z_low, z_high)
    sx, sy, sz = fine_beside(s)
    w = [SELF * a + f * (x + y + z) for a, x, y, z in zip(s, sx, sy, sz)]
    wx, wy, wz = fine_beside(w)
    for k in range(2 * wide_y):
        half = slice(LANES * (k % 2), LANES * (k % 2) + LANES)
        rows_s[k] = SELF * w[k] + f * (wx[k] + wy[k] + wz[k]) + back * s[k]
        base = (SELF * f + f2) * s[k] + f * w[k]
        rows_g[k] = base + f2 * (sy[k] + sz[k])
        gz = base + f2 * (sx[k] + sy[k])
        line = 48 * (k // 2)
        left_a[line + 16 : line + 17, half] = gz[0:1]
        left_a[line + 17 : line + 18, half] = gz[top : top + 1]
        left_a[line + 40 : line + 41, half] = (2.0 * f2) * s[k][0:1]
        left_a[line + 41 : line + 42, half] = (2.0 * f2) * s[k][top : top + 1]
        edge = gz + (f - f2) * s[k]
        for bit in range(blk_bits):
            upward = (blk_here // (1 << bit)) % 2 == 0
            msg_refs[bit][16 + k // 2 : 17 + k // 2, half] = jnp.where(
                upward, edge[top : top + 1], edge[0:1]
            )
            msg_refs[bit][16 + wide_y + k // 2 : 17 + wide_y + k // 2, half] = jnp.where(
                upward, s[k][top : top + 1], s[k][0:1]
            )
    for k in range(2 * wide_y):
        half = slice(LANES * (k % 2), LANES * (k % 2) + LANES)
        line = 48 * (k // 2)
        left_a[line : line + 16, half] = (
            rows_s[k, pl.ds(0, 16, stride=2), :] + rows_s[k, pl.ds(1, 16, stride=2), :]
        )
        left_a[line + 24 : line + 40, half] = (
            rows_g[k, pl.ds(0, 16, stride=2), :] + rows_g[k, pl.ds(1, 16, stride=2), :]
        )
    out_a = split_dot(left_a[...], table_a)
    lane24 = lane_iota((24, LANES))
    main = []
    side = []
    for half in range(2):
        first = out_a[96 * half : 96 * half + 24]
        second = out_a[96 * half + 48 : 96 * half + 72]
        main.append(jnp.where(lane24 < 64, first, turn(second, 64, 1)))
        first = out_a[96 * half + 24 : 96 * half + 48]
        second = out_a[96 * half + 72 : 96 * half + 96]
        side.append(jnp.where(lane24 < 64, turn(first, 64, 1), second))
    zero3 = jnp.zeros((3, LANES), jnp.float32)
    for half in range(2):
        lanes = slice(LANES * half, LANES * half + LANES)
        for base_row, piece in ((0, main[half]), (24, side[half])):
            own_ref[base_row : base_row + 3, lanes] = zero3
            own_ref[base_row + 3 : base_row + 4, lanes] = piece[16:17] * z_low
            own_ref[base_row + 4 : base_row + 20, lanes] = piece[0:16]
            own_ref[base_row + 20 : base_row + 21, lanes] = piece[17:18] * z_high
            own_ref[base_row + 21 : base_row + 24, lanes] = zero3
    cell8 = lane24 % 8
    row24 = row_iota((24, LANES))
    inside_z = jnp.where(row24 < 4, z_low, jnp.where(row24 >= 20, z_high, 1.0))
    main24 = [own_ref[0:24, 0:LANES], own_ref[0:24, LANES:256]]
    side24 = [own_ref[24:48, 0:LANES], own_ref[24:48, LANES:256]]
    gain = [inside_z, inside_z * jnp.where(cell8 < 4, x_high, x_low)]
    columns = [main24, [gain[1] * piece for piece in side24]]
    sums = coarse_sums(columns, ring=True)
    wp = []
    for b in range(2):
        near = sums(b)
        wp.append([gain[b] * (SELF * columns[b][h] + f * near[h]) for h in range(2)])
    sums = coarse_sums(wp, ring=True)
    zero8 = jnp.zeros((8, LANES), jnp.float32)
    pieces = []
    for b in range(2):
        near = sums(b)
        for h in range(2):
            k = 2 * b + h
            coarse_s[k, 0:24] = gain[b] * (SELF * wp[b][h] + f * near[h])
            coarse_s[k, 24:32] = zero8
    for k in range(4):
        pieces.append(
            coarse_s[k, pl.ds(0, 8, stride=4), :]
            + coarse_s[k, pl.ds(1, 8, stride=4), :]
            + coarse_s[k, pl.ds(2, 8, stride=4), :]
            + coarse_s[k, pl.ds(3, 8, stride=4), :]
        )
    root_left = jnp.concatenate(pieces, axis=1)
    root_lanes = 16 * sub_count
    root_part = split_dot(root_left, table_r)
    root_part = pltpu.roll(root_part, 2 * sub_here + root_lanes - 1, 1)
    for copy in copies[3:]:
        copy.wait()
    own_code = of_own(child_ref, codes, blocks, sub_count, sub_here, blk_here)
    good = lists_agree(
        sub_count, blk_count, leaf_ref, leaf_out, parent_ref, child_ref, place_ref, codes, own_code
    )
    if root_lanes < 256:
        root_part = jnp.concatenate(
            [root_part, jnp.zeros((8, 256 - root_lanes), jnp.float32)], axis=1
        )
    root_part = jnp.where(row_iota(root_part.shape) < 6, root_part, good)
    own_ref[48:56, :] = root_part
    root_ref[...] = root_part
    for bit in range(blk_bits):
        upward = (blk_here // (1 << bit)) % 2 == 0
        ref = msg_refs[bit]
        ref[8:16, :] = root_part
        for base_row, source in ((0, 0), (4, 24)):
            ref[base_row : base_row + 4, :] = jnp.where(
                upward, own_ref[source + 17 : source + 21, :], own_ref[source + 3 : source + 7, :]
            )


def side_kernel(
    sub_count, blk_count, slots,
    child_ref, owner_ref, place_ref, placed, table_ref,
    position_ref, slot_ref, part_ref, cross_ref, pair_ref,
    left_c
):
    blocks = placed.shape[0]
    wide_y = blocks // 2
    f = FACTOR
    f2 = f * f
    sub_here, blk_here, x_low, x_high, z_low, z_high = limits(sub_count, blk_count)
    _, positions = grid_codes(sub_count, wide_y, child_ref, place_ref)
    positions = of_own(child_ref, positions, blocks, sub_count, sub_here, blk_here)
    for slot in range(blocks):
        position_ref[slot] = positions[slot]
    s = placed_chunks(placed, wide_y)
    back = return_gain(s[0].shape, x_low, x_high, z_low, z_high)
    sx, sy, sz = fine_beside(s)
    w = [SELF * a + f * (x + y + z) for a, x, y, z in zip(s, sx, sy, sz)]
    wx, wy, wz = fine_beside(w)
    for k in range(2 * wide_y):
        half = slice(LANES * (k % 2), LANES * (k % 2) + LANES)
        r = SELF * w[k] + f * (wx[k] + wy[k] + wz[k]) + back * s[k]
        part = f * (s[k] + w[k] + r)
        part_ref[k // 2, :, half] = part[:16]
        part_ref[wide_y + k // 2, :, half] = part[16:]
        line = 64 * (k // 2)
        left_c[line : line + 32, half] = (
            (SELF * f + f) * s[k] + f * w[k] + f2 * (sy[k] + sz[k])
        )
        left_c[line + 32 : line + 64, half] = s[k]
    out_c = split_dot(left_c[...], table_ref[...])
    faces = out_c[0:64]
    for yy in range(1, wide_y):
        faces = faces + turn(out_c[64 * yy : 64 * yy + 64], 16 * yy, 1)
    lane = lane_iota((32, LANES))
    low = jnp.where(lane < 64, faces[0:32], turn(faces[32:64], 64, 1))
    high = jnp.where(lane < 64, turn(faces[0:32], 64, 1), faces[32:64])
    even = sub_here % 2 == 0
    cross_ref[...] = jnp.where(even, low, high)
    pair_ref[...] = jnp.where(even, high, low)
    owned = owned_slots(sub_count, blk_count, slots, sub_here, blk_here, owner_ref, place_ref)
    for k in range(slots):
        for j in range(3):
            slot_ref[3 * k + j] = owned[k][j]


def neighbour_pick(blk_here, blk_count, msg_refs):
    spans = []
    step = 1
    while step < blk_count:
        spans.append(step)
        step = 2 * step + 1

    def picker(other):
        choices = [(blk_here ^ other) == d for d in spans]

        def read(rows, lanes):
            value = msg_refs[spans[-1] - 1][rows, lanes]
            for choice, d in zip(choices[:-1], spans[:-1]):
                value = jnp.where(choice, msg_refs[d - 1][rows, lanes], value)
            return value

        return read

    return picker(blk_here - 1), picker(blk_here + 1)


def root_tiles(sub_count, blk_count):
    return (sub_count * blk_count // 16 + 1) // 2


def join_kernel(sub_count, blk_count, own_ref, cross_ref, *rest):
    msg_refs = rest[: blk_count - 1]
    out_ref, lines_ref, root_s = rest[blk_count - 1 :]
    _, blk_here, _, _, z_low, z_high = limits(sub_count, blk_count)
    below, above = neighbour_pick(blk_here, blk_count, msg_refs)
    row8 = row_iota((8, LANES))
    cell8 = lane_iota((8, LANES)) % 8
    low_rows = (row8 >= 1) & (row8 < 5)
    high_rows = (row8 >= 3) & (row8 < 7)

    def root_rows(d, lanes):
        if d == 0:
            return own_ref[48:56, lanes]
        ref = msg_refs[d - 1]
        return ref[0:8, lanes] if ref.shape[0] == 8 else ref[8:16, lanes]

    good = root_rows(0, slice(0, LANES))
    for d in range(1, blk_count):
        good = jnp.minimum(good, root_rows(d, slice(0, LANES)))
    for half in range(2):
        lanes = slice(LANES * half, LANES * half + LANES)
        low = below(slice(0, 8), lanes) * z_low
        high = above(slice(0, 8), lanes) * z_high
        tiles = []
        for base, low_turn, high_turn in ((0, 1, 3), (24, 5, 7)):
            tiles.append(
                (
                    own_ref[base : base + 8, lanes]
                    + jnp.where(low_rows, turn(low, low_turn, 0), 0.0),
                    own_ref[base + 8 : base + 16, lanes],
                    own_ref[base + 16 : base + 24, lanes]
                    + jnp.where(high_rows, turn(high, high_turn, 0), 0.0),
                )
            )
        packed = tiles[1][0]
        for g in range(3):
            out_ref[8 * g : 8 * g + 8, lanes] = tiles[0][g]
            if g > 0:
                packed = packed + turn(jnp.where(cell8 == 0, tiles[1][g], 0.0), g, 1)
                packed = packed + turn(jnp.where(cell8 == 7, tiles[1][g], 0.0), -g, 1)
        out_ref[24:32, lanes] = packed
        out_ref[23:24, lanes] = good[7:8]
    root_s[...] = jnp.zeros(root_s.shape, jnp.float32)
    for d in range(blk_count):
        start = 4 * (blk_here ^ d) + 3
        for part in range(root_s.shape[0]):
            lanes = slice(LANES * part, LANES * part + LANES)
            value = jnp.where(row8 < 6, root_rows(d, lanes), 0.0)
            root_s[part, pl.ds(start, 8), :] = root_s[part, pl.ds(start, 8), :] + value
    tile = 0
    for start in range(0, 4 * blk_count, 8):
        for part in range(root_s.shape[0]):
            row = ROOT_ROW + 8 * (tile // 2)
            lanes = slice(LANES * (tile % 2), LANES * (tile % 2) + LANES)
            out_ref[row : row + 8, lanes] = root_s[part, 4 + start : 12 + start]
            tile += 1
    row = ROOT_ROW + 8 * root_tiles(sub_count, blk_count)
    count = lines_ref.shape[0] // 2
    half = count // 2
    low = below(slice(16, 16 + count), slice(0, 256)) * z_low
    high = above(slice(16, 16 + count), slice(0, 256)) * z_high
    lines_ref[0:count] = low
    lines_ref[count : 2 * count] = high
    out_ref[row : row + half, :] = low[half:count]
    out_ref[row + half : row + count, :] = high[half:count]
    out_ref[row + 8 : row + 24, 0:LANES] = cross_ref[0:16]
    out_ref[row + 8 : row + 24, LANES:256] = cross_ref[16:32]


def owned_slots(sub_count, blk_count, slots, sub_here, blk_here, owner_ref, place_ref):
    parents = owner_ref.shape[1]
    parent_len = parents // blk_count
    side_x = sub_count // 2
    side_y = parent_len // side_x
    number = lane_iota((1, parents))
    here = (owner_ref[...] == sub_here) & (lax.div(number, parent_len) == blk_here)
    mine = jnp.where(here, 1.0, 0.0)
    shape = (parents, parents)
    rank = jnp.sum(
        jnp.where(row_iota(shape) < lane_iota(shape), as_column(mine), 0.0), axis=0, keepdims=True
    )
    places = place_ref[...].astype(jnp.float32)
    found = []
    for k in range(slots):
        chosen = jnp.where(rank == float(k), mine, 0.0)
        place = jnp.sum(chosen * places).astype(jnp.int32)
        found.append(
            (
                lax.rem(lax.div(place, side_x), side_y),
                lax.rem(place, side_x),
                jnp.sum(chosen).astype(jnp.int32),
            )
        )
    return found


def exchange_slot(sub_count, distance):
    return lax.shift_right_logical(distance, 1) + (distance & 1) * (sub_count // 2)


def solve_kernel(
    sub_count, blk_count, slots,
    positions_in, owned_in, all_ref, pair_ref, part_ref, lines_ref, table_w_ref, table_p_ref, table_l_ref, table_x_ref,
    leaf_ref, parent_ref, good_ref,
    placed, par_s, root_s, fine_s, push_s, positions, owned, sems
):
    position_copy = pltpu.make_async_copy(positions_in, positions, sems.at[0])
    owned_copy = pltpu.make_async_copy(owned_in, owned, sems.at[1])
    position_copy.start()
    owned_copy.start()
    blocks = part_ref.shape[0]
    wide_y = blocks // 2
    f = FACTOR
    f2 = f * f
    sub_here, blk_here, x_low, x_high, z_low, z_high = limits(sub_count, blk_count)
    slot_of = [exchange_slot(sub_count, sub_here ^ c) for c in range(sub_count)]
    row8 = row_iota((8, LANES))
    cell24 = lane_iota((24, LANES)) % 8
    row24 = row_iota((24, LANES))
    good = all_ref[0, 16:24, 0:LANES]
    for c in range(1, sub_count):
        good = jnp.minimum(good, all_ref[c, 16:24, 0:LANES])
    good_ref[0] = jnp.min(jnp.where(row8 == 7, good, 1.0)).astype(jnp.int32)
    cell8 = lane_iota((8, LANES)) % 8
    sides = []
    for c in range(sub_count):
        halves = []
        for half in range(2):
            packed = all_ref[slot_of[c], 24:32, LANES * half : LANES * half + LANES]
            halves.append(
                (
                    jnp.concatenate(
                        [jnp.where(cell8 == 7, turn(packed, g, 1), 0.0) for g in range(3)], axis=0
                    ),
                    jnp.concatenate(
                        [jnp.where(cell8 == 0, turn(packed, -g, 1), 0.0) for g in range(3)], axis=0
                    ),
                )
            )
        sides.append(halves)
    source = []
    for c in range(sub_count):
        halves = []
        for half in range(2):
            value = all_ref[slot_of[c], 0:24, LANES * half : LANES * half + LANES]
            if c + 1 < sub_count:
                value = value + sides[c + 1][half][0]
            if c > 0:
                value = value + sides[c - 1][half][1]
            halves.append(value)
        source.append(halves)

    root_lanes = 16 * sub_count
    row_len = 2 * sub_count
    root_rows = 4 * blk_count
    parts = root_lanes // LANES
    tile_rows = []
    tile = 0
    for _ in range(0, root_rows, 8):
        pieces = []
        for _ in range(parts):
            row = ROOT_ROW + 8 * (tile // 2)
            lanes = slice(LANES * (tile % 2), LANES * (tile % 2) + LANES)
            total = all_ref[0, row : row + 8, lanes]
            for c in range(1, sub_count):
                total = total + all_ref[c, row : row + 8, lanes]
            pieces.append(total)
            tile += 1
        tile_rows.append(jnp.concatenate(pieces, axis=1))
    root_source = jnp.concatenate(tile_rows, axis=0)
    root_source = root_source - jnp.sum(root_source) / (root_rows * root_lanes)
    shape = root_source.shape
    lane = lane_iota(shape)
    row = row_iota(shape)

    def root_sweep(values):
        total = jnp.where(lane % row_len > 0, turn(values, 1, 1), 0.0)
        total = total + jnp.where(lane % row_len < row_len - 1, turn(values, -1, 1), 0.0)
        total = total + jnp.where(lane >= row_len, turn(values, row_len, 1), 0.0)
        total = total + jnp.where(lane < root_lanes - row_len, turn(values, -row_len, 1), 0.0)
        total = total + jnp.where(row > 0, turn(values, 1, 0), 0.0)
        total = total + jnp.where(row < root_rows - 1, turn(values, -1, 0), 0.0)
        return SELF * values + f * (root_source + total)

    before = jnp.maximum(sub_here - 1, 0)
    after = jnp.minimum(sub_here + 1, sub_count - 1)
    slot_before = exchange_slot(sub_count, sub_here ^ before)
    slot_after = exchange_slot(sub_count, sub_here ^ after)
    line = ROOT_ROW + 8 * root_tiles(sub_count, blk_count)
    even = sub_here % 2 == 0

    def crossed(slot):
        rows = all_ref[slot, line + 8 : line + 24, :]
        return jnp.concatenate([rows[:, 0:LANES], rows[:, LANES:256]], axis=0)

    pair = pair_ref[...]
    from_low = jnp.where(even, crossed(slot_before), pair) * x_low
    from_high = jnp.where(even, pair, crossed(slot_after)) * x_high
    behind = jnp.where(lane_iota((32, LANES)) < 64, 1.0, f2)
    left = [from_low * behind, from_high * behind]
    lane128 = lane_iota((32, LANES))
    rows = []
    for yy in range(wide_y):
        rows.append(
            jnp.where(
                lax.rem(lane128, 64) < 16,
                turn(left[0], -16 * yy, 1),
                turn(left[1], 16 - 16 * yy, 1),
            )
        )
    push = split_dot(jnp.concatenate(rows, axis=0), table_x_ref[...])
    for yy in range(wide_y):
        push_s[:, 256 * yy : 256 * yy + 256] = push[32 * yy : 32 * yy + 32]
    cell = lane_iota((2 * wide_y, 256)) % 16
    across = jnp.where(
        cell == 0, turn(all_ref[slot_before, line : line + 2 * wide_y, :], -15, 1) * x_low, 0.0
    ) + jnp.where(
        cell == 15, turn(all_ref[slot_after, line : line + 2 * wide_y, :], 15, 1) * x_high, 0.0
    )
    across = (2.0 * f2) * across
    count = 2 * wide_y
    for yy in range(wide_y):
        lanes = slice(256 * yy, 256 * yy + 256)
        push_s[0:1, lanes] = push_s[0:1, lanes] + lines_ref[yy : yy + 1] + across[yy : yy + 1]
        push_s[1:2, lanes] = push_s[1:2, lanes] + f2 * lines_ref[wide_y + yy : wide_y + yy + 1]
        push_s[31:32, lanes] = (
            push_s[31:32, lanes]
            + lines_ref[count + yy : count + yy + 1]
            + across[wide_y + yy : wide_y + yy + 1]
        )
        push_s[30:31, lanes] = (
            push_s[30:31, lanes]
            + f2 * lines_ref[count + wide_y + yy : count + wide_y + yy + 1]
        )
    values = f * root_source
    left_sweeps = ROOT_SWEEPS - 1
    sums = coarse_sums(source)
    two = []
    for c in range(sub_count):
        if left_sweeps > 0:
            values = root_sweep(values)
            left_sweeps -= 1
        near = sums(c)
        two.append(
            [(f + f * SELF) * source[c][half] + f2 * near[half] for half in range(2)]
        )
    for _ in range(left_sweeps):
        values = root_sweep(values)
    root_s[...] = jnp.zeros(root_s.shape, jnp.float32)
    for part in range(parts):
        root_s[part, 4 : 4 + root_rows] = values[:, LANES * part : LANES * part + LANES]
    mine = jnp.concatenate(
        [root_s[part, pl.ds(4 * blk_here + 3, 8), :] for part in range(parts)], axis=1
    )
    left = jnp.concatenate([turn(mine, -2 * c, 1) for c in range(sub_count)], axis=0)
    wide = split_dot(left, table_w_ref[...])

    valid = (
        (row24 >= 2)
        & (row24 < 22)
        & ((row24 >= 4) | (z_low > 0.0))
        & ((row24 < 20) | (z_high > 0.0))
    )
    three = []
    for c in range(sub_count):
        halves = []
        for half in range(2):
            lanes = slice(LANES * half, LANES * half + LANES)
            tiles = []
            for t in range(3):
                first = wide[8 * c + 2 * t : 8 * c + 2 * t + 1, lanes]
                second = wide[8 * c + 2 * t + 1 : 8 * c + 2 * t + 2, lanes]
                tiles.append(
                    jnp.where(
                        row8 < 4,
                        jnp.broadcast_to(first, (8, LANES)),
                        jnp.broadcast_to(second, (8, LANES)),
                    )
                )
            value = two[c][half] + jnp.concatenate(tiles, axis=0)
            halves.append(jnp.where(valid, value, 0.0))
        three.append(halves)
    sums = coarse_sums(three)
    for c in range(sub_count):
        near = sums(c)
        for half in range(2):
            value = SELF * three[c][half] + f * (near[half] + source[c][half])
            par_s[c, half] = jnp.where(valid, value, 0.0)

    owned_copy.wait()
    pieces = []
    for k in range(slots):
        half = owned[3 * k]
        place_x = owned[3 * k + 1]
        filled = owned[3 * k + 2].astype(jnp.float32)
        pieces.append(
            jnp.concatenate(
                [par_s[2 * place_x, half, 4:20], par_s[2 * place_x + 1, half, 4:20]], axis=1
            )
            * filled
        )
    left = jnp.concatenate(pieces, axis=0)
    moved = split_dot(left, table_p_ref[...])
    for k in range(slots):
        parent_ref[k] = moved[16 * k : 16 * k + 16]

    columns = [
        [par_s[before, half] * x_low for half in range(2)],
        [par_s[sub_here, half] for half in range(2)],
        [par_s[after, half] * x_high for half in range(2)],
    ]
    centre = columns[1]
    up, down = coarse_turns(columns)
    in_y = coarse_y_pair(up[1], down[1])
    lane16 = lane_iota((16, LANES))
    left_rows = []
    in_x = [coarse_x_pair(columns, up, down, 1, half) for half in range(2)]
    blend = {}
    for half in range(2):
        for zp in range(2):
            base = (SELF + 3.0 * f) * centre[half] + f * turn(centre[half], 1 - 2 * zp, 0)
            for yp in range(2):
                for xp in range(2):
                    value = base + f * (in_y[yp][half] + in_x[half][xp])
                    blend[half, zp, 2 * yp + xp] = value[4:20]
    for yy in range(wide_y):
        half = yy // 2
        for zp in range(2):
            pair = []
            for v in (0, 2):
                first = blend[half, zp, v]
                second = blend[half, zp, v + 1]
                if yy % 2 == 0:
                    second = turn(second, 64, 1)
                else:
                    first = turn(first, 64, 1)
                pair.append(jnp.where(lane16 < 64, first, second))
            left_rows.append(jnp.concatenate(pair, axis=1))
    left = jnp.concatenate(left_rows, axis=0)
    spread = split_dot(left, table_l_ref[...])
    for yy in range(wide_y):
        for zp in range(2):
            top = 16 * (2 * yy + zp)
            fine_s[2 * yy, pl.ds(zp, 16, stride=2), :] = spread[top : top + 16, 0:128]
            fine_s[2 * yy + 1, pl.ds(zp, 16, stride=2), :] = spread[top : top + 16, 128:256]

    for zz in range(2):
        for yy in range(wide_y):
            rows = slice(16 * zz, 16 * zz + 16)
            lanes = slice(256 * yy, 256 * yy + 256)
            index = zz * wide_y + yy
            fine = jnp.concatenate([fine_s[2 * yy, rows], fine_s[2 * yy + 1, rows]], axis=1)
            placed[index] = part_ref[index] + fine + f * push_s[rows, lanes]
    position_copy.wait()
    for slot in range(blocks):
        leaf_ref[slot] = placed[positions[slot]]


def paired(count, step):
    return [(i, i ^ step) for i in range(count)]


def is_power(number):
    return number > 0 and number & (number - 1) == 0


def local(rhs, leaf_neighbors, parent_neighbors, children, owners, parent_places):
    blk_count = lax.axis_size("blk")
    sub_count = lax.axis_size("sub")
    blocks = rhs.shape[0]
    wide_y = blocks // 2
    lists = (leaf_neighbors, parent_neighbors, children, owners, parent_places)
    fits = 32 * blocks == 2 * LANES and 16 * sub_count in (LANES, 2 * LANES)
    if not (fits and blk_count > 1 and is_power(blk_count)):
        return general_local(rhs, *lists)
    blk_bits = blk_count.bit_length() - 1
    f32 = jnp.float32
    vmem = pl.BlockSpec(memory_space=pltpu.VMEM)
    smem = pl.BlockSpec(memory_space=pltpu.SMEM)
    params = pltpu.CompilerParams(vmem_limit_bytes=VMEM_LIMIT)
    owner_row = owners.reshape(1, -1)
    place_row = parent_places.reshape(1, -1)
    child_rows = children.T
    parent_rows = parent_neighbors.T
    grid_shape = (blocks, 16, 256)
    outs = pl.pallas_call(
        functools.partial(push_kernel, sub_count, blk_count, blk_bits),
        name="push",
        out_shape=[
            jax.ShapeDtypeStruct(grid_shape, f32),
            jax.ShapeDtypeStruct((OWN_ROWS, 256), f32),
            jax.ShapeDtypeStruct((8, 256), f32),
        ]
        + [
            jax.ShapeDtypeStruct(array.shape, jnp.int32)
            for array in (leaf_neighbors, parent_rows, child_rows, place_row, owner_row)
        ]
        + [jax.ShapeDtypeStruct((MSG_ROWS, 256), f32)] * blk_bits,
        in_specs=[pl.BlockSpec(memory_space=pltpu.HBM)] * 6,
        out_specs=[vmem] * (8 + blk_bits),
        scratch_shapes=[
            pltpu.SMEM(leaf_neighbors.shape, jnp.int32),
            pltpu.VMEM(grid_shape, f32),
            pltpu.VMEM((2 * wide_y, 32, LANES), f32),
            pltpu.VMEM((2 * wide_y, 32, LANES), f32),
            pltpu.VMEM((48 * wide_y, 256), f32),
            pltpu.VMEM((4, 32, LANES), f32),
            pltpu.SemaphoreType.DMA((7,)),
        ],
        compiler_params=params,
    )(
        *(
            pltpu.with_memory_space_constraint(array, pltpu.HBM)
            for array in (leaf_neighbors, parent_rows, child_rows, place_row, owner_row, rhs)
        )
    )
    placed, own, root_tile, leaf_neighbors, parent_rows, child_rows, place_row, owner_row = outs[:8]
    messages = outs[8:]
    lists = (
        leaf_neighbors, parent_rows.T, child_rows.T, owner_row.reshape(-1), place_row.reshape(-1),
    )
    received = []
    for d in range(1, blk_count):
        message = messages[d.bit_length() - 1] if is_power(d + 1) else root_tile
        received.append(lax.ppermute(message, "blk", paired(blk_count, d)))
    positions, owned, own_part, cross_faces, pair_faces = pl.pallas_call(
        functools.partial(side_kernel, sub_count, blk_count, PMOST),
        name="side",
        out_shape=[
            jax.ShapeDtypeStruct((blocks,), jnp.int32),
            jax.ShapeDtypeStruct((3 * PMOST,), jnp.int32),
            jax.ShapeDtypeStruct(grid_shape, f32),
        ]
        + [jax.ShapeDtypeStruct((32, LANES), f32)] * 2,
        in_specs=[vmem] * 5,
        out_specs=[smem] * 2 + [vmem] * 3,
        scratch_shapes=[pltpu.VMEM((64 * wide_y, 256), f32)],
        compiler_params=params,
    )(child_rows, owner_row, place_row, placed, jnp.asarray(face_table()))
    pair_faces = lax.ppermute(pair_faces, "sub", paired(sub_count, 1))
    root_parts = 16 * sub_count // LANES
    joined_rows = ROOT_ROW + 8 * root_tiles(sub_count, blk_count) + 8 + 16
    joined, lines = pl.pallas_call(
        functools.partial(join_kernel, sub_count, blk_count),
        name="join",
        out_shape=[
            jax.ShapeDtypeStruct((joined_rows, 256), f32),
            jax.ShapeDtypeStruct((4 * wide_y, 256), f32),
        ],
        in_specs=[vmem] * (1 + blk_count),
        out_specs=[vmem] * 2,
        scratch_shapes=[pltpu.VMEM((root_parts, 4 * blk_count + 8, LANES), f32)],
        compiler_params=params,
    )(own, cross_faces, *received)
    ring = []
    for d in range(2, sub_count, 2):
        ring.append(lax.ppermute(joined, "sub", paired(sub_count, d)))
    partner = lax.ppermute(joined, "sub", paired(sub_count, 1))
    ring = jnp.stack(ring)
    other = lax.ppermute(ring, "sub", paired(sub_count, 1))
    gathered = jnp.concatenate([joined[None], ring, partner[None], other], axis=0)
    leaf_solution, parent_solution, good = pl.pallas_call(
        functools.partial(solve_kernel, sub_count, blk_count, PMOST),
        name="solve",
        out_shape=[
            jax.ShapeDtypeStruct((blocks, 16, 256), f32),
            jax.ShapeDtypeStruct((PMOST, 16, 256), f32),
            jax.ShapeDtypeStruct((1,), jnp.int32),
        ],
        in_specs=[pl.BlockSpec(memory_space=pl.ANY)] * 2 + [vmem] * 8,
        out_specs=[vmem] * 2 + [smem],
        scratch_shapes=[
            pltpu.VMEM((blocks, 16, 256), f32),
            pltpu.VMEM((sub_count, 2, 24, LANES), f32),
            pltpu.VMEM((root_parts, 4 * blk_count + 8, LANES), f32),
            pltpu.VMEM((2 * wide_y, 32, LANES), f32),
            pltpu.VMEM((32, 256 * wide_y), f32),
            pltpu.SMEM((blocks,), jnp.int32),
            pltpu.SMEM((3 * PMOST,), jnp.int32),
            pltpu.SemaphoreType.DMA((2,)),
        ],
        compiler_params=params,
    )(
        positions, owned, gathered, pair_faces, own_part, lines,
        jnp.asarray(root_spread_table(sub_count)), jnp.asarray(parent_table()),
        jnp.asarray(leaf_table_of_cells()), jnp.asarray(push_table()),
    )

    def general(state):
        return (*general_local(rhs, *lists), jnp.ones_like(state[2]))

    state = lax.while_loop(
        lambda state: state[2][0] == 0, general, (leaf_solution, parent_solution, good)
    )
    return state[0], state[1]


def solution(mesh):
    in_specs = (P(("blk", "sub"), None, None), P(("blk", "sub"), None), P(), P(), P(), P())
    out_specs = (P(("blk", "sub"), None, None), P(("blk", "sub"), None, None))
    return jax.shard_map(local, mesh=mesh, in_specs=in_specs, out_specs=out_specs, check_vma=False)
```
